256 devices in a mesh: tile: 4 (over x), expert: 64 (over y, z, core).
Axes of the slice: x: 4, y: 4, z: 8, core: 2. Of those that a mesh axis runs over, the one named last changes fastest.
Arguments:
- patches: bfloat16 [64, 16, 32, 1152], P('expert', 'tile'), may hold values from -6 to 6
- norm1_gain: float32 [1152], replicated, may hold values from 0.1 to 1.9
- qkv_weight: bfloat16 [1152, 3, 1152], P(None, None, 'tile'), may hold values from -8 to 8
- qkv_bias: float32 [3, 1152], P(None, 'tile'), may hold values from -3 to 3
- out_weight: bfloat16 [1152, 1152], P('tile'), may hold values from -0.1875 to 0.1875
- out_bias: float32 [1152], replicated, may hold values from -3 to 3
- norm2_gain: float32 [1152], replicated, may hold values from 0.1 to 1.9
- proj_weight: bfloat16 [4608, 2048], P('expert', 'tile'), may hold values from -0.09375 to 0.09375
- moe_gain: float32 [2048], replicated, may hold values from 0.1 to 1.9
- expert_in: bfloat16 [64, 2048, 2, 1408], P('expert', None, None, 'tile'), may hold values from -0.125 to 0.125
- expert_out: bfloat16 [64, 1408, 2048], P('expert', 'tile'), may hold values from -0.15625 to 0.15625
- shared_in: bfloat16 [2048, 2, 1408], P(None, None, 'tile'), may hold values from -0.125 to 0.125
- shared_out: bfloat16 [1408, 2048], P('tile'), may hold values from -0.15625 to 0.15625
- routes: int32 [64, 8, 16, 6], P('expert'), may hold values from 0 to 63, all different within a row; in each aligned block of 32 rows (0 to 31, 32 to 63, ..., all dimensions but the last counted through in order) at most 6 rows name the same one
- gates: float32 [64, 8, 16, 6], P('expert', 'tile'), may hold values from 0.1 to 1
Outputs:
- moe_tokens: bfloat16 [64, 8, 16, 2048], P('expert', 'tile')
The draws below stay inside these ranges and needn't reach their ends.
Inputs may be any that keep to these rules, and one draw needn't show every extreme that they name: `routes`: each merged token names 6 different experts. Flattening the merged tokens in the order page, row, column into aligned blocks of 32 (the merged tokens of one device), no expert is named more than 6 times in a block, a bound that some block reaches.
All inputs are finite; a program needn't handle non-finite values.
Results may differ from the reference program's by a relative error of at most 0.02.
Values may be sent and summed in bfloat16 or wider, within the bound.
A program may use at most 128 MiB of HBM per device.

```python
import math
from functools import partial
import jax
import jax.numpy as jnp
import numpy as np
from jax import lax

HEADS = 16
HD = 72
DV = 1152
D = 2048
FF = 1408
SFF = 1408
TOP = 6
PCOLS = 32
PROWS = 16
PAGES = 64
MROWS = 8
MCOLS = 16
MTOK_DEV = 32
EXPERTS = 64
CAP = 6
SHARES = 4


def draw_qkv_weight(key, part):
    entries = jnp.clip(jax.random.normal(key, (DV, 3, DV), jnp.float32), -6.0, 6.0) * DV ** (-0.5)
    return entries.astype(jnp.bfloat16)


def block_scale(rng, dims, pieces, low, largest):
    def one(dim, blocks):
        steps = jax.random.uniform(jax.random.fold_in(jax.random.fold_in(rng, 6), dim), (blocks,), jnp.float32, low / len(pieces), largest / len(pieces))
        return jnp.repeat(jnp.exp(steps), dims[dim] // blocks).reshape((-1,) + (1,) * (len(dims) - dim - 1))

    level = one(*pieces[0])
    for cut in pieces[1:]:
        level = level * one(*cut)
    return level


def routed_block(rng, own, number, rows, number_of, top, reach, slope):
    sequence = jax.random.permutation(rng, number_of)
    crowded, usual = load_shares(number_of, rows * top, reach, slope, True), load_shares(number_of, rows * top, reach, slope, False)
    places = jnp.arange(number_of)

    def named(tallies, turn):
        used = int((tallies > 0).sum())
        fixed = max(1, used // 4)
        shifted = fixed + (places - fixed + turn * (used - fixed)) % max(1, number_of - fixed)
        return jnp.zeros((number_of,), jnp.int32).at[sequence[jnp.where(places < fixed, places, shifted)]].set(jnp.asarray(tallies, jnp.int32))

    tallies = jnp.where(number % 4 == 0, named(crowded, number // 4), named(usual, number - number // 4 - 1))
    mixed = jax.random.permutation(jax.random.fold_in(own, 3), number_of)
    donor, taker = mixed[0:number_of // 2 * 2:2], mixed[1:number_of // 2 * 2:2]
    slack = jnp.minimum(tallies[donor] - 1, reach - tallies[taker]) // 2
    slack = jnp.where((donor == sequence[0]) | (taker == sequence[0]) | (tallies[taker] == 0), 0, jnp.maximum(slack, 0))
    shifted = jax.random.randint(jax.random.fold_in(own, 4), (number_of // 2,), 0, 1 << 20) % (slack + 1)
    tallies = tallies.at[donor].add(-shifted).at[taker].add(shifted)
    members = jnp.searchsorted(jnp.cumsum(tallies), jnp.arange(rows * top), side="right").astype(jnp.int32)
    table = members.reshape(top, rows).T
    table = table[jax.random.permutation(jax.random.fold_in(own, 1), rows)]
    turn = jax.random.randint(jax.random.fold_in(own, 2), (rows, 1), 0, top)
    return jnp.take_along_axis(table, (jnp.arange(top)[None, :] + turn) % top, axis=1)


def load_shares(amount, total, bound, slope, full):
    weights = [(1 << 20) // math.isqrt(grade ** slope) + 1 for grade in range(1, amount + 1)]
    largest = bound if full else min(bound, max(-(-total // amount), total * weights[0] // sum(weights)))
    least = 1 if total - largest >= amount - 1 else 0
    counts, spare = [largest] + [least] * (amount - 1), total - largest - least * (amount - 1)
    while spare > 0:
        candidates = [i for i in range(1, amount) if counts[i] < largest] or [i for i in range(1, amount) if counts[i] < bound]
        pool, remaining = sum([weights[i] for i in candidates]), spare
        for i in candidates:
            extra = min(bound - counts[i], max(1, remaining * weights[i] // pool), spare)
            counts[i] = counts[i] + extra
            spare = spare - extra
    return np.array(counts)


def normal_values(stream_key, extent, deviation, bound, cuts=(), kind=jnp.bfloat16):
    gain = block_scale(stream_key, extent, cuts, -0.22, 0.18) if cuts else 1.0
    values = jax.random.normal(stream_key, extent, jnp.float32) * deviation * gain
    return jnp.minimum(jnp.maximum(values, -bound), bound).astype(kind)


def setup_inputs(seed: int = 0) -> dict:
    keys = jax.random.split(jax.random.key(seed), 16)
    patches = normal_values(keys[0], (PAGES, PROWS, PCOLS, DV), 1.0, 6.0, ((0, 64), (1, 4)))
    norm1_gain = jnp.clip(1.0 + 0.18 * jax.random.normal(keys[1], (DV,), jnp.float32), 0.1, 1.9)
    qkv_weight = draw_qkv_weight(jax.random.fold_in(keys[15], 71), 0)
    qkv_bias = normal_values(keys[3], (3, DV), 0.5, 3.0, ((1, 4),), jnp.float32)
    out_weight = normal_values(keys[4], (DV, DV), DV ** -0.5, 0.1875, ((0, 4),))
    out_bias = normal_values(keys[5], (DV,), 0.5, 3.0, (), jnp.float32)
    norm2_gain = jnp.clip(1.0 + 0.18 * jax.random.normal(keys[6], (DV,), jnp.float32), 0.1, 1.9)
    proj_weight = normal_values(keys[7], (4 * DV, D), (4 * DV) ** -0.5, 0.09375, ((0, 64), (1, 4)))
    moe_gain = jnp.clip(1.0 + 0.18 * jax.random.normal(keys[8], (D,), jnp.float32), 0.1, 1.9)
    expert_in = normal_values(keys[9], (EXPERTS, D, 2, FF), D ** -0.5, 0.125, ((0, 64), (3, 4)))
    expert_out = normal_values(keys[10], (EXPERTS, FF, D), FF ** -0.5, 0.15625, ((0, 64), (1, 4)))
    shared_in = normal_values(keys[11], (D, 2, SFF), D ** -0.5, 0.125, ((2, 4),))
    shared_out = normal_values(keys[12], (SFF, D), SFF ** -0.5, 0.15625, ((0, 4),))
    routes_keys = jax.random.split(jax.random.fold_in(keys[13], 1), PAGES * MROWS * MCOLS // MTOK_DEV)
    routes_turns = jax.random.permutation(jax.random.fold_in(keys[13], 3), PAGES * MROWS * MCOLS // MTOK_DEV)
    routes = jax.vmap(lambda own, number: routed_block(jax.random.fold_in(keys[13], 2), own, number, MTOK_DEV, EXPERTS, TOP, CAP, 2))(routes_keys, routes_turns).reshape((PAGES, MROWS, MCOLS, TOP))
    gates = jnp.clip(jnp.exp(math.log(1.0) - 2.3025851 * jax.random.uniform(keys[14], (PAGES, MROWS, MCOLS, TOP), jnp.float32) ** block_scale(keys[14], (PAGES, MROWS, MCOLS, TOP), ((0, 64), (1, 4)), -0.2, 0.2)), 0.1, 1.0)
    return {"patches": patches, "norm1_gain": norm1_gain, "qkv_weight": qkv_weight, "qkv_bias": qkv_bias, "out_weight": out_weight, "out_bias": out_bias, "norm2_gain": norm2_gain, "proj_weight": proj_weight, "moe_gain": moe_gain, "expert_in": expert_in, "expert_out": expert_out, "shared_in": shared_in, "shared_out": shared_out, "routes": routes, "gates": gates}


norm_eps = 1e-06
rope_base = 10000.0

def layer_norm(values, gain_vec):
    centre = values - lax.optimization_barrier(jnp.mean(values, axis=-1, keepdims=True))
    spread = lax.optimization_barrier(jnp.mean(centre * centre, axis=-1, keepdims=True))
    return centre * lax.rsqrt(spread + norm_eps) * gain_vec

def rms_norm(values, gain_vec):
    return values * lax.rsqrt(lax.optimization_barrier(jnp.mean(values * values, axis=-1, keepdims=True)) + norm_eps) * gain_vec

def rope_tables(positions, columns, head_size):
    quarter = head_size // 4
    inverse = jnp.exp(jnp.arange(quarter).astype(jnp.float32) * (-math.log(rope_base) / quarter))
    row_angle = (positions // columns).astype(jnp.float32)[:, None] * inverse[None, :]
    col_angle = (positions % columns).astype(jnp.float32)[:, None] * inverse[None, :]
    return (jnp.cos(row_angle), jnp.sin(row_angle), jnp.cos(col_angle), jnp.sin(col_angle))

def rotate(values, tables):
    cos_row, sin_row, cos_col, sin_col = tables
    quarter = values.shape[-1] // 4
    row_a = values[..., :quarter]
    row_b = values[..., quarter:2 * quarter]
    col_a = values[..., 2 * quarter:3 * quarter]
    col_b = values[..., 3 * quarter:]
    return jnp.concatenate([row_a * cos_row[:, None] - row_b * sin_row[:, None], row_b * cos_row[:, None] + row_a * sin_row[:, None], col_a * cos_col[:, None] - col_b * sin_col[:, None], col_b * cos_col[:, None] + col_a * sin_col[:, None]], axis=-1)

def attend(query_rows, key_rows, value_rows, divisor):
    count = query_rows.shape[0]
    width = min(count, 512)
    blocks = query_rows.reshape(count // width, width, query_rows.shape[1], query_rows.shape[2])

    def one_block(block):
        scores = jnp.einsum('qhd,khd->hqk', block.astype(jnp.float32), key_rows.astype(jnp.float32)) / divisor
        weights = jax.nn.softmax(scores, axis=-1).astype(jnp.bfloat16)
        return jnp.einsum('hqk,khd->qhd', weights.astype(jnp.float32), value_rows.astype(jnp.float32)).astype(jnp.bfloat16)
    return lax.map(one_block, blocks).reshape(count, -1)

def block_slots(block_routes, experts_count, capacity):
    picks = block_routes.reshape(-1)
    onehot = (picks[:, None] == jnp.arange(experts_count).astype(jnp.int32)[None, :]).astype(jnp.int32)
    earlier = jnp.cumsum(onehot, axis=0).astype(jnp.int32) - onehot
    ranks = lax.optimization_barrier(jnp.sum(earlier * onehot, axis=1)).astype(jnp.int32)
    owners_flat = (jnp.arange(picks.shape[0]) // block_routes.shape[1]).astype(jnp.int32)
    table = jnp.full((experts_count * capacity,), -1, dtype=jnp.int32).at[picks * capacity + ranks].set(owners_flat)
    return (ranks.reshape(block_routes.shape), table.reshape(experts_count, capacity))

def reference(patches, norm1_gain, qkv_weight, qkv_bias, out_weight, out_bias, norm2_gain, proj_weight, moe_gain, expert_in, expert_out, shared_in, shared_out, routes, gates):
    count = PROWS * PCOLS

    def page_merge(single_page):
        inputs = single_page.reshape(count, DV).astype(jnp.float32)
        normed = layer_norm(inputs, norm1_gain).astype(jnp.bfloat16)
        mixed = jnp.dot(normed, qkv_weight.reshape(DV, 3 * DV), preferred_element_type=jnp.float32).reshape(count, 3, HEADS, HD)
        mixed = mixed + qkv_bias.reshape(1, 3, HEADS, HD)
        tables = rope_tables(jnp.arange(count).astype(jnp.int32), PCOLS, HD)
        query_rows = rotate(mixed[:, 0], tables).astype(jnp.bfloat16)
        key_rows = rotate(mixed[:, 1], tables).astype(jnp.bfloat16)
        value_rows = mixed[:, 2].astype(jnp.bfloat16)
        attended = attend(query_rows, key_rows, value_rows, math.sqrt(HD))
        hidden = inputs + jnp.dot(attended, out_weight, preferred_element_type=jnp.float32) + out_bias
        normed_out = layer_norm(hidden, norm2_gain).astype(jnp.bfloat16)
        windows = normed_out.reshape(PROWS // 2, 2, PCOLS // 2, 2, DV).transpose(0, 2, 1, 3, 4)
        return windows.reshape(PROWS // 2 * (PCOLS // 2), 4 * DV)
    merged = lax.map(page_merge, patches).reshape(-1, 4 * DV)
    tokens_moe = jnp.dot(merged, proj_weight, preferred_element_type=jnp.float32).astype(jnp.bfloat16)
    moe_in = rms_norm(tokens_moe.astype(jnp.float32), moe_gain).astype(jnp.bfloat16)
    total = tokens_moe.shape[0]
    blocks = total // MTOK_DEV
    block_routes = routes.reshape(blocks, MTOK_DEV, TOP)
    ranks, owners = jax.vmap(partial(block_slots, experts_count=EXPERTS, capacity=CAP))(block_routes)
    base_rows = (jnp.arange(blocks) * MTOK_DEV).astype(jnp.int32)[:, None]
    share = FF // SHARES

    def run_expert(expert_id):
        table = owners[:, expert_id, :]
        used = table >= 0
        rows_index = jnp.where(used, base_rows + table, 0)
        inputs = jnp.where(used[..., None], moe_in[rows_index], jnp.zeros((), moe_in.dtype)).reshape(-1, D)
        gated = jnp.dot(inputs, expert_in[expert_id].reshape(D, 2 * FF), preferred_element_type=jnp.float32).reshape(-1, 2, FF)
        hidden = (jax.nn.silu(gated[:, 0]) * gated[:, 1]).astype(jnp.bfloat16)
        total_out = jnp.zeros((hidden.shape[0], D), jnp.float32)
        for portion in range(SHARES):
            partial_out = jnp.dot(hidden[:, portion * share:(portion + 1) * share], expert_out[expert_id, portion * share:(portion + 1) * share], preferred_element_type=jnp.float32)
            total_out = total_out + lax.optimization_barrier(partial_out.astype(jnp.bfloat16)).astype(jnp.float32)
        return total_out.astype(jnp.bfloat16).reshape(blocks, CAP, D)
    results = lax.map(run_expert, jnp.arange(EXPERTS).astype(jnp.int32))
    flat_results = results.reshape(EXPERTS * blocks * CAP, D)
    block_ids = jnp.arange(blocks).astype(jnp.int32)[:, None, None]
    flat_index = ((block_routes * blocks + block_ids) * CAP + ranks).reshape(total, TOP)
    gate_rows = gates.reshape(total, TOP)
    routed = jnp.zeros((total, D), jnp.float32)
    for position in range(TOP):
        routed = routed + gate_rows[:, position:position + 1] * flat_results[flat_index[:, position]].astype(jnp.float32)
    shared_gated = jnp.dot(moe_in, shared_in.reshape(D, 2 * SFF), preferred_element_type=jnp.float32).reshape(total, 2, SFF)
    shared_hidden = (jax.nn.silu(shared_gated[:, 0]) * shared_gated[:, 1]).astype(jnp.bfloat16)
    shared_part = jnp.dot(shared_hidden, shared_out, preferred_element_type=jnp.float32)
    output = tokens_moe.astype(jnp.float32) + shared_part + routed
    return output.astype(jnp.bfloat16).reshape(PAGES, MROWS, MCOLS, D)
```

```python
import math

import jax
import jax.numpy as jnp
from jax import lax
from jax.experimental import pallas as pl
from jax.experimental.pallas import tpu as pltpu
from jax.sharding import PartitionSpec as P

HD = 72
NX, NY, NZ, NC = 4, 4, 8, 2
GROUP = NY * NC
CAP = 6
MESH = pl.DeviceIdType.MESH

norm_eps = 1e-06
rope_base = 10000.0


def layer_norm(values, gain_vec):
    centre = values - jnp.mean(values, axis=-1, keepdims=True)
    spread = jnp.mean(centre * centre, axis=-1, keepdims=True)
    return centre * lax.rsqrt(spread + norm_eps) * gain_vec


def rms_norm(values, gain_vec):
    return (
        values * lax.rsqrt(jnp.mean(values * values, axis=-1, keepdims=True) + norm_eps) * gain_vec
    )


def rope_tables(positions, columns, head_size):
    quarter = head_size // 4
    inverse = jnp.exp(jnp.arange(quarter).astype(jnp.float32) * (-math.log(rope_base) / quarter))
    row_angle = (positions // columns).astype(jnp.float32)[:, None] * inverse[None, :]
    col_angle = (positions % columns).astype(jnp.float32)[:, None] * inverse[None, :]
    return (jnp.cos(row_angle), jnp.sin(row_angle), jnp.cos(col_angle), jnp.sin(col_angle))


def rotate(values, tables):
    cos_row, sin_row, cos_col, sin_col = tables
    quarter = values.shape[-1] // 4
    row_a = values[..., :quarter]
    row_b = values[..., quarter : 2 * quarter]
    col_a = values[..., 2 * quarter : 3 * quarter]
    col_b = values[..., 3 * quarter :]
    return jnp.concatenate(
        [
            row_a * cos_row[:, None] - row_b * sin_row[:, None],
            row_b * cos_row[:, None] + row_a * sin_row[:, None],
            col_a * cos_col[:, None] - col_b * sin_col[:, None],
            col_b * cos_col[:, None] + col_a * sin_col[:, None],
        ],
        axis=-1,
    )


def attend(query_rows, key_rows, value_rows, divisor):
    scores = (
        jnp.einsum("qhd,khd->hqk", query_rows, key_rows, preferred_element_type=jnp.float32)
        / divisor
    )
    weights = jax.nn.softmax(scores, axis=-1).astype(jnp.bfloat16)
    attended = jnp.einsum(
        "hqk,khd->qhd", weights, value_rows, preferred_element_type=jnp.float32
    ).astype(jnp.bfloat16)
    return attended.reshape(attended.shape[0], -1)


def ring_place(axis):
    if axis == "x":
        return lax.axis_index("tile"), NX, lambda place: {"tile": place}
    here = lax.axis_index("expert")
    y, z, core = here // (NZ * NC), (here // NC) % NZ, here % NC
    return z, NZ, lambda place: {"expert": (y * NZ + place) * NC + core}


def greet(device_ids):
    barrier = pltpu.get_barrier_semaphore()
    for device_id in device_ids:
        pl.semaphore_signal(barrier, inc=1, device_id=device_id, device_id_type=MESH)
    pl.semaphore_wait(barrier, len(device_ids))


def ring_chunks(rows, step):
    starts = list(range(0, rows, step))
    half = (len(starts) + 1) // 2
    return [(s, step, 1 if i < half else -1) for i, s in enumerate(starts)]


def dir_order(chunks, sign):
    ids = range(len(chunks))
    return [i for i in ids if chunks[i][2] == sign] + [i for i in ids if chunks[i][2] != sign]


def interleave(a, b):
    out = []
    for i in range(max(len(a), len(b))):
        out += a[i : i + 1] + b[i : i + 1]
    return out


def ring_gather_kernel(plan, *refs):
    count = len(plan)
    ins, outs = refs[:count], refs[count : 2 * count]
    send_sem, recv_sem, local_sem = refs[2 * count :]
    rings = {axis: ring_place(axis) for axis, _ in plan}
    greet(
        [
            device((here + sign) % size)
            for here, size, device in rings.values()
            for sign in (1, -1)
        ]
    )
    arrivals, sends, number = {}, [], 0
    longest = max(rings[axis][1] // 2 for axis, _ in plan)
    local = []
    for hop in range(1, longest + 1):
        for task, (axis, chunks) in enumerate(plan):
            here, size, device = rings[axis]
            if hop > size // 2:
                continue
            order = interleave(
                [(1, i) for i in dir_order(chunks, 1)], [(-1, i) for i in dir_order(chunks, -1)]
            )
            for sign, i in order:
                start, rows, far = chunks[i]
                if hop == size // 2 and far != sign:
                    continue
                block = (here - sign * (hop - 1) + size) % size
                part = pl.ds(start, rows)
                if hop == 1:
                    source = ins[task].at[part]
                else:
                    arrivals.pop((task, sign, i)).wait_recv()
                    source = outs[task].at[block, part]
                copy = pltpu.make_async_remote_copy(
                    src_ref=source,
                    dst_ref=outs[task].at[block, part],
                    send_sem=send_sem.at[number],
                    recv_sem=recv_sem.at[number],
                    device_id=device((here + sign + size) % size),
                    device_id_type=MESH,
                )
                copy.start()
                arrivals[(task, sign, i)] = copy
                sends.append(copy)
                number += 1
        if hop == 1:
            for task, (axis, _) in enumerate(plan):
                own = pltpu.make_async_copy(
                    ins[task], outs[task].at[rings[axis][0]], local_sem.at[task]
                )
                own.start()
                local.append(own)
    for copy in arrivals.values():
        copy.wait_recv()
    for copy in sends:
        copy.wait_send()
    for own in local:
        own.wait()


def copies_of(axis, chunks):
    half = (NX if axis == "x" else NZ) // 2
    return sum(half + half - 1 for _ in chunks)


def ring_gather(tasks, collective_id):
    plan = [(axis, ring_chunks(block.shape[0], step)) for axis, block, step in tasks]
    copies = sum(copies_of(*entry) for entry in plan)
    sizes = {"x": NX, "z": NZ}

    def kernel(*refs):
        ring_gather_kernel(plan, *refs)

    return pl.pallas_call(
        kernel,
        out_shape=[
            jax.ShapeDtypeStruct((sizes[axis],) + block.shape, block.dtype)
            for axis, block, _ in tasks
        ],
        in_specs=[pl.BlockSpec(memory_space=pltpu.VMEM)] * len(tasks),
        out_specs=[pl.BlockSpec(memory_space=pltpu.VMEM)] * len(tasks),
        scratch_shapes=[
            pltpu.SemaphoreType.DMA((copies,)),
            pltpu.SemaphoreType.DMA((copies,)),
            pltpu.SemaphoreType.DMA((len(tasks),)),
        ],
        compiler_params=pltpu.CompilerParams(collective_id=collective_id, has_side_effects=True),
    )(*[block for _, block, _ in tasks])


def ring_reduce_kernel(axis, plan, *refs):
    count = len(plan)
    ins, outs = refs[:count], refs[count : 2 * count]
    landed, staged = refs[2 * count : 3 * count], refs[3 * count : 4 * count]
    send_sem, recv_sem = refs[4 * count :]
    here, size, device = ring_place(axis)
    greet([device((here + sign + size) % size) for sign in (1, -1)])
    half = size // 2
    last, sends, number = {}, [], 0
    slots = [0] * count
    for step in range(half):
        for task, chunks in enumerate(plan):
            order = interleave(
                [(1, i) for i in dir_order(chunks, 1)], [(-1, i) for i in dir_order(chunks, -1)]
            )
            for sign, i in order:
                start, rows, far = chunks[i]
                length = half if far == sign else half - 1
                if step >= length:
                    continue
                part = pl.ds(start, rows)
                target = (here + sign * (length - step) + size) % size
                slot = slots[task]
                slots[task] += 1
                if step == 0:
                    source = ins[task].at[target, part]
                else:
                    copy, before = last[(task, sign, i)]
                    copy.wait_recv()
                    staged[task][slot] = (
                        ins[task][target, part].astype(jnp.float32)
                        + landed[task][before].astype(jnp.float32)
                    ).astype(staged[task].dtype)
                    source = staged[task].at[slot]
                copy = pltpu.make_async_remote_copy(
                    src_ref=source,
                    dst_ref=landed[task].at[slot],
                    send_sem=send_sem.at[number],
                    recv_sem=recv_sem.at[number],
                    device_id=device((here + sign + size) % size),
                    device_id_type=MESH,
                )
                copy.start()
                last[(task, sign, i)] = (copy, slot)
                sends.append(copy)
                number += 1
    for task, chunks in enumerate(plan):
        for i, (start, rows, _) in enumerate(chunks):
            part = pl.ds(start, rows)
            total = ins[task][here, part].astype(jnp.float32)
            for sign in (1, -1):
                if (task, sign, i) in last:
                    copy, slot = last[(task, sign, i)]
                    copy.wait_recv()
                    total = total + landed[task][slot].astype(jnp.float32)
            outs[task][part] = total.astype(outs[task].dtype)
    for copy in sends:
        copy.wait_send()


def ring_reduce(axis, tasks, collective_id):
    plan = [ring_chunks(block.shape[1], step) for block, step, _ in tasks]
    copies = [copies_of(axis, chunks) for chunks in plan]

    def kernel(*refs):
        ring_reduce_kernel(axis, plan, *refs)

    boxes = [
        pltpu.VMEM((number, step, block.shape[2]), block.dtype)
        for number, (block, step, _) in zip(copies, tasks)
    ]
    return pl.pallas_call(
        kernel,
        out_shape=[jax.ShapeDtypeStruct(block.shape[1:], kind) for block, _, kind in tasks],
        in_specs=[pl.BlockSpec(memory_space=pltpu.VMEM)] * len(tasks),
        out_specs=[pl.BlockSpec(memory_space=pltpu.VMEM)] * len(tasks),
        scratch_shapes=boxes
        + boxes
        + [pltpu.SemaphoreType.DMA((sum(copies),)), pltpu.SemaphoreType.DMA((sum(copies),))],
        compiler_params=pltpu.CompilerParams(collective_id=collective_id, has_side_effects=True),
    )(*[block for block, _, _ in tasks])


def group_exchange_kernel(in_ref, out_ref, send_sem, recv_sem, local_sem):
    here = lax.axis_index("expert")
    y, z, core = here // (NZ * NC), (here // NC) % NZ, here % NC
    me = y * NC + core

    def device(member):
        return {"expert": ((member // NC) * NZ + z) * NC + member % NC}

    peers = [(me + k) % GROUP for k in range(1, GROUP)]
    greet([device(peer) for peer in peers])
    copies = []
    for k, peer in enumerate(peers):
        copy = pltpu.make_async_remote_copy(
            src_ref=in_ref.at[peer],
            dst_ref=out_ref.at[me],
            send_sem=send_sem.at[k],
            recv_sem=recv_sem.at[k],
            device_id=device(peer),
            device_id_type=MESH,
        )
        copy.start()
        copies.append(copy)
    own = pltpu.make_async_copy(in_ref.at[me], out_ref.at[me], local_sem)
    own.start()
    for copy in copies:
        copy.wait_recv()
    for copy in copies:
        copy.wait_send()
    own.wait()


def group_exchange(blocks, collective_id):
    return pl.pallas_call(
        group_exchange_kernel,
        out_shape=jax.ShapeDtypeStruct(blocks.shape, blocks.dtype),
        in_specs=[pl.BlockSpec(memory_space=pltpu.VMEM)],
        out_specs=pl.BlockSpec(memory_space=pltpu.VMEM),
        scratch_shapes=[
            pltpu.SemaphoreType.DMA((GROUP - 1,)),
            pltpu.SemaphoreType.DMA((GROUP - 1,)),
            pltpu.SemaphoreType.DMA,
        ],
        compiler_params=pltpu.CompilerParams(collective_id=collective_id, has_side_effects=True),
    )(blocks)


def slot_tables(table, tokens, top):
    picks = table[:, :top, :tokens].transpose(1, 0, 2).reshape(top, NZ * tokens)
    gates = table[:, 8 : 8 + top, :tokens].transpose(1, 0, 2).reshape(top, NZ * tokens)
    z = (lax.axis_index("expert") // NC) % NZ
    member = jnp.arange(GROUP)
    experts = ((member // NC) * NZ + z) * NC + member % NC
    match = picks[None] == experts.astype(jnp.float32)[:, None, None]
    hit = jnp.any(match, axis=1)
    gate = jnp.sum(jnp.where(match, gates[None], 0.0), axis=1)
    column = jnp.arange(NZ * tokens)
    page = column // tokens
    earlier = (page[:, None] == page[None, :]) & (column[:, None] < column[None, :])
    rank = jnp.dot(
        hit.astype(jnp.bfloat16), earlier.astype(jnp.bfloat16), preferred_element_type=jnp.float32
    )
    slot = jnp.arange(NZ * CAP)
    here = (slot // CAP)[:, None] == page[None, :]
    ranked = rank[:, None, :] == (slot % CAP).astype(jnp.float32)[None, :, None]
    chosen = here[None] & ranked & hit[:, None, :]
    select = chosen.astype(jnp.bfloat16).reshape(GROUP * NZ * CAP, NZ * tokens)
    gated = jnp.where(chosen, gate[:, None, :], 0.0).reshape(GROUP * NZ * CAP, NZ * tokens)
    return select, gated


def per_device(
    patches,
    norm1_gain,
    qkv_weight,
    qkv_bias,
    out_weight,
    out_bias,
    norm2_gain,
    proj_weight,
    moe_gain,
    expert_in,
    expert_out,
    shared_in,
    shared_out,
    routes,
    gates,
):
    tile_id = lax.axis_index("tile")
    row_count = patches.shape[1]
    columns = patches.shape[2]
    width_vit = patches.shape[3]
    local_rows = row_count * columns
    tokens = local_rows // 4
    top = routes.shape[-1]
    project = lax.all_gather(proj_weight, "expert", axis=0, tiled=True)

    inputs = patches.reshape(local_rows, width_vit).astype(jnp.float32)
    normed = layer_norm(inputs, norm1_gain).astype(jnp.bfloat16)
    own_routes = lax.dynamic_index_in_dim(
        routes.reshape(NX, tokens, top), tile_id, 0, keepdims=False
    )
    table = jnp.zeros((16, 128), jnp.float32)
    table = table.at[:top, :tokens].set(own_routes.T.astype(jnp.float32))
    table = table.at[8 : 8 + top, :tokens].set(gates.reshape(tokens, top).T)
    piece, tables_z = ring_gather([("x", normed, 32), ("z", table, 16)], 0)
    piece = piece.reshape(NX * local_rows, width_vit)

    heads_here = qkv_weight.shape[2] // HD
    qkv_flat = qkv_weight.reshape(width_vit, -1)
    bias_rows = qkv_bias.reshape(1, 3, heads_here, HD)
    mixed = (
        jnp.dot(piece, qkv_flat, preferred_element_type=jnp.float32).reshape(
            piece.shape[0], 3, heads_here, HD
        )
        + bias_rows
    )
    tables = rope_tables(jnp.arange(piece.shape[0]), columns, HD)
    attended = attend(
        rotate(mixed[:, 0], tables).astype(jnp.bfloat16),
        rotate(mixed[:, 1], tables).astype(jnp.bfloat16),
        mixed[:, 2].astype(jnp.bfloat16),
        math.sqrt(HD),
    )
    partial_rows = (
        jnp.dot(attended, out_weight, preferred_element_type=jnp.float32)
        .astype(jnp.bfloat16)
        .reshape(NX, local_rows, width_vit)
    )
    (mixed_heads,) = ring_reduce("x", [(partial_rows, 32, jnp.float32)], 1)
    hidden = inputs + mixed_heads + out_bias
    normed_out = layer_norm(hidden, norm2_gain).astype(jnp.bfloat16)
    merged = (
        normed_out.reshape(row_count // 2, 2, columns // 2, 2, width_vit)
        .transpose(0, 2, 1, 3, 4)
        .reshape(tokens, 4 * width_vit)
    )
    (group_merged,) = ring_gather([("x", merged, 16)], 2)
    select, gated = slot_tables(tables_z, tokens, top)
    projected = jnp.dot(
        group_merged.reshape(NX * tokens, -1), project, preferred_element_type=jnp.float32
    ).astype(jnp.bfloat16)
    (pieces,) = ring_gather([("x", projected, 32)], 3)
    page_tokens = pieces.transpose(1, 0, 2).reshape(NX * tokens, -1)
    width_moe = page_tokens.shape[1]
    page_in = rms_norm(page_tokens.astype(jnp.float32), moe_gain).astype(jnp.bfloat16)
    tokens_moe = lax.dynamic_slice_in_dim(page_tokens, tile_id * tokens, tokens, 0)
    moe_in = lax.dynamic_slice_in_dim(page_in, tile_id * tokens, tokens, 0)

    shared_gated = jnp.dot(
        page_in, shared_in.reshape(width_moe, -1), preferred_element_type=jnp.float32
    ).reshape(NX * tokens, 2, -1)
    shared_hidden = (jax.nn.silu(shared_gated[:, 0]) * shared_gated[:, 1]).astype(jnp.bfloat16)
    shared_rows = (
        jnp.dot(shared_hidden, shared_out, preferred_element_type=jnp.float32)
        .astype(jnp.bfloat16)
        .reshape(NX, tokens, width_moe)
    )

    (ring_in,) = ring_gather([("z", moe_in, 16)], 4)
    outgoing = jnp.dot(
        select, ring_in.reshape(NZ * tokens, width_moe), preferred_element_type=jnp.float32
    ).astype(jnp.bfloat16)
    received = group_exchange(outgoing.reshape(GROUP, NZ * CAP, width_moe), 5)
    slots = GROUP * NZ * CAP
    (arrived,) = ring_gather([("x", received.reshape(slots, width_moe), 48)], 6)
    slot_rows = arrived.reshape(NX * slots, width_moe)
    hidden_in = jnp.dot(
        slot_rows, expert_in.reshape(width_moe, -1), preferred_element_type=jnp.float32
    ).reshape(slot_rows.shape[0], 2, -1)
    expert_hidden = (jax.nn.silu(hidden_in[:, 0]) * hidden_in[:, 1]).astype(jnp.bfloat16)
    partial_out = (
        jnp.dot(
            expert_hidden,
            expert_out.reshape(expert_hidden.shape[1], width_moe),
            preferred_element_type=jnp.float32,
        )
        .astype(jnp.bfloat16)
        .reshape(NX, slots, width_moe)
    )
    results, shared_part = ring_reduce(
        "x", [(partial_out, 48, jnp.bfloat16), (shared_rows, 16, jnp.float32)], 7
    )
    returned = group_exchange(results.reshape(GROUP, NZ * CAP, width_moe), 8).reshape(
        slots, width_moe
    )
    gated_high = lax.reduce_precision(gated, 8, 7)
    gated_low = (gated - gated_high).astype(jnp.bfloat16)
    contract = (((0,), (0,)), ((), ()))
    weighted = lax.dot_general(
        gated_high.astype(jnp.bfloat16), returned, contract, preferred_element_type=jnp.float32
    ) + lax.dot_general(gated_low, returned, contract, preferred_element_type=jnp.float32)
    (routed,) = ring_reduce(
        "z", [(weighted.astype(jnp.bfloat16).reshape(NZ, tokens, width_moe), 16, jnp.float32)], 9
    )
    output = tokens_moe.astype(jnp.float32) + shared_part + routed
    return output.astype(jnp.bfloat16).reshape(1, row_count // 2, columns // 2, width_moe)


def solution(mesh):
    placed = (
        P("expert", "tile", None, None),
        P(),
        P(None, None, "tile"),
        P(None, "tile"),
        P("tile", None),
        P(),
        P(),
        P("expert", "tile"),
        P(),
        P("expert", None, None, "tile"),
        P("expert", "tile", None),
        P(None, None, "tile"),
        P("tile", None),
        P("expert", None, None, None),
        P("expert", "tile", None, None),
    )
    return jax.shard_map(
        per_device,
        mesh=mesh,
        in_specs=placed,
        out_specs=P("expert", "tile", None, None),
        check_vma=False,
    )
```

```python
import math

import jax
import jax.numpy as jnp
from jax import lax
from jax.experimental import pallas as pl
from jax.experimental.pallas import tpu as pltpu
from jax.sharding import PartitionSpec as P

HD = 72
NX, NY, NZ, NC = 4, 4, 8, 2
GROUP = NY * NC
CAP = 6
MESH = pl.DeviceIdType.MESH

norm_eps = 1e-06
rope_base = 10000.0


def layer_norm(values, gain_vec):
    centre = values - jnp.mean(values, axis=-1, keepdims=True)
    spread = jnp.mean(centre * centre, axis=-1, keepdims=True)
    return centre * lax.rsqrt(spread + norm_eps) * gain_vec


def rms_norm(values, gain_vec):
    return (
        values * lax.rsqrt(jnp.mean(values * values, axis=-1, keepdims=True) + norm_eps) * gain_vec
    )


def rope_tables(positions, columns, head_size):
    quarter = head_size // 4
    inverse = jnp.exp(jnp.arange(quarter).astype(jnp.float32) * (-math.log(rope_base) / quarter))
    row_angle = (positions // columns).astype(jnp.float32)[:, None] * inverse[None, :]
    col_angle = (positions % columns).astype(jnp.float32)[:, None] * inverse[None, :]
    return (jnp.cos(row_angle), jnp.sin(row_angle), jnp.cos(col_angle), jnp.sin(col_angle))


def rotate(values, tables):
    cos_row, sin_row, cos_col, sin_col = tables
    quarter = values.shape[-1] // 4
    row_a = values[..., :quarter]
    row_b = values[..., quarter : 2 * quarter]
    col_a = values[..., 2 * quarter : 3 * quarter]
    col_b = values[..., 3 * quarter :]
    return jnp.concatenate(
        [
            row_a * cos_row[:, None] - row_b * sin_row[:, None],
            row_b * cos_row[:, None] + row_a * sin_row[:, None],
            col_a * cos_col[:, None] - col_b * sin_col[:, None],
            col_b * cos_col[:, None] + col_a * sin_col[:, None],
        ],
        axis=-1,
    )


def attend(query_rows, key_rows, value_rows, divisor):
    scores = (
        jnp.einsum("qhd,khd->hqk", query_rows, key_rows, preferred_element_type=jnp.float32)
        / divisor
    )
    weights = jax.nn.softmax(scores, axis=-1).astype(jnp.bfloat16)
    attended = jnp.einsum(
        "hqk,khd->qhd", weights, value_rows, preferred_element_type=jnp.float32
    ).astype(jnp.bfloat16)
    return attended.reshape(attended.shape[0], -1)


def ring_place(axis):
    if axis == "x":
        return lax.axis_index("tile"), NX, lambda place: {"tile": place}
    here = lax.axis_index("expert")
    y, z, core = here // (NZ * NC), (here // NC) % NZ, here % NC
    return z, NZ, lambda place: {"expert": (y * NZ + place) * NC + core}


def greet(device_ids):
    barrier = pltpu.get_barrier_semaphore()
    for device_id in device_ids:
        pl.semaphore_signal(barrier, inc=1, device_id=device_id, device_id_type=MESH)
    pl.semaphore_wait(barrier, len(device_ids))


def ring_chunks(rows, step):
    starts = list(range(0, rows, step))
    half = (len(starts) + 1) // 2
    return [(s, step, 1 if i < half else -1) for i, s in enumerate(starts)]


def dir_order(chunks, sign):
    ids = range(len(chunks))
    return [i for i in ids if chunks[i][2] == sign] + [i for i in ids if chunks[i][2] != sign]


def interleave(a, b):
    out = []
    for i in range(max(len(a), len(b))):
        out += a[i : i + 1] + b[i : i + 1]
    return out


def ring_gather_kernel(plan, *refs):
    count = len(plan)
    ins, outs = refs[:count], refs[count : 2 * count]
    send_sem, recv_sem, local_sem = refs[2 * count :]
    rings = {axis: ring_place(axis) for axis, _ in plan}
    greet(
        [
            device((here + sign) % size)
            for here, size, device in rings.values()
            for sign in (1, -1)
        ]
    )
    arrivals, sends, number = {}, [], 0
    longest = max(rings[axis][1] // 2 for axis, _ in plan)
    local = []
    for hop in range(1, longest + 1):
        for task, (axis, chunks) in enumerate(plan):
            here, size, device = rings[axis]
            if hop > size // 2:
                continue
            order = interleave(
                [(1, i) for i in dir_order(chunks, 1)], [(-1, i) for i in dir_order(chunks, -1)]
            )
            for sign, i in order:
                start, rows, far = chunks[i]
                if hop == size // 2 and far != sign:
                    continue
                block = (here - sign * (hop - 1) + size) % size
                part = pl.ds(start, rows)
                if hop == 1:
                    source = ins[task].at[part]
                else:
                    arrivals.pop((task, sign, i)).wait_recv()
                    source = outs[task].at[block, part]
                copy = pltpu.make_async_remote_copy(
                    src_ref=source,
                    dst_ref=outs[task].at[block, part],
                    send_sem=send_sem.at[number],
                    recv_sem=recv_sem.at[number],
                    device_id=device((here + sign + size) % size),
                    device_id_type=MESH,
                )
                copy.start()
                arrivals[(task, sign, i)] = copy
                sends.append(copy)
                number += 1
        if hop == 1:
            for task, (axis, _) in enumerate(plan):
                own = pltpu.make_async_copy(
                    ins[task], outs[task].at[rings[axis][0]], local_sem.at[task]
                )
                own.start()
                local.append(own)
    for copy in arrivals.values():
        copy.wait_recv()
    for copy in sends:
        copy.wait_send()
    for own in local:
        own.wait()


def copies_of(axis, chunks):
    half = (NX if axis == "x" else NZ) // 2
    return sum(half + half - 1 for _ in chunks)


def ring_gather(tasks, collective_id):
    plan = [(axis, ring_chunks(block.shape[0], step)) for axis, block, step in tasks]
    copies = sum(copies_of(*entry) for entry in plan)
    sizes = {"x": NX, "z": NZ}

    def kernel(*refs):
        ring_gather_kernel(plan, *refs)

    return pl.pallas_call(
        kernel,
        out_shape=[
            jax.ShapeDtypeStruct((sizes[axis],) + block.shape, block.dtype)
            for axis, block, _ in tasks
        ],
        in_specs=[pl.BlockSpec(memory_space=pltpu.VMEM)] * len(tasks),
        out_specs=[pl.BlockSpec(memory_space=pltpu.VMEM)] * len(tasks),
        scratch_shapes=[
            pltpu.SemaphoreType.DMA((copies,)),
            pltpu.SemaphoreType.DMA((copies,)),
            pltpu.SemaphoreType.DMA((len(tasks),)),
        ],
        compiler_params=pltpu.CompilerParams(collective_id=collective_id, has_side_effects=True),
    )(*[block for _, block, _ in tasks])


def ring_reduce_kernel(plan, *refs):
    count = len(plan)
    ins, outs = refs[:count], refs[count : 2 * count]
    landed, staged = refs[2 * count : 3 * count], refs[3 * count : 4 * count]
    send_sem, recv_sem = refs[4 * count :]
    rings = {axis: ring_place(axis) for axis, _ in plan}
    greet(
        [
            device((here + sign + size) % size)
            for here, size, device in rings.values()
            for sign in (1, -1)
        ]
    )
    last, sends, number = {}, [], 0
    slots = [0] * count
    for step in range(max(rings[axis][1] // 2 for axis, _ in plan)):
        for task, (axis, chunks) in enumerate(plan):
            here, size, device = rings[axis]
            half = size // 2
            order = interleave(
                [(1, i) for i in dir_order(chunks, 1)], [(-1, i) for i in dir_order(chunks, -1)]
            )
            for sign, i in order:
                start, rows, far = chunks[i]
                length = half if far == sign else half - 1
                if step >= length:
                    continue
                part = pl.ds(start, rows)
                target = (here + sign * (length - step) + size) % size
                slot = slots[task]
                slots[task] += 1
                if step == 0:
                    source = ins[task].at[target, part]
                else:
                    copy, before = last[(task, sign, i)]
                    copy.wait_recv()
                    staged[task][slot] = (
                        ins[task][target, part].astype(jnp.float32)
                        + landed[task][before].astype(jnp.float32)
                    ).astype(staged[task].dtype)
                    source = staged[task].at[slot]
                copy = pltpu.make_async_remote_copy(
                    src_ref=source,
                    dst_ref=landed[task].at[slot],
                    send_sem=send_sem.at[number],
                    recv_sem=recv_sem.at[number],
                    device_id=device((here + sign + size) % size),
                    device_id_type=MESH,
                )
                copy.start()
                last[(task, sign, i)] = (copy, slot)
                sends.append(copy)
                number += 1
    for task, (axis, chunks) in enumerate(plan):
        here = rings[axis][0]
        for i, (start, rows, _) in enumerate(chunks):
            part = pl.ds(start, rows)
            total = ins[task][here, part].astype(jnp.float32)
            for sign in (1, -1):
                if (task, sign, i) in last:
                    copy, slot = last[(task, sign, i)]
                    copy.wait_recv()
                    total = total + landed[task][slot].astype(jnp.float32)
            outs[task][part] = total.astype(outs[task].dtype)
    for copy in sends:
        copy.wait_send()


def ring_reduce(tasks, collective_id):
    plan = [(axis, ring_chunks(block.shape[1], step)) for axis, block, step, _ in tasks]
    copies = [copies_of(*entry) for entry in plan]

    def kernel(*refs):
        ring_reduce_kernel(plan, *refs)

    boxes = [
        pltpu.VMEM((number, step, block.shape[2]), block.dtype)
        for number, (_, block, step, _) in zip(copies, tasks)
    ]
    return pl.pallas_call(
        kernel,
        out_shape=[jax.ShapeDtypeStruct(block.shape[1:], kind) for _, block, _, kind in tasks],
        in_specs=[pl.BlockSpec(memory_space=pltpu.VMEM)] * len(tasks),
        out_specs=[pl.BlockSpec(memory_space=pltpu.VMEM)] * len(tasks),
        scratch_shapes=boxes
        + boxes
        + [pltpu.SemaphoreType.DMA((sum(copies),)), pltpu.SemaphoreType.DMA((sum(copies),))],
        compiler_params=pltpu.CompilerParams(collective_id=collective_id, has_side_effects=True),
    )(*[block for _, block, _, _ in tasks])


def group_exchange_kernel(in_ref, out_ref, send_sem, recv_sem, local_sem):
    here = lax.axis_index("expert")
    y, z, core = here // (NZ * NC), (here // NC) % NZ, here % NC
    me = y * NC + core

    def device(member):
        return {"expert": ((member // NC) * NZ + z) * NC + member % NC}

    peers = [(me + k) % GROUP for k in range(1, GROUP)]
    greet([device(peer) for peer in peers])
    copies = []
    for k, peer in enumerate(peers):
        copy = pltpu.make_async_remote_copy(
            src_ref=in_ref.at[peer],
            dst_ref=out_ref.at[me],
            send_sem=send_sem.at[k],
            recv_sem=recv_sem.at[k],
            device_id=device(peer),
            device_id_type=MESH,
        )
        copy.start()
        copies.append(copy)
    own = pltpu.make_async_copy(in_ref.at[me], out_ref.at[me], local_sem)
    own.start()
    for copy in copies:
        copy.wait_recv()
    for copy in copies:
        copy.wait_send()
    own.wait()


def group_exchange(blocks, collective_id):
    return pl.pallas_call(
        group_exchange_kernel,
        out_shape=jax.ShapeDtypeStruct(blocks.shape, blocks.dtype),
        in_specs=[pl.BlockSpec(memory_space=pltpu.VMEM)],
        out_specs=pl.BlockSpec(memory_space=pltpu.VMEM),
        scratch_shapes=[
            pltpu.SemaphoreType.DMA((GROUP - 1,)),
            pltpu.SemaphoreType.DMA((GROUP - 1,)),
            pltpu.SemaphoreType.DMA,
        ],
        compiler_params=pltpu.CompilerParams(collective_id=collective_id, has_side_effects=True),
    )(blocks)


def slot_tables(table, tokens, top):
    picks = table[:, :top, :tokens].transpose(1, 0, 2).reshape(top, NZ * tokens)
    gates = table[:, 8 : 8 + top, :tokens].transpose(1, 0, 2).reshape(top, NZ * tokens)
    z = (lax.axis_index("expert") // NC) % NZ
    member = jnp.arange(GROUP)
    experts = ((member // NC) * NZ + z) * NC + member % NC
    match = picks[None] == experts.astype(jnp.float32)[:, None, None]
    hit = jnp.any(match, axis=1)
    gate = jnp.sum(jnp.where(match, gates[None], 0.0), axis=1)
    column = jnp.arange(NZ * tokens)
    page = column // tokens
    earlier = (page[:, None] == page[None, :]) & (column[:, None] < column[None, :])
    rank = jnp.dot(
        hit.astype(jnp.bfloat16), earlier.astype(jnp.bfloat16), preferred_element_type=jnp.float32
    )
    slot = jnp.arange(NZ * CAP)
    here = (slot // CAP)[:, None] == page[None, :]
    ranked = rank[:, None, :] == (slot % CAP).astype(jnp.float32)[None, :, None]
    chosen = here[None] & ranked & hit[:, None, :]
    select = chosen.astype(jnp.bfloat16).reshape(GROUP * NZ * CAP, NZ * tokens)
    gated = jnp.where(chosen, gate[:, None, :], 0.0).reshape(GROUP * NZ * CAP, NZ * tokens)
    return select, gated


def per_device(
    patches,
    norm1_gain,
    qkv_weight,
    qkv_bias,
    out_weight,
    out_bias,
    norm2_gain,
    proj_weight,
    moe_gain,
    expert_in,
    expert_out,
    shared_in,
    shared_out,
    routes,
    gates,
):
    tile_id = lax.axis_index("tile")
    row_count = patches.shape[1]
    columns = patches.shape[2]
    width_vit = patches.shape[3]
    local_rows = row_count * columns
    tokens = local_rows // 4
    top = routes.shape[-1]
    pieces_in, pieces_out = [expert_in], [expert_out]
    for shift in range(1, NX):
        ring = [(t, (t + shift) % NX) for t in range(NX)]
        pieces_in.append(lax.ppermute(expert_in, "tile", ring))
        pieces_out.append(lax.ppermute(expert_out, "tile", ring))
    project = lax.all_gather(proj_weight, "expert", axis=0, tiled=True)

    inputs = patches.reshape(local_rows, width_vit).astype(jnp.float32)
    normed = layer_norm(inputs, norm1_gain).astype(jnp.bfloat16)
    own_routes = lax.dynamic_index_in_dim(
        routes.reshape(NX, tokens, top), tile_id, 0, keepdims=False
    )
    table = jnp.zeros((16, 128), jnp.float32)
    table = table.at[:top, :tokens].set(own_routes.T.astype(jnp.float32))
    table = table.at[8 : 8 + top, :tokens].set(gates.reshape(tokens, top).T)
    piece, tables_z = ring_gather([("x", normed, 32), ("z", table, 16)], 0)
    piece = piece.reshape(NX * local_rows, width_vit)

    heads_here = qkv_weight.shape[2] // HD
    qkv_flat = qkv_weight.reshape(width_vit, -1)
    bias_rows = qkv_bias.reshape(1, 3, heads_here, HD)
    mixed = (
        jnp.dot(piece, qkv_flat, preferred_element_type=jnp.float32).reshape(
            piece.shape[0], 3, heads_here, HD
        )
        + bias_rows
    )
    tables = rope_tables(jnp.arange(piece.shape[0]), columns, HD)
    attended = attend(
        rotate(mixed[:, 0], tables).astype(jnp.bfloat16),
        rotate(mixed[:, 1], tables).astype(jnp.bfloat16),
        mixed[:, 2].astype(jnp.bfloat16),
        math.sqrt(HD),
    )
    partial_rows = (
        jnp.dot(attended, out_weight, preferred_element_type=jnp.float32)
        .astype(jnp.bfloat16)
        .reshape(NX, local_rows, width_vit)
    )
    (mixed_heads,) = ring_reduce([("x", partial_rows, 32, jnp.float32)], 1)
    hidden = inputs + mixed_heads + out_bias
    normed_out = layer_norm(hidden, norm2_gain).astype(jnp.bfloat16)
    merged = (
        normed_out.reshape(row_count // 2, 2, columns // 2, 2, width_vit)
        .transpose(0, 2, 1, 3, 4)
        .reshape(tokens, 4 * width_vit)
    )
    (group_merged,) = ring_gather([("x", merged, 16)], 2)
    select, gated = slot_tables(tables_z, tokens, top)
    projected = jnp.dot(
        group_merged.reshape(NX * tokens, -1), project, preferred_element_type=jnp.float32
    ).astype(jnp.bfloat16)
    (pieces,) = ring_gather([("x", projected, 32)], 3)
    page_tokens = pieces.transpose(1, 0, 2).reshape(NX * tokens, -1)
    width_moe = page_tokens.shape[1]
    page_in = rms_norm(page_tokens.astype(jnp.float32), moe_gain).astype(jnp.bfloat16)
    tokens_moe = lax.dynamic_slice_in_dim(page_tokens, tile_id * tokens, tokens, 0)
    moe_in = lax.dynamic_slice_in_dim(page_in, tile_id * tokens, tokens, 0)

    shared_gated = jnp.dot(
        page_in, shared_in.reshape(width_moe, -1), preferred_element_type=jnp.float32
    ).reshape(NX * tokens, 2, -1)
    shared_hidden = (jax.nn.silu(shared_gated[:, 0]) * shared_gated[:, 1]).astype(jnp.bfloat16)
    shared_rows = (
        jnp.dot(shared_hidden, shared_out, preferred_element_type=jnp.float32)
        .astype(jnp.bfloat16)
        .reshape(NX, tokens, width_moe)
    )

    (ring_in,) = ring_gather([("z", moe_in, 16)], 4)
    outgoing = jnp.dot(
        select, ring_in.reshape(NZ * tokens, width_moe), preferred_element_type=jnp.float32
    ).astype(jnp.bfloat16)
    received = group_exchange(outgoing.reshape(GROUP, NZ * CAP, width_moe), 5)
    slots = GROUP * NZ * CAP
    slot_rows = received.reshape(slots, width_moe)
    total = jnp.zeros((slots, width_moe), jnp.float32)
    for piece_in, piece_out in zip(pieces_in, pieces_out):
        hidden_in = jnp.dot(
            slot_rows, piece_in.reshape(width_moe, -1), preferred_element_type=jnp.float32
        ).reshape(slots, 2, -1)
        expert_hidden = (jax.nn.silu(hidden_in[:, 0]) * hidden_in[:, 1]).astype(jnp.bfloat16)
        partial_out = jnp.dot(
            expert_hidden, piece_out.reshape(-1, width_moe), preferred_element_type=jnp.float32
        ).astype(jnp.bfloat16)
        total = total + partial_out.astype(jnp.float32)
    results = total.astype(jnp.bfloat16)
    returned = group_exchange(results.reshape(GROUP, NZ * CAP, width_moe), 8).reshape(
        slots, width_moe
    )
    gated_high = lax.reduce_precision(gated, 8, 7)
    gated_low = (gated - gated_high).astype(jnp.bfloat16)
    contract = (((0,), (0,)), ((), ()))
    weighted = lax.dot_general(
        gated_high.astype(jnp.bfloat16), returned, contract, preferred_element_type=jnp.float32
    ) + lax.dot_general(gated_low, returned, contract, preferred_element_type=jnp.float32)
    routed, shared_part = ring_reduce(
        [
            ("z", weighted.astype(jnp.bfloat16).reshape(NZ, tokens, width_moe), 16, jnp.float32),
            ("x", shared_rows, 16, jnp.float32),
        ],
        9,
    )
    output = tokens_moe.astype(jnp.float32) + shared_part + routed
    return output.astype(jnp.bfloat16).reshape(1, row_count // 2, columns // 2, width_moe)


def solution(mesh):
    placed = (
        P("expert", "tile", None, None),
        P(),
        P(None, None, "tile"),
        P(None, "tile"),
        P("tile", None),
        P(),
        P(),
        P("expert", "tile"),
        P(),
        P("expert", None, None, "tile"),
        P("expert", "tile", None),
        P(None, None, "tile"),
        P("tile", None),
        P("expert", None, None, None),
        P("expert", "tile", None, None),
    )
    return jax.shard_map(
        per_device,
        mesh=mesh,
        in_specs=placed,
        out_specs=P("expert", "tile", None, None),
        check_vma=False,
    )
```

```python
import math

import jax
import jax.numpy as jnp
from jax import lax
from jax.experimental import pallas as pl
from jax.experimental.pallas import tpu as pltpu
from jax.sharding import PartitionSpec as P


HD = 72
NX, NY, NZ, NC = 4, 4, 8, 2
GROUP = NY * NC
CAP = 6
MESH = pl.DeviceIdType.MESH

norm_eps = 1e-06
rope_base = 10000.0


def layer_norm(values, gain_vec):
    centre = values - jnp.mean(values, axis=-1, keepdims=True)
    spread = jnp.mean(centre * centre, axis=-1, keepdims=True)
    return centre * lax.rsqrt(spread + norm_eps) * gain_vec


def rms_norm(values, gain_vec):
    return (
        values * lax.rsqrt(jnp.mean(values * values, axis=-1, keepdims=True) + norm_eps) * gain_vec
    )


def rope_tables(positions, columns, head_size):
    quarter = head_size // 4
    inverse = jnp.exp(jnp.arange(quarter).astype(jnp.float32) * (-math.log(rope_base) / quarter))
    row_angle = (positions // columns).astype(jnp.float32)[:, None] * inverse[None, :]
    col_angle = (positions % columns).astype(jnp.float32)[:, None] * inverse[None, :]
    return (jnp.cos(row_angle), jnp.sin(row_angle), jnp.cos(col_angle), jnp.sin(col_angle))


def rotate(values, tables):
    cos_row, sin_row, cos_col, sin_col = tables
    quarter = values.shape[-1] // 4
    row_a = values[..., :quarter]
    row_b = values[..., quarter : 2 * quarter]
    col_a = values[..., 2 * quarter : 3 * quarter]
    col_b = values[..., 3 * quarter :]
    return jnp.concatenate(
        [
            row_a * cos_row[:, None] - row_b * sin_row[:, None],
            row_b * cos_row[:, None] + row_a * sin_row[:, None],
            col_a * cos_col[:, None] - col_b * sin_col[:, None],
            col_b * cos_col[:, None] + col_a * sin_col[:, None],
        ],
        axis=-1,
    )


def attend(query_rows, key_rows, value_rows, divisor):
    scores = (
        jnp.einsum("qhd,khd->hqk", query_rows, key_rows, preferred_element_type=jnp.float32)
        / divisor
    )
    weights = jax.nn.softmax(scores, axis=-1).astype(jnp.bfloat16)
    attended = jnp.einsum(
        "hqk,khd->qhd", weights, value_rows, preferred_element_type=jnp.float32
    ).astype(jnp.bfloat16)
    return attended.reshape(attended.shape[0], -1)


def ring_place(axis):
    if axis == "x":
        return lax.axis_index("tile"), NX, lambda place: {"tile": place}
    here = lax.axis_index("expert")
    y, z, core = here // (NZ * NC), (here // NC) % NZ, here % NC
    return z, NZ, lambda place: {"expert": (y * NZ + place) * NC + core}


def greet(device_ids):
    barrier = pltpu.get_barrier_semaphore()
    for device_id in device_ids:
        pl.semaphore_signal(barrier, inc=1, device_id=device_id, device_id_type=MESH)
    pl.semaphore_wait(barrier, len(device_ids))


def ring_chunks(rows, step):
    starts = list(range(0, rows, step))
    half = (len(starts) + 1) // 2
    return [(s, step, 1 if i < half else -1) for i, s in enumerate(starts)]


def dir_order(chunks, sign):
    ids = range(len(chunks))
    return [i for i in ids if chunks[i][2] == sign] + [i for i in ids if chunks[i][2] != sign]


def interleave(a, b):
    out = []
    for i in range(max(len(a), len(b))):
        out += a[i : i + 1] + b[i : i + 1]
    return out


def ring_gather_kernel(plan, *refs):
    count = len(plan)
    ins, outs = refs[:count], refs[count : 2 * count]
    send_sem, recv_sem, local_sem = refs[2 * count :]
    rings = {axis: ring_place(axis) for axis, _ in plan}
    greet(
        [
            device((here + sign) % size)
            for here, size, device in rings.values()
            for sign in (1, -1)
        ]
    )
    arrivals, sends, number = {}, [], 0
    longest = max(rings[axis][1] // 2 for axis, _ in plan)
    local = []
    for hop in range(1, longest + 1):
        for task, (axis, chunks) in enumerate(plan):
            here, size, device = rings[axis]
            if hop > size // 2:
                continue
            order = interleave(
                [(1, i) for i in dir_order(chunks, 1)], [(-1, i) for i in dir_order(chunks, -1)]
            )
            for sign, i in order:
                start, rows, far = chunks[i]
                if hop == size // 2 and far != sign:
                    continue
                block = (here - sign * (hop - 1) + size) % size
                part = pl.ds(start, rows)
                if hop == 1:
                    source = ins[task].at[part]
                else:
                    arrivals.pop((task, sign, i)).wait_recv()
                    source = outs[task].at[block, part]
                copy = pltpu.make_async_remote_copy(
                    src_ref=source,
                    dst_ref=outs[task].at[block, part],
                    send_sem=send_sem.at[number],
                    recv_sem=recv_sem.at[number],
                    device_id=device((here + sign + size) % size),
                    device_id_type=MESH,
                )
                copy.start()
                arrivals[(task, sign, i)] = copy
                sends.append(copy)
                number += 1
        if hop == 1:
            for task, (axis, _) in enumerate(plan):
                own = pltpu.make_async_copy(
                    ins[task], outs[task].at[rings[axis][0]], local_sem.at[task]
                )
                own.start()
                local.append(own)
    for copy in arrivals.values():
        copy.wait_recv()
    for copy in sends:
        copy.wait_send()
    for own in local:
        own.wait()


def copies_of(axis, chunks):
    half = (NX if axis == "x" else NZ) // 2
    return sum(half + half - 1 for _ in chunks)


def ring_gather(tasks, collective_id):
    plan = [(axis, ring_chunks(block.shape[0], step)) for axis, block, step in tasks]
    copies = sum(copies_of(*entry) for entry in plan)
    sizes = {"x": NX, "z": NZ}

    def kernel(*refs):
        ring_gather_kernel(plan, *refs)

    return pl.pallas_call(
        kernel,
        out_shape=[
            jax.ShapeDtypeStruct((sizes[axis],) + block.shape, block.dtype)
            for axis, block, _ in tasks
        ],
        in_specs=[pl.BlockSpec(memory_space=pltpu.VMEM)] * len(tasks),
        out_specs=[pl.BlockSpec(memory_space=pltpu.VMEM)] * len(tasks),
        scratch_shapes=[
            pltpu.SemaphoreType.DMA((copies,)),
            pltpu.SemaphoreType.DMA((copies,)),
            pltpu.SemaphoreType.DMA((len(tasks),)),
        ],
        compiler_params=pltpu.CompilerParams(collective_id=collective_id, has_side_effects=True),
    )(*[block for _, block, _ in tasks])


def ring_reduce_kernel(plan, *refs):
    count = len(plan)
    ins, outs = refs[:count], refs[count : 2 * count]
    landed, staged = refs[2 * count : 3 * count], refs[3 * count : 4 * count]
    send_sem, recv_sem = refs[4 * count :]
    rings = {axis: ring_place(axis) for axis, _ in plan}
    greet(
        [
            device((here + sign + size) % size)
            for here, size, device in rings.values()
            for sign in (1, -1)
        ]
    )
    last, sends, number = {}, [], 0
    slots = [0] * count
    for step in range(max(rings[axis][1] // 2 for axis, _ in plan)):
        for task, (axis, chunks) in enumerate(plan):
            here, size, device = rings[axis]
            half = size // 2
            order = interleave(
                [(1, i) for i in dir_order(chunks, 1)], [(-1, i) for i in dir_order(chunks, -1)]
            )
            for sign, i in order:
                start, rows, far = chunks[i]
                length = half if far == sign else half - 1
                if step >= length:
                    continue
                part = pl.ds(start, rows)
                target = (here + sign * (length - step) + size) % size
                slot = slots[task]
                slots[task] += 1
                if step == 0:
                    source = ins[task].at[target, part]
                else:
                    copy, before = last[(task, sign, i)]
                    copy.wait_recv()
                    staged[task][slot] = (
                        ins[task][target, part].astype(jnp.float32)
                        + landed[task][before].astype(jnp.float32)
                    ).astype(staged[task].dtype)
                    source = staged[task].at[slot]
                copy = pltpu.make_async_remote_copy(
                    src_ref=source,
                    dst_ref=landed[task].at[slot],
                    send_sem=send_sem.at[number],
                    recv_sem=recv_sem.at[number],
                    device_id=device((here + sign + size) % size),
                    device_id_type=MESH,
                )
                copy.start()
                last[(task, sign, i)] = (copy, slot)
                sends.append(copy)
                number += 1
    for task, (axis, chunks) in enumerate(plan):
        here = rings[axis][0]
        for i, (start, rows, _) in enumerate(chunks):
            part = pl.ds(start, rows)
            total = ins[task][here, part].astype(jnp.float32)
            for sign in (1, -1):
                if (task, sign, i) in last:
                    copy, slot = last[(task, sign, i)]
                    copy.wait_recv()
                    total = total + landed[task][slot].astype(jnp.float32)
            outs[task][part] = total.astype(outs[task].dtype)
    for copy in sends:
        copy.wait_send()


def ring_reduce(tasks, collective_id):
    plan = [(axis, ring_chunks(block.shape[1], step)) for axis, block, step, _ in tasks]
    copies = [copies_of(*entry) for entry in plan]

    def kernel(*refs):
        ring_reduce_kernel(plan, *refs)

    boxes = [
        pltpu.VMEM((number, step, block.shape[2]), block.dtype)
        for number, (_, block, step, _) in zip(copies, tasks)
    ]
    return pl.pallas_call(
        kernel,
        out_shape=[jax.ShapeDtypeStruct(block.shape[1:], kind) for _, block, _, kind in tasks],
        in_specs=[pl.BlockSpec(memory_space=pltpu.VMEM)] * len(tasks),
        out_specs=[pl.BlockSpec(memory_space=pltpu.VMEM)] * len(tasks),
        scratch_shapes=boxes
        + boxes
        + [pltpu.SemaphoreType.DMA((sum(copies),)), pltpu.SemaphoreType.DMA((sum(copies),))],
        compiler_params=pltpu.CompilerParams(collective_id=collective_id, has_side_effects=True),
    )(*[block for _, block, _, _ in tasks])


CHUNKS = 4


def places():
    tile, here = lax.axis_index("tile"), lax.axis_index("expert")
    y, z, core = here // (NZ * NC), (here // NC) % NZ, here % NC
    across = {"tile": tile + 1 - 2 * (tile % 2)}, {"tile": NX - 1 - tile}

    def group(member):
        return {"expert": ((member // NC) * NZ + z) * NC + member % NC}

    def ring(place):
        return {"expert": (y * NZ + place) * NC + core}

    return tile, z, y * NC + core, across, group, ring


class Sender:
    def __init__(self, send_sem, recv_sem):
        self.send_sem, self.recv_sem, self.made = send_sem, recv_sem, []

    def send(self, source, target, device):
        number = len(self.made)
        copy = pltpu.make_async_remote_copy(
            src_ref=source,
            dst_ref=target,
            send_sem=self.send_sem.at[number],
            recv_sem=self.recv_sem.at[number],
            device_id=device,
            device_id_type=MESH,
        )
        copy.start()
        self.made.append(copy)
        return copy


Z_HALF = NZ // 2
Z_STREAMS = [(sign, half, Z_HALF if (half == 0) == (sign == 1) else Z_HALF - 1)
             for sign in (1, -1) for half in (0, 1)]
Z_STREAMS.sort(key=lambda stream: -stream[2])
X_HALF = NX // 2
X_STREAMS = [(sign, half, X_HALF if (half == 0) == (sign == 1) else X_HALF - 1)
             for sign in (1, -1) for half in (0, 1)]
X_STREAMS.sort(key=lambda stream: -stream[2])
Z_COPIES = sum(length for _, _, length in Z_STREAMS)
X_COPIES = sum(length for _, _, length in X_STREAMS)


def dispatch_kernel(
    rows_ref, select_ref, shared_ref, out_ref, sum_ref, ring_ref, chosen_ref, land_ref, stage_ref,
    send_sem, recv_sem, local_sem,
):
    tile, z, me, across, group, ring = places()
    tokens, width = rows_ref.shape
    chunk, half_rows = width // CHUNKS, tokens // 2
    post = Sender(send_sem, recv_sem)
    peers = [(me + k) % GROUP for k in range(1, GROUP)]
    greet(
        [ring((z + 1) % NZ), ring((z + NZ - 1) % NZ)]
        + [group(peer) for peer in peers]
        + list(across)
    )
    cols = [pl.ds(j * chunk, chunk) for j in range(CHUNKS)]
    part = [pl.ds(h * half_rows, half_rows) for h in (0, 1)]
    arrivals = {}

    def hop(j, number):
        for sign, half, length in Z_STREAMS:
            if number > length:
                continue
            block = (z - sign * (number - 1) + NZ) % NZ
            if number == 1:
                source = rows_ref.at[part[half], cols[j]]
            else:
                arrivals[(j, sign, half)].wait_recv()
                source = ring_ref.at[j, block, part[half]]
            arrivals[(j, sign, half)] = post.send(
                source, ring_ref.at[j, block, part[half]], ring((z + sign + NZ) % NZ)
            )

    for j in range(CHUNKS):
        hop(j, 1)

    sums = {}

    def shared_step(step):
        for sign, half, length in X_STREAMS:
            if step >= length:
                continue
            target = (tile + sign * (length - step) + NX) % NX
            slot = len(sums)
            if step == 0:
                source = shared_ref.at[target, part[half]]
            else:
                copy, before = sums[(sign, half, step - 1)]
                copy.wait_recv()
                stage_ref[slot] = (
                    shared_ref[target, part[half]].astype(jnp.float32)
                    + land_ref[before].astype(jnp.float32)
                ).astype(stage_ref.dtype)
                source = stage_ref.at[slot]
            copy = post.send(source, land_ref.at[slot], {"tile": (tile + sign + NX) % NX})
            sums[(sign, half, step)] = (copy, slot)

    shared_step(0)
    for j in range(CHUNKS):
        ring_ref[j, z] = rows_ref[:, j * chunk : (j + 1) * chunk]

    swaps, own = {}, []

    def hand_on(j, member, source):
        for side in (0, 1):
            post_to = out_ref.at[2 * side, member, :, cols[j]]
            handed.append(post.send(source, post_to, across[side]))

    handed = []

    def choose(j):
        for sign, half, _ in Z_STREAMS:
            arrivals[(j, sign, half)].wait_recv()
        gathered = ring_ref[j].reshape(NZ * tokens, chunk)
        chosen_ref[j] = (
            jnp.dot(select_ref[...], gathered, preferred_element_type=jnp.float32)
            .astype(chosen_ref.dtype)
            .reshape(chosen_ref.shape[1:])
        )
        for k, peer in enumerate(peers):
            swaps[(j, k)] = post.send(
                chosen_ref.at[j, peer], out_ref.at[1, me, :, cols[j]], group(peer)
            )
        copy = pltpu.make_async_copy(
            chosen_ref.at[j, me], out_ref.at[1, me, :, cols[j]], local_sem.at[j]
        )
        copy.start()
        own.append(copy)
        hand_on(j, me, chosen_ref.at[j, me])

    for wave in range(CHUNKS + Z_HALF - 1):
        for number in range(Z_HALF, 1, -1):
            j = wave - (number - 2)
            if 0 <= j < CHUNKS:
                hop(j, number)
        j = wave - (Z_HALF - 1)
        if wave == 0:
            shared_step(1)
        if 0 <= j < CHUNKS:
            choose(j)
    for j in range(CHUNKS):
        for k in range(GROUP - 1):
            swaps[(j, k)].wait_recv()
            source = (me - 1 - k + GROUP) % GROUP
            hand_on(j, source, out_ref.at[1, source, :, cols[j]])
    for half in (0, 1):
        total = shared_ref[tile, part[half]].astype(jnp.float32)
        for sign, this, length in X_STREAMS:
            if this == half:
                copy, slot = sums[(sign, half, length - 1)]
                copy.wait_recv()
                total = total + land_ref[slot].astype(jnp.float32)
        sum_ref[part[half]] = total
    for copy in handed:
        copy.wait_recv()
    for copy in post.made:
        copy.wait_send()
    for copy in own:
        copy.wait()


def dispatch(rows, select, shared_rows, collective_id):
    tokens, width = rows.shape
    slots = NZ * CAP
    chunk = width // CHUNKS
    copies = CHUNKS * (Z_COPIES + (GROUP - 1) + 2 * GROUP) + X_COPIES
    return pl.pallas_call(
        dispatch_kernel,
        out_shape=[
            jax.ShapeDtypeStruct((3, GROUP, slots, width), rows.dtype),
            jax.ShapeDtypeStruct((tokens, width), jnp.float32),
        ],
        in_specs=[pl.BlockSpec(memory_space=pltpu.VMEM)] * 3,
        out_specs=[pl.BlockSpec(memory_space=pltpu.VMEM)] * 2,
        scratch_shapes=[
            pltpu.VMEM((CHUNKS, NZ, tokens, chunk), rows.dtype),
            pltpu.VMEM((CHUNKS, GROUP, slots, chunk), rows.dtype),
            pltpu.VMEM((X_COPIES, tokens // 2, width), rows.dtype),
            pltpu.VMEM((X_COPIES, tokens // 2, width), rows.dtype),
            pltpu.SemaphoreType.DMA((copies,)),
            pltpu.SemaphoreType.DMA((copies,)),
            pltpu.SemaphoreType.DMA((CHUNKS,)),
        ],
        compiler_params=pltpu.CompilerParams(collective_id=collective_id, has_side_effects=True),
    )(rows, select, shared_rows)


def give_back_kernel(
    first_ref, second_ref, gated_ref, out_ref, high_ref, low_ref, side_ref, stage_ref, back_ref, mix_ref,
    land_ref, step_ref, send_sem, recv_sem,
):
    _, z, me, across, group, ring = places()
    tokens, width = out_ref.shape
    chunk, half_rows = width // CHUNKS, tokens // 2
    post = Sender(send_sem, recv_sem)
    peers = [(me + k) % GROUP for k in range(1, GROUP)]
    greet(
        [ring((z + 1) % NZ), ring((z + NZ - 1) % NZ)]
        + [group(peer) for peer in peers]
        + list(across)
    )
    cols = [pl.ds(j * chunk, chunk) for j in range(CHUNKS)]
    part = [pl.ds(h * half_rows, half_rows) for h in (0, 1)]
    order = peers + [me]
    sides, swaps, steps = {}, {}, {}
    for j in range(CHUNKS):
        for k, member in enumerate(order):
            for side, source in ((0, first_ref.at[0]), (1, second_ref.at[1])):
                sides[(j, k, side)] = post.send(
                    source.at[member, :, cols[j]], side_ref.at[side, j, member], across[side]
                )

    gated = gated_ref[...].T
    high = gated.astype(high_ref.dtype)
    high_ref[...] = high
    low_ref[...] = (gated - high.astype(jnp.float32)).astype(low_ref.dtype)

    def add_up(j):
        for k, member in enumerate(order):
            for side in (0, 1):
                sides[(j, k, side)].wait_recv()
            total = (
                first_ref[1, member, :, j * chunk : (j + 1) * chunk].astype(jnp.float32)
                + second_ref[0, member, :, j * chunk : (j + 1) * chunk].astype(jnp.float32)
                + side_ref[0, j, member].astype(jnp.float32)
                + side_ref[1, j, member].astype(jnp.float32)
            ).astype(stage_ref.dtype)
            if k == GROUP - 1:
                back_ref[j, member] = total
            else:
                stage_ref[j, member] = total
                swaps[(j, k)] = post.send(
                    stage_ref.at[j, member], back_ref.at[j, me], group(member)
                )

    def step(j, number):
        for i, (sign, half, length) in enumerate(Z_STREAMS):
            if number >= length:
                continue
            target = (z + sign * (length - number) + NZ) % NZ
            slot = i * Z_HALF + number
            if number == 0:
                source = mix_ref.at[j, target, part[half]]
            else:
                steps[(j, i, number - 1)].wait_recv()
                step_ref[j, slot] = (
                    mix_ref[j, target, part[half]].astype(jnp.float32)
                    + land_ref[j, slot - 1].astype(jnp.float32)
                ).astype(step_ref.dtype)
                source = step_ref.at[j, slot]
            steps[(j, i, number)] = post.send(
                source, land_ref.at[j, slot], ring((z + sign + NZ) % NZ)
            )

    def combine(j):
        for k in range(GROUP - 1):
            swaps[(j, k)].wait_recv()
        back = back_ref[j].reshape(high_ref.shape[1], chunk)
        mix_ref[j] = (
            (
                jnp.dot(high_ref[...], back, preferred_element_type=jnp.float32)
                + jnp.dot(low_ref[...], back, preferred_element_type=jnp.float32)
            )
            .astype(mix_ref.dtype)
            .reshape(mix_ref.shape[1:])
        )
        step(j, 0)

    def finish(j):
        for half in (0, 1):
            total = mix_ref[j, z, part[half]].astype(jnp.float32)
            for i, (_, this, length) in enumerate(Z_STREAMS):
                if this == half:
                    steps[(j, i, length - 1)].wait_recv()
                    total = total + land_ref[j, i * Z_HALF + length - 1].astype(jnp.float32)
            out_ref[half * half_rows : (half + 1) * half_rows, j * chunk : (j + 1) * chunk] = total

    for wave in range(CHUNKS + Z_HALF + 1):
        if wave < CHUNKS:
            add_up(wave)
        if 0 <= wave - 1 < CHUNKS:
            combine(wave - 1)
        for number in range(1, Z_HALF):
            if 0 <= wave - 1 - number < CHUNKS:
                step(wave - 1 - number, number)
    for j in range(CHUNKS):
        finish(j)
    for copy in post.made:
        copy.wait_send()


def give_back(first, second, gated, tokens, collective_id):
    width = first.shape[-1]
    slots = NZ * CAP
    chunk = width // CHUNKS
    copies = CHUNKS * (2 * GROUP + (GROUP - 1) + Z_COPIES)
    boxes = pltpu.VMEM((CHUNKS, len(Z_STREAMS) * Z_HALF, tokens // 2, chunk), first.dtype)
    blocks = pltpu.VMEM((CHUNKS, GROUP, slots, chunk), first.dtype)
    return pl.pallas_call(
        give_back_kernel,
        out_shape=jax.ShapeDtypeStruct((tokens, width), jnp.float32),
        in_specs=[pl.BlockSpec(memory_space=pltpu.VMEM)] * 3,
        out_specs=pl.BlockSpec(memory_space=pltpu.VMEM),
        scratch_shapes=[
            pltpu.VMEM(gated.shape[::-1], first.dtype),
            pltpu.VMEM(gated.shape[::-1], first.dtype),
            pltpu.VMEM((2, CHUNKS, GROUP, slots, chunk), first.dtype),
            blocks,
            blocks,
            pltpu.VMEM((CHUNKS, NZ, tokens, chunk), first.dtype),
            boxes,
            boxes,
            pltpu.SemaphoreType.DMA((copies,)),
            pltpu.SemaphoreType.DMA((copies,)),
        ],
        compiler_params=pltpu.CompilerParams(collective_id=collective_id, has_side_effects=True),
    )(first, second, gated)


def slot_tables(table, tokens, top):
    picks = table[:, :top, :tokens].transpose(1, 0, 2).reshape(top, NZ * tokens)
    gates = table[:, 8 : 8 + top, :tokens].transpose(1, 0, 2).reshape(top, NZ * tokens)
    z = (lax.axis_index("expert") // NC) % NZ
    member = jnp.arange(GROUP)
    experts = ((member // NC) * NZ + z) * NC + member % NC
    match = picks[None] == experts.astype(jnp.float32)[:, None, None]
    hit = jnp.any(match, axis=1)
    gate = jnp.sum(jnp.where(match, gates[None], 0.0), axis=1)
    column = jnp.arange(NZ * tokens)
    page = column // tokens
    earlier = (page[:, None] == page[None, :]) & (column[:, None] < column[None, :])
    rank = jnp.dot(
        hit.astype(jnp.bfloat16), earlier.astype(jnp.bfloat16), preferred_element_type=jnp.float32
    )
    slot = jnp.arange(NZ * CAP)
    here = (slot // CAP)[:, None] == page[None, :]
    ranked = rank[:, None, :] == (slot % CAP).astype(jnp.float32)[None, :, None]
    chosen = here[None] & ranked & hit[:, None, :]
    select = chosen.astype(jnp.bfloat16).reshape(GROUP * NZ * CAP, NZ * tokens)
    gated = jnp.where(chosen, gate[:, None, :], 0.0).reshape(GROUP * NZ * CAP, NZ * tokens)
    return select, gated


def per_device(
    patches,
    norm1_gain,
    qkv_weight,
    qkv_bias,
    out_weight,
    out_bias,
    norm2_gain,
    proj_weight,
    moe_gain,
    expert_in,
    expert_out,
    shared_in,
    shared_out,
    routes,
    gates,
):
    tile_id = lax.axis_index("tile")
    row_count = patches.shape[1]
    columns = patches.shape[2]
    width_vit = patches.shape[3]
    local_rows = row_count * columns
    tokens = local_rows // 4
    top = routes.shape[-1]
    side_a = [(t, t + 1 - 2 * (t % 2)) for t in range(NX)]
    side_b = [(t, NX - 1 - t) for t in range(NX)]
    units = expert_out.shape[1] // 2
    gate_halves, up_halves = (
        [expert_in[0, :, which, i * units : (i + 1) * units] for i in (0, 1)] for which in (0, 1)
    )
    out_halves = [expert_out[0, i * units : (i + 1) * units] for i in (0, 1)]

    def swap(halves, after):
        first, second, after = lax.optimization_barrier((halves[0], halves[1], after))
        from_a = lax.ppermute(first, "tile", side_a)
        from_b = lax.ppermute(second, "tile", side_b)
        return from_a, from_b, after

    project = lax.all_gather(proj_weight, "expert", axis=0, tiled=True)

    inputs = patches.reshape(local_rows, width_vit).astype(jnp.float32)
    normed = layer_norm(inputs, norm1_gain).astype(jnp.bfloat16)
    own_routes = lax.dynamic_index_in_dim(
        routes.reshape(NX, tokens, top), tile_id, 0, keepdims=False
    )
    table = jnp.zeros((16, 128), jnp.float32)
    table = table.at[:top, :tokens].set(own_routes.T.astype(jnp.float32))
    table = table.at[8 : 8 + top, :tokens].set(gates.reshape(tokens, top).T)
    piece, tables_z = ring_gather([("x", normed, 32), ("z", table, 16)], 0)
    out_a, out_b, piece = swap(out_halves, piece)
    piece = piece.reshape(NX * local_rows, width_vit)

    heads_here = qkv_weight.shape[2] // HD
    qkv_flat = qkv_weight.reshape(width_vit, -1)
    bias_rows = qkv_bias.reshape(1, 3, heads_here, HD)
    mixed_flat = jnp.dot(piece, qkv_flat, preferred_element_type=jnp.float32)
    mixed = (
        mixed_flat.reshape(
            piece.shape[0], 3, heads_here, HD
        )
        + bias_rows
    )
    tables = rope_tables(jnp.arange(piece.shape[0]), columns, HD)
    attended = attend(
        rotate(mixed[:, 0], tables).astype(jnp.bfloat16),
        rotate(mixed[:, 1], tables).astype(jnp.bfloat16),
        mixed[:, 2].astype(jnp.bfloat16),
        math.sqrt(HD),
    )
    partial_rows = (
        jnp.dot(attended, out_weight, preferred_element_type=jnp.float32)
        .astype(jnp.bfloat16)
        .reshape(NX, local_rows, width_vit)
    )
    (mixed_heads,) = ring_reduce([("x", partial_rows, 32, jnp.float32)], 1)
    hidden = inputs + mixed_heads + out_bias
    normed_out = layer_norm(hidden, norm2_gain).astype(jnp.bfloat16)
    merged = (
        normed_out.reshape(row_count // 2, 2, columns // 2, 2, width_vit)
        .transpose(0, 2, 1, 3, 4)
        .reshape(tokens, 4 * width_vit)
    )
    (group_merged,) = ring_gather([("x", merged, 16)], 2)
    gate_a, gate_b, group_merged = swap(gate_halves, group_merged)
    select, gated = slot_tables(tables_z, tokens, top)
    projected = jnp.dot(
        group_merged.reshape(NX * tokens, -1), project, preferred_element_type=jnp.float32
    ).astype(jnp.bfloat16)
    (pieces,) = ring_gather([("x", projected, 32)], 3)
    up_a, up_b, pieces = swap(up_halves, pieces)
    page_tokens = pieces.transpose(1, 0, 2).reshape(NX * tokens, -1)
    width_moe = page_tokens.shape[1]
    page_in = rms_norm(page_tokens.astype(jnp.float32), moe_gain).astype(jnp.bfloat16)
    tokens_moe = lax.dynamic_slice_in_dim(page_tokens, tile_id * tokens, tokens, 0)
    moe_in = lax.dynamic_slice_in_dim(page_in, tile_id * tokens, tokens, 0)

    shared_gated = jnp.dot(
        page_in, shared_in.reshape(width_moe, -1), preferred_element_type=jnp.float32
    ).reshape(NX * tokens, 2, -1)
    shared_hidden = (jax.nn.silu(shared_gated[:, 0]) * shared_gated[:, 1]).astype(jnp.bfloat16)
    shared_rows = (
        jnp.dot(shared_hidden, shared_out, preferred_element_type=jnp.float32)
        .astype(jnp.bfloat16)
        .reshape(NX, tokens, width_moe)
    )

    arrived, shared_part = dispatch(moe_in, select, shared_rows, 4)
    slots = GROUP * NZ * CAP
    arrived = arrived.reshape(3 * slots, width_moe)

    def feed_forward(rows, halves):
        hidden_rows = []
        for gate_piece, up_piece, _ in halves:
            gate_rows = jnp.dot(rows, gate_piece, preferred_element_type=jnp.float32)
            up_rows = jnp.dot(rows, up_piece, preferred_element_type=jnp.float32)
            hidden_rows.append((jax.nn.silu(gate_rows) * up_rows).astype(jnp.bfloat16))
        total = jnp.dot(
            jnp.concatenate(hidden_rows, axis=1),
            jnp.concatenate([out_piece for _, _, out_piece in halves]),
            preferred_element_type=jnp.float32,
        )
        return total.astype(jnp.bfloat16).reshape(2, GROUP, NZ * CAP, width_moe)

    second = feed_forward(
        arrived[slots:], [(gate_halves[0], up_halves[0], out_halves[0]), (gate_a, up_a, out_a)]
    )
    first = feed_forward(
        arrived[: 2 * slots], [(gate_halves[1], up_halves[1], out_halves[1]), (gate_b, up_b, out_b)]
    )
    routed = give_back(first, second, gated, tokens, 5)
    output = tokens_moe.astype(jnp.float32) + shared_part + routed
    return output.astype(jnp.bfloat16).reshape(1, row_count // 2, columns // 2, width_moe)


def solution(mesh):
    placed = (
        P("expert", "tile", None, None),
        P(),
        P(None, None, "tile"),
        P(None, "tile"),
        P("tile", None),
        P(),
        P(),
        P("expert", "tile"),
        P(),
        P("expert", None, None, "tile"),
        P("expert", "tile", None),
        P(None, None, "tile"),
        P("tile", None),
        P("expert", None, None, None),
        P("expert", "tile", None, None),
    )
    return jax.shard_map(
        per_device,
        mesh=mesh,
        in_specs=placed,
        out_specs=P("expert", "tile", None, None),
        check_vma=False,
    )
```

```python
import math

import jax
import jax.numpy as jnp
from jax import lax
from jax.experimental import pallas as pl
from jax.experimental.pallas import tpu as pltpu
from jax.sharding import PartitionSpec as P


HD = 72
NX, NY, NZ, NC = 4, 4, 8, 2
GROUP = NY * NC
CAP = 6
MESH = pl.DeviceIdType.MESH

norm_eps = 1e-06
rope_base = 10000.0


def layer_norm(values, gain_vec):
    centre = values - jnp.mean(values, axis=-1, keepdims=True)
    spread = jnp.mean(centre * centre, axis=-1, keepdims=True)
    return centre * lax.rsqrt(spread + norm_eps) * gain_vec


def rope_tables(positions, columns, head_size):
    quarter = head_size // 4
    inverse = jnp.exp(jnp.arange(quarter).astype(jnp.float32) * (-math.log(rope_base) / quarter))
    row_angle = (positions // columns).astype(jnp.float32)[:, None] * inverse[None, :]
    col_angle = (positions % columns).astype(jnp.float32)[:, None] * inverse[None, :]
    return (jnp.cos(row_angle), jnp.sin(row_angle), jnp.cos(col_angle), jnp.sin(col_angle))


def rotate(values, tables):
    cos_row, sin_row, cos_col, sin_col = tables
    quarter = values.shape[-1] // 4
    row_a = values[..., :quarter]
    row_b = values[..., quarter : 2 * quarter]
    col_a = values[..., 2 * quarter : 3 * quarter]
    col_b = values[..., 3 * quarter :]
    return jnp.concatenate(
        [
            row_a * cos_row[:, None] - row_b * sin_row[:, None],
            row_b * cos_row[:, None] + row_a * sin_row[:, None],
            col_a * cos_col[:, None] - col_b * sin_col[:, None],
            col_b * cos_col[:, None] + col_a * sin_col[:, None],
        ],
        axis=-1,
    )


def attend(query_rows, key_rows, value_rows, divisor):
    scores = (
        jnp.einsum("qhd,khd->hqk", query_rows, key_rows, preferred_element_type=jnp.float32)
        / divisor
    )
    weights = jax.nn.softmax(scores, axis=-1).astype(jnp.bfloat16)
    attended = jnp.einsum(
        "hqk,khd->qhd", weights, value_rows, preferred_element_type=jnp.float32
    ).astype(jnp.bfloat16)
    return attended.reshape(attended.shape[0], -1)


def ring_place(axis):
    if axis == "x":
        return lax.axis_index("tile"), NX, lambda place: {"tile": place}
    here = lax.axis_index("expert")
    y, z, core = here // (NZ * NC), (here // NC) % NZ, here % NC
    return z, NZ, lambda place: {"expert": (y * NZ + place) * NC + core}


def greet(device_ids):
    barrier = pltpu.get_barrier_semaphore()
    for device_id in device_ids:
        pl.semaphore_signal(barrier, inc=1, device_id=device_id, device_id_type=MESH)
    pl.semaphore_wait(barrier, len(device_ids))


def ring_chunks(rows, step):
    starts = list(range(0, rows, step))
    half = (len(starts) + 1) // 2
    return [(s, step, 1 if i < half else -1) for i, s in enumerate(starts)]


def dir_order(chunks, sign):
    ids = range(len(chunks))
    return [i for i in ids if chunks[i][2] == sign] + [i for i in ids if chunks[i][2] != sign]


def interleave(a, b):
    out = []
    for i in range(max(len(a), len(b))):
        out += a[i : i + 1] + b[i : i + 1]
    return out


def ring_gather_kernel(plan, *refs):
    count = len(plan)
    ins, outs = refs[:count], refs[count : 2 * count]
    send_sem, recv_sem, local_sem = refs[2 * count :]
    rings = {axis: ring_place(axis) for axis, _ in plan}
    greet(
        [
            device((here + sign) % size)
            for here, size, device in rings.values()
            for sign in (1, -1)
        ]
    )
    arrivals, sends, number = {}, [], 0
    longest = max(rings[axis][1] // 2 for axis, _ in plan)
    local = []
    for hop in range(1, longest + 1):
        for task, (axis, chunks) in enumerate(plan):
            here, size, device = rings[axis]
            if hop > size // 2:
                continue
            order = interleave(
                [(1, i) for i in dir_order(chunks, 1)], [(-1, i) for i in dir_order(chunks, -1)]
            )
            for sign, i in order:
                start, rows, far = chunks[i]
                if hop == size // 2 and far != sign:
                    continue
                block = (here - sign * (hop - 1) + size) % size
                part = pl.ds(start, rows)
                if hop == 1:
                    source = ins[task].at[part]
                else:
                    arrivals.pop((task, sign, i)).wait_recv()
                    source = outs[task].at[block, part]
                copy = pltpu.make_async_remote_copy(
                    src_ref=source,
                    dst_ref=outs[task].at[block, part],
                    send_sem=send_sem.at[number],
                    recv_sem=recv_sem.at[number],
                    device_id=device((here + sign + size) % size),
                    device_id_type=MESH,
                )
                copy.start()
                arrivals[(task, sign, i)] = copy
                sends.append(copy)
                number += 1
        if hop == 1:
            for task, (axis, _) in enumerate(plan):
                own = pltpu.make_async_copy(
                    ins[task], outs[task].at[rings[axis][0]], local_sem.at[task]
                )
                own.start()
                local.append(own)
    for copy in arrivals.values():
        copy.wait_recv()
    for copy in sends:
        copy.wait_send()
    for own in local:
        own.wait()


def copies_of(axis, chunks):
    half = (NX if axis == "x" else NZ) // 2
    return sum(half + half - 1 for _ in chunks)


def ring_gather(tasks, collective_id):
    plan = [(axis, ring_chunks(block.shape[0], step)) for axis, block, step in tasks]
    copies = sum(copies_of(*entry) for entry in plan)
    sizes = {"x": NX, "z": NZ}

    def kernel(*refs):
        ring_gather_kernel(plan, *refs)

    return pl.pallas_call(
        kernel,
        out_shape=[
            jax.ShapeDtypeStruct((sizes[axis],) + block.shape, block.dtype)
            for axis, block, _ in tasks
        ],
        in_specs=[pl.BlockSpec(memory_space=pltpu.VMEM)] * len(tasks),
        out_specs=[pl.BlockSpec(memory_space=pltpu.VMEM)] * len(tasks),
        scratch_shapes=[
            pltpu.SemaphoreType.DMA((copies,)),
            pltpu.SemaphoreType.DMA((copies,)),
            pltpu.SemaphoreType.DMA((len(tasks),)),
        ],
        compiler_params=pltpu.CompilerParams(collective_id=collective_id, has_side_effects=True),
    )(*[block for _, block, _ in tasks])


def ring_reduce_kernel(plan, *refs):
    count = len(plan)
    ins, outs = refs[:count], refs[count : 2 * count]
    landed, staged = refs[2 * count : 3 * count], refs[3 * count : 4 * count]
    send_sem, recv_sem = refs[4 * count :]
    rings = {axis: ring_place(axis) for axis, _ in plan}
    greet(
        [
            device((here + sign + size) % size)
            for here, size, device in rings.values()
            for sign in (1, -1)
        ]
    )
    last, sends, number = {}, [], 0
    slots = [0] * count
    for step in range(max(rings[axis][1] // 2 for axis, _ in plan)):
        for task, (axis, chunks) in enumerate(plan):
            here, size, device = rings[axis]
            half = size // 2
            order = interleave(
                [(1, i) for i in dir_order(chunks, 1)], [(-1, i) for i in dir_order(chunks, -1)]
            )
            for sign, i in order:
                start, rows, far = chunks[i]
                length = half if far == sign else half - 1
                if step >= length:
                    continue
                part = pl.ds(start, rows)
                target = (here + sign * (length - step) + size) % size
                slot = slots[task]
                slots[task] += 1
                if step == 0:
                    source = ins[task].at[target, part]
                else:
                    copy, before = last[(task, sign, i)]
                    copy.wait_recv()
                    staged[task][slot] = (
                        ins[task][target, part].astype(jnp.float32)
                        + landed[task][before].astype(jnp.float32)
                    ).astype(staged[task].dtype)
                    source = staged[task].at[slot]
                copy = pltpu.make_async_remote_copy(
                    src_ref=source,
                    dst_ref=landed[task].at[slot],
                    send_sem=send_sem.at[number],
                    recv_sem=recv_sem.at[number],
                    device_id=device((here + sign + size) % size),
                    device_id_type=MESH,
                )
                copy.start()
                last[(task, sign, i)] = (copy, slot)
                sends.append(copy)
                number += 1
    for task, (axis, chunks) in enumerate(plan):
        here = rings[axis][0]
        for i, (start, rows, _) in enumerate(chunks):
            part = pl.ds(start, rows)
            total = ins[task][here, part].astype(jnp.float32)
            for sign in (1, -1):
                if (task, sign, i) in last:
                    copy, slot = last[(task, sign, i)]
                    copy.wait_recv()
                    total = total + landed[task][slot].astype(jnp.float32)
            outs[task][part] = total.astype(outs[task].dtype)
    for copy in sends:
        copy.wait_send()


def ring_reduce(tasks, collective_id):
    plan = [(axis, ring_chunks(block.shape[1], step)) for axis, block, step, _ in tasks]
    copies = [copies_of(*entry) for entry in plan]

    def kernel(*refs):
        ring_reduce_kernel(plan, *refs)

    boxes = [
        pltpu.VMEM((number, step, block.shape[2]), block.dtype)
        for number, (_, block, step, _) in zip(copies, tasks)
    ]
    return pl.pallas_call(
        kernel,
        out_shape=[jax.ShapeDtypeStruct(block.shape[1:], kind) for _, block, _, kind in tasks],
        in_specs=[pl.BlockSpec(memory_space=pltpu.VMEM)] * len(tasks),
        out_specs=[pl.BlockSpec(memory_space=pltpu.VMEM)] * len(tasks),
        scratch_shapes=boxes
        + boxes
        + [pltpu.SemaphoreType.DMA((sum(copies),)), pltpu.SemaphoreType.DMA((sum(copies),))],
        compiler_params=pltpu.CompilerParams(collective_id=collective_id, has_side_effects=True),
    )(*[block for _, block, _, _ in tasks])


CHUNKS = 4


def places():
    tile, here = lax.axis_index("tile"), lax.axis_index("expert")
    y, z, core = here // (NZ * NC), (here // NC) % NZ, here % NC
    across = {"tile": tile + 1 - 2 * (tile % 2)}, {"tile": NX - 1 - tile}

    def group(member):
        return {"expert": ((member // NC) * NZ + z) * NC + member % NC}

    def ring(place):
        return {"expert": (y * NZ + place) * NC + core}

    return tile, z, y * NC + core, across, group, ring


class Sender:
    def __init__(self, send_sem, recv_sem):
        self.send_sem, self.recv_sem, self.made = send_sem, recv_sem, []

    def send(self, source, target, device):
        number = len(self.made)
        copy = pltpu.make_async_remote_copy(
            src_ref=source,
            dst_ref=target,
            send_sem=self.send_sem.at[number],
            recv_sem=self.recv_sem.at[number],
            device_id=device,
            device_id_type=MESH,
        )
        copy.start()
        self.made.append(copy)
        return copy


Z_HALF = NZ // 2
Z_STREAMS = [(sign, half, Z_HALF if (half == 0) == (sign == 1) else Z_HALF - 1)
             for sign in (1, -1) for half in (0, 1)]
Z_STREAMS.sort(key=lambda stream: -stream[2])
X_HALF = NX // 2
X_STREAMS = [(sign, half, X_HALF if (half == 0) == (sign == 1) else X_HALF - 1)
             for sign in (1, -1) for half in (0, 1)]
X_STREAMS.sort(key=lambda stream: -stream[2])
Z_COPIES = sum(length for _, _, length in Z_STREAMS)
X_COPIES = sum(length for _, _, length in X_STREAMS)


PER_JOB = GROUP // 2


def expert_kernel(
    rows_ref, select_ref, shared_ref, gated_ref, tokens_ref, in_ref, down_ref,
    gate_a_ref, up_a_ref, down_a_ref, gate_b_ref, up_b_ref, down_b_ref,
    out_ref,
    ring_ref, chosen_ref, sum_land_ref, sum_stage_ref, slots_ref, weight_ref, hidden_ref, part_ref,
    high_ref, low_ref, side_ref, stage_ref, back_ref, mix_ref, land_ref, step_ref, base_ref,
    send_sem, recv_sem, local_sem, weight_sem, side_send, side_recv,
):
    tile, z, me, across, group, ring = places()
    tokens, width = rows_ref.shape
    chunk, half_rows = width // CHUNKS, tokens // 2
    slots = NZ * CAP
    units = down_a_ref.shape[0]
    post = Sender(send_sem, recv_sem)
    peers = [(me + k) % GROUP for k in range(1, GROUP)]
    low_units, high_units = pl.ds(0, units), pl.ds(units, units)
    loads = []
    for where, source in (
        ((0, 0, 0), in_ref.at[0, high_units]),
        ((0, 0, 1), in_ref.at[1, high_units]),
        ((0, 0, 2), down_ref.at[high_units]),
        ((0, 1, 0), gate_b_ref),
        ((0, 1, 1), up_b_ref),
        ((0, 1, 2), down_b_ref),
        ((1, 0, 0), in_ref.at[0, low_units]),
        ((1, 0, 1), in_ref.at[1, low_units]),
        ((1, 0, 2), down_ref.at[low_units]),
        ((1, 1, 0), gate_a_ref),
        ((1, 1, 1), up_a_ref),
        ((1, 1, 2), down_a_ref),
    ):
        copy = pltpu.make_async_copy(source, weight_ref.at[where], weight_sem.at[len(loads)])
        copy.start()
        loads.append(copy)
    greet(
        [ring((z + 1) % NZ), ring((z + NZ - 1) % NZ)]
        + [group(peer) for peer in peers]
        + list(across)
    )
    cols = [pl.ds(j * chunk, chunk) for j in range(CHUNKS)]
    part = [pl.ds(h * half_rows, half_rows) for h in (0, 1)]
    arrivals = {}

    def hop(j, number):
        for sign, half, length in Z_STREAMS:
            if number > length:
                continue
            block = (z - sign * (number - 1) + NZ) % NZ
            if number == 1:
                source = rows_ref.at[part[half], cols[j]]
            else:
                arrivals[(j, sign, half)].wait_recv()
                source = ring_ref.at[j, block, part[half]]
            arrivals[(j, sign, half)] = post.send(
                source, ring_ref.at[j, block, part[half]], ring((z + sign + NZ) % NZ)
            )

    for j in range(CHUNKS):
        hop(j, 1)

    sums = {}

    def shared_step(step):
        for sign, half, length in X_STREAMS:
            if step >= length:
                continue
            target = (tile + sign * (length - step) + NX) % NX
            slot = len(sums)
            if step == 0:
                source = shared_ref.at[target, part[half]]
            else:
                copy, before = sums[(sign, half, step - 1)]
                copy.wait_recv()
                sum_stage_ref[slot] = (
                    shared_ref[target, part[half]].astype(jnp.float32)
                    + sum_land_ref[before].astype(jnp.float32)
                ).astype(sum_stage_ref.dtype)
                source = sum_stage_ref.at[slot]
            copy = post.send(source, sum_land_ref.at[slot], {"tile": (tile + sign + NX) % NX})
            sums[(sign, half, step)] = (copy, slot)

    shared_step(0)
    for j in range(CHUNKS):
        ring_ref[j, z] = rows_ref[:, j * chunk : (j + 1) * chunk]
    gated = gated_ref[...].T
    high = gated.astype(high_ref.dtype)
    high_ref[...] = high
    low_ref[...] = (gated - high.astype(jnp.float32)).astype(low_ref.dtype)

    swaps, own, handed = {}, [], []

    def hand_on(j, k, source):
        for side in (0, 1):
            handed.append(post.send(source, slots_ref.at[2 * side, k, :, cols[j]], across[side]))

    def choose(j):
        for sign, half, _ in Z_STREAMS:
            arrivals[(j, sign, half)].wait_recv()
        gathered = ring_ref[j].reshape(NZ * tokens, chunk)
        chosen_ref[j] = (
            jnp.dot(select_ref[...], gathered, preferred_element_type=jnp.float32)
            .astype(chosen_ref.dtype)
            .reshape(chosen_ref.shape[1:])
        )
        for k, peer in enumerate(peers, 1):
            swaps[(j, k)] = post.send(
                chosen_ref.at[j, peer], slots_ref.at[1, k, :, cols[j]], group(peer)
            )
        copy = pltpu.make_async_copy(
            chosen_ref.at[j, me], slots_ref.at[1, 0, :, cols[j]], local_sem.at[j]
        )
        copy.start()
        own.append(copy)
        hand_on(j, 0, chosen_ref.at[j, me])

    def forward(j):
        for k in range(1, GROUP):
            swaps[(j, k)].wait_recv()
            hand_on(j, k, slots_ref.at[1, k, :, cols[j]])

    for wave in range(CHUNKS + Z_HALF - 1):
        for number in range(Z_HALF, 1, -1):
            j = wave - (number - 2)
            if 0 <= j < CHUNKS:
                hop(j, number)
        if wave == 0:
            shared_step(1)
        j = wave - (Z_HALF - 1)
        if 0 <= j < CHUNKS:
            choose(j)
        if 0 <= j - 2 < CHUNKS:
            forward(j - 2)
    for j in range(CHUNKS - 2, CHUNKS):
        forward(j)

    def feed_forward(which, mine, job):
        first = job * PER_JOB
        place = 2 * which * (1 - mine) + mine
        rows = slots_ref[place, pl.ds(first, PER_JOB)].reshape(PER_JOB * slots, width)
        contract = (((1,), (1,)), ((), ()))
        for piece in (0, 1):
            gate = lax.dot_general(
                rows, weight_ref[which, piece, 0], contract, preferred_element_type=jnp.float32
            )
            up = lax.dot_general(
                rows, weight_ref[which, piece, 1], contract, preferred_element_type=jnp.float32
            )
            hidden_ref[piece] = (gate / (1.0 + jnp.exp(-gate)) * up).astype(hidden_ref.dtype)
        for j in range(CHUNKS):
            total = jnp.dot(
                hidden_ref[0], weight_ref[which, 0, 2, :, cols[j]],
                preferred_element_type=jnp.float32,
            ) + jnp.dot(
                hidden_ref[1], weight_ref[which, 1, 2, :, cols[j]],
                preferred_element_type=jnp.float32,
            )
            part_ref[which, mine, pl.ds(first, PER_JOB), :, cols[j]] = total.astype(
                part_ref.dtype
            ).reshape(PER_JOB, slots, chunk)

    def side_copy(which, j, k):
        number = (which * CHUNKS + j) * GROUP + k
        neighbour = tile + 1 - 2 * (tile % 2)
        other = NX - 1 - tile
        return pltpu.make_async_remote_copy(
            src_ref=part_ref.at[which, 0, k, :, cols[j]],
            dst_ref=side_ref.at[which, j, k],
            send_sem=side_send.at[number],
            recv_sem=side_recv.at[number],
            device_id={"tile": neighbour + which * (other - neighbour)},
            device_id_type=MESH,
        )

    for copy in loads + own:
        copy.wait()

    def own_job(i, carry):
        feed_forward(i % 2, 1, i // 2)
        return carry

    lax.fori_loop(0, 4, own_job, 0)
    for copy in handed:
        copy.wait_recv()

    def side_job(i, carry):
        which, job = i % 2, i // 2
        feed_forward(which, 0, job)
        for j in range(CHUNKS):
            for k in range(PER_JOB):
                side_copy(which, j, job * PER_JOB + k).start()
        return carry

    lax.fori_loop(0, 4, side_job, 0)

    for half in (0, 1):
        total = shared_ref[tile, part[half]].astype(jnp.float32)
        for sign, this, length in X_STREAMS:
            if this == half:
                copy, slot = sums[(sign, half, length - 1)]
                copy.wait_recv()
                total = total + sum_land_ref[slot].astype(jnp.float32)
        base_ref[part[half]] = total + tokens_ref[part[half]].astype(jnp.float32)
    returns, steps = {}, {}

    def add_up(j, ks):
        for k in ks:
            for which in (0, 1):
                side_copy(which, j, k).wait_recv()
            total = (
                part_ref[0, 1, k, :, cols[j]].astype(jnp.float32)
                + part_ref[1, 1, k, :, cols[j]].astype(jnp.float32)
                + side_ref[0, j, k].astype(jnp.float32)
                + side_ref[1, j, k].astype(jnp.float32)
            ).astype(stage_ref.dtype)
            if k == 0:
                back_ref[j, me] = total
            else:
                stage_ref[j, k] = total
                returns[(j, k)] = post.send(
                    stage_ref.at[j, k], back_ref.at[j, me], group((me - k + GROUP) % GROUP)
                )

    def step(j, number):
        for i, (sign, half, length) in enumerate(Z_STREAMS):
            if number >= length:
                continue
            target = (z + sign * (length - number) + NZ) % NZ
            slot = i * Z_HALF + number
            if number == 0:
                source = mix_ref.at[j, target, part[half]]
            else:
                steps[(j, i, number - 1)].wait_recv()
                step_ref[j, slot] = (
                    mix_ref[j, target, part[half]].astype(jnp.float32)
                    + land_ref[j, slot - 1].astype(jnp.float32)
                ).astype(step_ref.dtype)
                source = step_ref.at[j, slot]
            steps[(j, i, number)] = post.send(
                source, land_ref.at[j, slot], ring((z + sign + NZ) % NZ)
            )

    def combine(j):
        for k in range(1, GROUP):
            returns[(j, k)].wait_recv()
        back = back_ref[j].reshape(high_ref.shape[1], chunk)
        mix_ref[j] = (
            (
                jnp.dot(high_ref[...], back, preferred_element_type=jnp.float32)
                + jnp.dot(low_ref[...], back, preferred_element_type=jnp.float32)
            )
            .astype(mix_ref.dtype)
            .reshape(mix_ref.shape[1:])
        )
        step(j, 0)

    for j in range(CHUNKS):
        add_up(j, range(PER_JOB))
    for wave in range(CHUNKS + Z_HALF + 1):
        if wave < CHUNKS:
            add_up(wave, range(PER_JOB, GROUP))
        if 0 <= wave - 1 < CHUNKS:
            combine(wave - 1)
        for number in range(1, Z_HALF):
            if 0 <= wave - 1 - number < CHUNKS:
                step(wave - 1 - number, number)
    for j in range(CHUNKS):
        for half in (0, 1):
            total = base_ref[part[half], cols[j]] + mix_ref[j, z, part[half]].astype(
                jnp.float32
            )
            for i, (_, this, length) in enumerate(Z_STREAMS):
                if this == half:
                    steps[(j, i, length - 1)].wait_recv()
                    total = total + land_ref[j, i * Z_HALF + length - 1].astype(jnp.float32)
            out_ref[part[half], cols[j]] = total.astype(out_ref.dtype)
    for copy in post.made:
        copy.wait_send()
    for which in (0, 1):
        for j in range(CHUNKS):
            for k in range(GROUP):
                side_copy(which, j, k).wait_send()


def expert_layer(rows, select, shared_rows, gated, tokens_moe, weights, collective_id):
    tokens, width = rows.shape
    slots = NZ * CAP
    chunk = width // CHUNKS
    kind = rows.dtype
    units = weights[-1].shape[0]
    copies = CHUNKS * (2 * Z_COPIES + 2 * (GROUP - 1) + 2 * GROUP) + X_COPIES
    boxes = pltpu.VMEM((CHUNKS, len(Z_STREAMS) * Z_HALF, tokens // 2, chunk), kind)
    blocks = pltpu.VMEM((CHUNKS, GROUP, slots, chunk), kind)
    shared_boxes = pltpu.VMEM((X_COPIES, tokens // 2, width), kind)
    spread = pltpu.VMEM((CHUNKS, NZ, tokens, chunk), kind)
    return pl.pallas_call(
        expert_kernel,
        out_shape=jax.ShapeDtypeStruct((tokens, width), kind),
        in_specs=[pl.BlockSpec(memory_space=pltpu.VMEM)] * 5
        + [pl.BlockSpec(memory_space=pl.ANY)] * len(weights),
        out_specs=pl.BlockSpec(memory_space=pltpu.VMEM),
        scratch_shapes=[
            spread,
            blocks,
            shared_boxes,
            shared_boxes,
            pltpu.VMEM((3, GROUP, slots, width), kind),
            pltpu.VMEM((2, 2, 3, units, width), kind),
            pltpu.VMEM((2, PER_JOB * slots, units), kind),
            pltpu.VMEM((2, 2, GROUP, slots, width), kind),
            pltpu.VMEM(gated.shape[::-1], kind),
            pltpu.VMEM(gated.shape[::-1], kind),
            pltpu.VMEM((2, CHUNKS, GROUP, slots, chunk), kind),
            blocks,
            blocks,
            spread,
            boxes,
            boxes,
            pltpu.VMEM((tokens, width), jnp.float32),
            pltpu.SemaphoreType.DMA((copies,)),
            pltpu.SemaphoreType.DMA((copies,)),
            pltpu.SemaphoreType.DMA((CHUNKS,)),
            pltpu.SemaphoreType.DMA((12,)),
            pltpu.SemaphoreType.DMA((2 * CHUNKS * GROUP,)),
            pltpu.SemaphoreType.DMA((2 * CHUNKS * GROUP,)),
        ],
        compiler_params=pltpu.CompilerParams(
            collective_id=collective_id, has_side_effects=True, vmem_limit_bytes=56 * 2**20
        ),
    )(rows, select, shared_rows, gated, tokens_moe, *weights)


def token_kernel(chunks, block_ref, gain_ref, own_ref, in_ref, page_ref, all_ref, send_sem, recv_sem, local_sem):
    tile = lax.axis_index("tile")
    rows, width = block_ref.shape
    tokens = own_ref.shape[0]
    post = Sender(send_sem, recv_sem)
    greet([{"tile": (tile + sign + NX) % NX} for sign in (1, -1)])

    def at(block, part):
        return all_ref.at[part, pl.ds(pl.multiple_of(block * width, width), width)]

    arrivals = {}
    for hop in (1, 2):
        for sign, i in interleave(
            [(1, i) for i in dir_order(chunks, 1)], [(-1, i) for i in dir_order(chunks, -1)]
        ):
            start, size, far = chunks[i]
            if hop == 2 and far != sign:
                continue
            block, part = (tile - sign * (hop - 1) + NX) % NX, pl.ds(start, size)
            if hop == 1:
                source = block_ref.at[part]
            else:
                arrivals[(sign, i, 1)].wait_recv()
                source = at(block, part)
            arrivals[(sign, i, hop)] = post.send(
                source, at(block, part), {"tile": (tile + sign + NX) % NX}
            )
        if hop == 1:
            own = pltpu.make_async_copy(block_ref, at(tile, pl.ds(0, rows)), local_sem)
            own.start()
    for (sign, i, hop), copy in arrivals.items():
        if hop == 2 or chunks[i][2] != sign:
            copy.wait_recv()
    own.wait()

    def normed(values):
        values = values.astype(jnp.float32)
        mean = jnp.mean(values * values, axis=-1, keepdims=True)
        return (values * lax.rsqrt(mean + norm_eps) * gain_ref[...]).astype(jnp.bfloat16)

    for start in range(0, rows, tokens):
        page_ref[start : start + tokens] = normed(all_ref[start : start + tokens])
    mine = pl.ds(pl.multiple_of(tile * tokens, tokens), tokens)
    own_ref[...] = all_ref[mine]
    in_ref[...] = page_ref[mine]
    for copy in post.made:
        copy.wait_send()


def gather_tokens(block, gain, tokens, collective_id):
    rows, width = block.shape
    chunks = ring_chunks(rows, tokens)
    copies = copies_of("x", chunks)

    def kernel(*refs):
        token_kernel(chunks, *refs)

    return pl.pallas_call(
        kernel,
        out_shape=[
            jax.ShapeDtypeStruct((tokens, NX * width), block.dtype),
            jax.ShapeDtypeStruct((tokens, NX * width), block.dtype),
            jax.ShapeDtypeStruct((rows, NX * width), block.dtype),
        ],
        in_specs=[pl.BlockSpec(memory_space=pltpu.VMEM)] * 2,
        out_specs=[pl.BlockSpec(memory_space=pltpu.VMEM)] * 3,
        scratch_shapes=[
            pltpu.VMEM((rows, NX * width), block.dtype),
            pltpu.SemaphoreType.DMA((copies,)),
            pltpu.SemaphoreType.DMA((copies,)),
            pltpu.SemaphoreType.DMA,
        ],
        compiler_params=pltpu.CompilerParams(collective_id=collective_id, has_side_effects=True),
    )(block, gain.reshape(1, -1))


def slot_tables(table, tokens, top):
    picks = table[:, :top, :tokens].transpose(1, 0, 2).reshape(top, NZ * tokens)
    gates = table[:, 8 : 8 + top, :tokens].transpose(1, 0, 2).reshape(top, NZ * tokens)
    z = (lax.axis_index("expert") // NC) % NZ
    member = jnp.arange(GROUP)
    experts = ((member // NC) * NZ + z) * NC + member % NC
    match = picks[None] == experts.astype(jnp.float32)[:, None, None]
    hit = jnp.any(match, axis=1)
    gate = jnp.sum(jnp.where(match, gates[None], 0.0), axis=1)
    column = jnp.arange(NZ * tokens)
    page = column // tokens
    earlier = (page[:, None] == page[None, :]) & (column[:, None] < column[None, :])
    rank = jnp.dot(
        hit.astype(jnp.bfloat16), earlier.astype(jnp.bfloat16), preferred_element_type=jnp.float32
    )
    slot = jnp.arange(NZ * CAP)
    here = (slot // CAP)[:, None] == page[None, :]
    ranked = rank[:, None, :] == (slot % CAP).astype(jnp.float32)[None, :, None]
    chosen = here[None] & ranked & hit[:, None, :]
    select = chosen.astype(jnp.bfloat16).reshape(GROUP * NZ * CAP, NZ * tokens)
    gated = jnp.where(chosen, gate[:, None, :], 0.0).reshape(GROUP * NZ * CAP, NZ * tokens)
    return select, gated


def per_device(
    patches,
    norm1_gain,
    qkv_weight,
    qkv_bias,
    out_weight,
    out_bias,
    norm2_gain,
    proj_weight,
    moe_gain,
    expert_in,
    expert_out,
    shared_in,
    shared_out,
    routes,
    gates,
):
    tile_id = lax.axis_index("tile")
    row_count = patches.shape[1]
    columns = patches.shape[2]
    width_vit = patches.shape[3]
    local_rows = row_count * columns
    tokens = local_rows // 4
    top = routes.shape[-1]
    side_a = [(t, t + 1 - 2 * (t % 2)) for t in range(NX)]
    side_b = [(t, NX - 1 - t) for t in range(NX)]
    units = expert_out.shape[1] // 2
    in_rows = expert_in[0].transpose(1, 2, 0)
    gate_halves, up_halves, out_halves = (
        [block[:units], block[units:]] for block in (in_rows[0], in_rows[1], expert_out[0])
    )

    def swap(halves, after):
        first, second = halves
        if after is not None:
            first, second, after = lax.optimization_barrier((first, second, after))
        from_a = lax.ppermute(first, "tile", side_a)
        from_b = lax.ppermute(second, "tile", side_b)
        return from_a, from_b, after

    out_a, out_b, _ = swap(out_halves, None)
    project = lax.all_gather(proj_weight, "expert", axis=0, tiled=True)

    inputs = patches.reshape(local_rows, width_vit).astype(jnp.float32)
    normed = layer_norm(inputs, norm1_gain).astype(jnp.bfloat16)
    own_routes = lax.dynamic_index_in_dim(
        routes.reshape(NX, tokens, top), tile_id, 0, keepdims=False
    )
    table = jnp.zeros((16, 128), jnp.float32)
    table = table.at[:top, :tokens].set(own_routes.T.astype(jnp.float32))
    table = table.at[8 : 8 + top, :tokens].set(gates.reshape(tokens, top).T)
    piece, tables_z = ring_gather([("x", normed, 32), ("z", table, 16)], 0)
    gate_a, gate_b, piece = swap(gate_halves, piece)
    piece = piece.reshape(NX * local_rows, width_vit)

    heads_here = qkv_weight.shape[2] // HD
    qkv_flat = qkv_weight.reshape(width_vit, -1)
    bias_rows = qkv_bias.reshape(1, 3, heads_here, HD)
    mixed_flat = jnp.dot(piece, qkv_flat, preferred_element_type=jnp.float32)
    mixed = (
        mixed_flat.reshape(
            piece.shape[0], 3, heads_here, HD
        )
        + bias_rows
    )
    tables = rope_tables(jnp.arange(piece.shape[0]), columns, HD)
    attended = attend(
        rotate(mixed[:, 0], tables).astype(jnp.bfloat16),
        rotate(mixed[:, 1], tables).astype(jnp.bfloat16),
        mixed[:, 2].astype(jnp.bfloat16),
        math.sqrt(HD),
    )
    partial_rows = (
        jnp.dot(attended, out_weight, preferred_element_type=jnp.float32)
        .astype(jnp.bfloat16)
        .reshape(NX, local_rows, width_vit)
    )
    (mixed_heads,) = ring_reduce([("x", partial_rows, 32, jnp.float32)], 1)
    hidden = inputs + mixed_heads + out_bias
    normed_out = layer_norm(hidden, norm2_gain).astype(jnp.bfloat16)
    merged = (
        normed_out.reshape(row_count // 2, 2, columns // 2, 2, width_vit)
        .transpose(0, 2, 1, 3, 4)
        .reshape(tokens, 4 * width_vit)
    )
    (group_merged,) = ring_gather([("x", merged, 16)], 2)
    up_a, up_b, group_merged = swap(up_halves, group_merged)
    select, gated = slot_tables(tables_z, tokens, top)
    projected = jnp.dot(
        group_merged.reshape(NX * tokens, -1), project, preferred_element_type=jnp.float32
    ).astype(jnp.bfloat16)
    tokens_moe, moe_in, page_in = gather_tokens(projected, moe_gain, tokens, 3)
    width_moe = page_in.shape[1]
    shared_gated = jnp.dot(
        page_in, shared_in.reshape(width_moe, -1), preferred_element_type=jnp.float32
    ).reshape(NX * tokens, 2, -1)
    shared_hidden = (jax.nn.silu(shared_gated[:, 0]) * shared_gated[:, 1]).astype(jnp.bfloat16)
    shared_rows = (
        jnp.dot(shared_hidden, shared_out, preferred_element_type=jnp.float32)
        .astype(jnp.bfloat16)
        .reshape(NX, tokens, width_moe)
    )

    output = expert_layer(
        moe_in,
        select,
        shared_rows,
        gated,
        tokens_moe,
        (in_rows, expert_out[0], gate_a, up_a, out_a, gate_b, up_b, out_b),
        4,
    )
    return output.reshape(1, row_count // 2, columns // 2, width_moe)


def solution(mesh):
    placed = (
        P("expert", "tile", None, None),
        P(),
        P(None, None, "tile"),
        P(None, "tile"),
        P("tile", None),
        P(),
        P(),
        P("expert", "tile"),
        P(),
        P("expert", None, None, "tile"),
        P("expert", "tile", None),
        P(None, None, "tile"),
        P("tile", None),
        P("expert", None, None, None),
        P("expert", "tile", None, None),
    )
    return jax.shard_map(
        per_device,
        mesh=mesh,
        in_specs=placed,
        out_specs=P("expert", "tile", None, None),
        check_vma=False,
    )
```

```python
import math

import jax
import jax.numpy as jnp
from jax import lax
from jax.experimental import pallas as pl
from jax.experimental.pallas import tpu as pltpu
from jax.sharding import PartitionSpec as P


HD = 72
NX, NY, NZ, NC = 4, 4, 8, 2
GROUP = NY * NC
CAP = 6
MESH = pl.DeviceIdType.MESH

norm_eps = 1e-06
rope_base = 10000.0


def layer_norm(values, gain_vec):
    centre = values - jnp.mean(values, axis=-1, keepdims=True)
    spread = jnp.mean(centre * centre, axis=-1, keepdims=True)
    return centre * lax.rsqrt(spread + norm_eps) * gain_vec


def rope_tables(positions, columns, head_size):
    quarter = head_size // 4
    inverse = jnp.exp(jnp.arange(quarter).astype(jnp.float32) * (-math.log(rope_base) / quarter))
    row_angle = (positions // columns).astype(jnp.float32)[:, None] * inverse[None, :]
    col_angle = (positions % columns).astype(jnp.float32)[:, None] * inverse[None, :]
    return (jnp.cos(row_angle), jnp.sin(row_angle), jnp.cos(col_angle), jnp.sin(col_angle))


def rotate(values, tables):
    cos_row, sin_row, cos_col, sin_col = tables
    quarter = values.shape[-1] // 4
    row_a = values[..., :quarter]
    row_b = values[..., quarter : 2 * quarter]
    col_a = values[..., 2 * quarter : 3 * quarter]
    col_b = values[..., 3 * quarter :]
    return jnp.concatenate(
        [
            row_a * cos_row[:, None] - row_b * sin_row[:, None],
            row_b * cos_row[:, None] + row_a * sin_row[:, None],
            col_a * cos_col[:, None] - col_b * sin_col[:, None],
            col_b * cos_col[:, None] + col_a * sin_col[:, None],
        ],
        axis=-1,
    )


def attend(query_rows, key_rows, value_rows, divisor):
    scores = (
        jnp.einsum("qhd,khd->hqk", query_rows, key_rows, preferred_element_type=jnp.float32)
        / divisor
    )
    weights = jax.nn.softmax(scores, axis=-1).astype(jnp.bfloat16)
    attended = jnp.einsum(
        "hqk,khd->qhd", weights, value_rows, preferred_element_type=jnp.float32
    ).astype(jnp.bfloat16)
    return attended.reshape(attended.shape[0], -1)


def ring_place(axis):
    if axis == "x":
        return lax.axis_index("tile"), NX, lambda place: {"tile": place}
    here = lax.axis_index("expert")
    y, z, core = here // (NZ * NC), (here // NC) % NZ, here % NC
    return z, NZ, lambda place: {"expert": (y * NZ + place) * NC + core}


def greet(device_ids):
    barrier = pltpu.get_barrier_semaphore()
    for device_id in device_ids:
        pl.semaphore_signal(barrier, inc=1, device_id=device_id, device_id_type=MESH)
    pl.semaphore_wait(barrier, len(device_ids))


def ring_chunks(rows, step):
    starts = list(range(0, rows, step))
    half = (len(starts) + 1) // 2
    return [(s, step, 1 if i < half else -1) for i, s in enumerate(starts)]


def dir_order(chunks, sign):
    ids = range(len(chunks))
    return [i for i in ids if chunks[i][2] == sign] + [i for i in ids if chunks[i][2] != sign]


def interleave(a, b):
    out = []
    for i in range(max(len(a), len(b))):
        out += a[i : i + 1] + b[i : i + 1]
    return out


def ring_gather_kernel(plan, *refs):
    count = len(plan)
    ins, outs = refs[:count], refs[count : 2 * count]
    send_sem, recv_sem, local_sem = refs[2 * count :]
    rings = {axis: ring_place(axis) for axis, _ in plan}
    greet(
        [
            device((here + sign) % size)
            for here, size, device in rings.values()
            for sign in (1, -1)
        ]
    )
    arrivals, sends, number = {}, [], 0
    longest = max(rings[axis][1] // 2 for axis, _ in plan)
    local = []
    for hop in range(1, longest + 1):
        for task, (axis, chunks) in enumerate(plan):
            here, size, device = rings[axis]
            if hop > size // 2:
                continue
            order = interleave(
                [(1, i) for i in dir_order(chunks, 1)], [(-1, i) for i in dir_order(chunks, -1)]
            )
            for sign, i in order:
                start, rows, far = chunks[i]
                if hop == size // 2 and far != sign:
                    continue
                block = (here - sign * (hop - 1) + size) % size
                part = pl.ds(start, rows)
                if hop == 1:
                    source = ins[task].at[part]
                else:
                    arrivals.pop((task, sign, i)).wait_recv()
                    source = outs[task].at[block, part]
                copy = pltpu.make_async_remote_copy(
                    src_ref=source,
                    dst_ref=outs[task].at[block, part],
                    send_sem=send_sem.at[number],
                    recv_sem=recv_sem.at[number],
                    device_id=device((here + sign + size) % size),
                    device_id_type=MESH,
                )
                copy.start()
                arrivals[(task, sign, i)] = copy
                sends.append(copy)
                number += 1
        if hop == 1:
            for task, (axis, _) in enumerate(plan):
                own = pltpu.make_async_copy(
                    ins[task], outs[task].at[rings[axis][0]], local_sem.at[task]
                )
                own.start()
                local.append(own)
    for copy in arrivals.values():
        copy.wait_recv()
    for copy in sends:
        copy.wait_send()
    for own in local:
        own.wait()


def copies_of(axis, chunks):
    half = (NX if axis == "x" else NZ) // 2
    return sum(half + half - 1 for _ in chunks)


def ring_gather(tasks, collective_id):
    plan = [(axis, ring_chunks(block.shape[0], step)) for axis, block, step in tasks]
    copies = sum(copies_of(*entry) for entry in plan)
    sizes = {"x": NX, "z": NZ}

    def kernel(*refs):
        ring_gather_kernel(plan, *refs)

    return pl.pallas_call(
        kernel,
        out_shape=[
            jax.ShapeDtypeStruct((sizes[axis],) + block.shape, block.dtype)
            for axis, block, _ in tasks
        ],
        in_specs=[pl.BlockSpec(memory_space=pltpu.VMEM)] * len(tasks),
        out_specs=[pl.BlockSpec(memory_space=pltpu.VMEM)] * len(tasks),
        scratch_shapes=[
            pltpu.SemaphoreType.DMA((copies,)),
            pltpu.SemaphoreType.DMA((copies,)),
            pltpu.SemaphoreType.DMA((len(tasks),)),
        ],
        compiler_params=pltpu.CompilerParams(collective_id=collective_id, has_side_effects=True),
    )(*[block for _, block, _ in tasks])


def ring_reduce_kernel(plan, *refs):
    count = len(plan)
    ins, outs = refs[:count], refs[count : 2 * count]
    landed, staged = refs[2 * count : 3 * count], refs[3 * count : 4 * count]
    send_sem, recv_sem = refs[4 * count :]
    rings = {axis: ring_place(axis) for axis, _ in plan}
    greet(
        [
            device((here + sign + size) % size)
            for here, size, device in rings.values()
            for sign in (1, -1)
        ]
    )
    last, sends, number = {}, [], 0
    slots = [0] * count
    for step in range(max(rings[axis][1] // 2 for axis, _ in plan)):
        for task, (axis, chunks) in enumerate(plan):
            here, size, device = rings[axis]
            half = size // 2
            order = interleave(
                [(1, i) for i in dir_order(chunks, 1)], [(-1, i) for i in dir_order(chunks, -1)]
            )
            for sign, i in order:
                start, rows, far = chunks[i]
                length = half if far == sign else half - 1
                if step >= length:
                    continue
                part = pl.ds(start, rows)
                target = (here + sign * (length - step) + size) % size
                slot = slots[task]
                slots[task] += 1
                if step == 0:
                    source = ins[task].at[target, part]
                else:
                    copy, before = last[(task, sign, i)]
                    copy.wait_recv()
                    staged[task][slot] = (
                        ins[task][target, part].astype(jnp.float32)
                        + landed[task][before].astype(jnp.float32)
                    ).astype(staged[task].dtype)
                    source = staged[task].at[slot]
                copy = pltpu.make_async_remote_copy(
                    src_ref=source,
                    dst_ref=landed[task].at[slot],
                    send_sem=send_sem.at[number],
                    recv_sem=recv_sem.at[number],
                    device_id=device((here + sign + size) % size),
                    device_id_type=MESH,
                )
                copy.start()
                last[(task, sign, i)] = (copy, slot)
                sends.append(copy)
                number += 1
    for task, (axis, chunks) in enumerate(plan):
        here = rings[axis][0]
        for i, (start, rows, _) in enumerate(chunks):
            part = pl.ds(start, rows)
            total = ins[task][here, part].astype(jnp.float32)
            for sign in (1, -1):
                if (task, sign, i) in last:
                    copy, slot = last[(task, sign, i)]
                    copy.wait_recv()
                    total = total + landed[task][slot].astype(jnp.float32)
            outs[task][part] = total.astype(outs[task].dtype)
    for copy in sends:
        copy.wait_send()


def ring_reduce(tasks, collective_id):
    plan = [(axis, ring_chunks(block.shape[1], step)) for axis, block, step, _ in tasks]
    copies = [copies_of(*entry) for entry in plan]

    def kernel(*refs):
        ring_reduce_kernel(plan, *refs)

    boxes = [
        pltpu.VMEM((number, step, block.shape[2]), block.dtype)
        for number, (_, block, step, _) in zip(copies, tasks)
    ]
    return pl.pallas_call(
        kernel,
        out_shape=[jax.ShapeDtypeStruct(block.shape[1:], kind) for _, block, _, kind in tasks],
        in_specs=[pl.BlockSpec(memory_space=pltpu.VMEM)] * len(tasks),
        out_specs=[pl.BlockSpec(memory_space=pltpu.VMEM)] * len(tasks),
        scratch_shapes=boxes
        + boxes
        + [pltpu.SemaphoreType.DMA((sum(copies),)), pltpu.SemaphoreType.DMA((sum(copies),))],
        compiler_params=pltpu.CompilerParams(collective_id=collective_id, has_side_effects=True),
    )(*[block for _, block, _, _ in tasks])


CHUNKS = 2


def places():
    tile, here = lax.axis_index("tile"), lax.axis_index("expert")
    y, z, core = here // (NZ * NC), (here // NC) % NZ, here % NC
    across = {"tile": tile + 1 - 2 * (tile % 2)}, {"tile": NX - 1 - tile}

    def group(member):
        return {"expert": ((member // NC) * NZ + z) * NC + member % NC}

    def ring(place):
        return {"expert": (y * NZ + place) * NC + core}

    return tile, z, y * NC + core, across, group, ring


class Sender:
    def __init__(self, send_sem, recv_sem):
        self.send_sem, self.recv_sem, self.made = send_sem, recv_sem, []

    def send(self, source, target, device):
        number = len(self.made)
        copy = pltpu.make_async_remote_copy(
            src_ref=source,
            dst_ref=target,
            send_sem=self.send_sem.at[number],
            recv_sem=self.recv_sem.at[number],
            device_id=device,
            device_id_type=MESH,
        )
        copy.start()
        self.made.append(copy)
        return copy


Z_HALF = NZ // 2
Z_STREAMS = [(sign, half, Z_HALF if (half == 0) == (sign == 1) else Z_HALF - 1)
             for sign in (1, -1) for half in (0, 1)]
Z_STREAMS.sort(key=lambda stream: -stream[2])
X_HALF = NX // 2
X_STREAMS = [(sign, half, X_HALF if (half == 0) == (sign == 1) else X_HALF - 1)
             for sign in (1, -1) for half in (0, 1)]
X_STREAMS.sort(key=lambda stream: -stream[2])
Z_COPIES = sum(length for _, _, length in Z_STREAMS)
X_COPIES = sum(length for _, _, length in X_STREAMS)


PER_JOB = GROUP // 2


def expert_kernel(
    rows_ref, select_ref, shared_ref, gated_ref, tokens_ref, in_ref, down_ref,
    gate_a_ref, gate_b_ref,
    out_ref,
    ring_ref, chosen_ref, sum_land_ref, sum_stage_ref, slots_ref, weight_ref, hidden_ref, part_ref,
    high_ref, low_ref, side_ref, stage_ref, back_ref, mix_ref, land_ref, step_ref, base_ref,
    send_sem, recv_sem, local_sem, weight_sem, side_send, side_recv,
):
    tile, z, me, across, group, ring = places()
    tokens, width = rows_ref.shape
    chunk, half_rows = width // CHUNKS, tokens // 2
    slots = NZ * CAP
    units = gate_a_ref.shape[0]
    post = Sender(send_sem, recv_sem)
    peers = [(me + k) % GROUP for k in range(1, GROUP)]
    low_units, high_units = pl.ds(0, units), pl.ds(units, units)
    loads = []
    for where, source in (
        ((0, 0, 0), in_ref.at[0, high_units]),
        ((0, 0, 1), in_ref.at[1, high_units]),
        ((0, 0, 2), down_ref.at[high_units]),
        ((0, 1, 0), gate_b_ref),
        ((1, 0, 0), in_ref.at[0, low_units]),
        ((1, 0, 1), in_ref.at[1, low_units]),
        ((1, 0, 2), down_ref.at[low_units]),
        ((1, 1, 0), gate_a_ref),
    ):
        copy = pltpu.make_async_copy(source, weight_ref.at[where], weight_sem.at[len(loads)])
        copy.start()
        loads.append(copy)
    greet(
        [ring((z + 1) % NZ), ring((z + NZ - 1) % NZ)]
        + [group(peer) for peer in peers]
        + list(across)
    )
    cols = [pl.ds(j * chunk, chunk) for j in range(CHUNKS)]
    part = [pl.ds(h * half_rows, half_rows) for h in (0, 1)]
    arrivals = {}

    def hop(j, number):
        for sign, half, length in Z_STREAMS:
            if number > length:
                continue
            block = (z - sign * (number - 1) + NZ) % NZ
            if number == 1:
                source = rows_ref.at[part[half], cols[j]]
            else:
                arrivals[(j, sign, half)].wait_recv()
                source = ring_ref.at[j, block, part[half]]
            arrivals[(j, sign, half)] = post.send(
                source, ring_ref.at[j, block, part[half]], ring((z + sign + NZ) % NZ)
            )

    for j in range(CHUNKS):
        hop(j, 1)

    sums = {}

    def shared_step(step):
        for sign, half, length in X_STREAMS:
            if step >= length:
                continue
            target = (tile + sign * (length - step) + NX) % NX
            slot = len(sums)
            if step == 0:
                source = shared_ref.at[target, part[half]]
            else:
                copy, before = sums[(sign, half, step - 1)]
                copy.wait_recv()
                sum_stage_ref[slot] = (
                    shared_ref[target, part[half]].astype(jnp.float32)
                    + sum_land_ref[before].astype(jnp.float32)
                ).astype(sum_stage_ref.dtype)
                source = sum_stage_ref.at[slot]
            copy = post.send(source, sum_land_ref.at[slot], {"tile": (tile + sign + NX) % NX})
            sums[(sign, half, step)] = (copy, slot)

    shared_step(0)
    swapped = [
        post.send(source.at[half_units], weight_ref.at[1 - side, 1, kind], across[side])
        for kind, source in ((1, in_ref.at[1]), (2, down_ref))
        for side, half_units in ((0, low_units), (1, high_units))
    ]
    for j in range(CHUNKS):
        ring_ref[j, z] = rows_ref[:, j * chunk : (j + 1) * chunk]
    gated = gated_ref[...].T
    high = gated.astype(high_ref.dtype)
    high_ref[...] = high
    low_ref[...] = (gated - high.astype(jnp.float32)).astype(low_ref.dtype)

    swaps, own, handed = {}, [], []

    def hand_on(j, k, source):
        for side in (0, 1):
            handed.append(post.send(source, slots_ref.at[2 * side, k, :, cols[j]], across[side]))

    def choose(j):
        for sign, half, _ in Z_STREAMS:
            arrivals[(j, sign, half)].wait_recv()
        gathered = ring_ref[j].reshape(NZ * tokens, chunk)
        chosen_ref[j] = (
            jnp.dot(select_ref[...], gathered, preferred_element_type=jnp.float32)
            .astype(chosen_ref.dtype)
            .reshape(chosen_ref.shape[1:])
        )
        for k, peer in enumerate(peers, 1):
            swaps[(j, k)] = post.send(
                chosen_ref.at[j, peer], slots_ref.at[1, k, :, cols[j]], group(peer)
            )
        copy = pltpu.make_async_copy(
            chosen_ref.at[j, me], slots_ref.at[1, 0, :, cols[j]], local_sem.at[j]
        )
        copy.start()
        own.append(copy)
        hand_on(j, 0, chosen_ref.at[j, me])

    def forward(j):
        for k in range(1, GROUP):
            swaps[(j, k)].wait_recv()
            hand_on(j, k, slots_ref.at[1, k, :, cols[j]])

    for wave in range(CHUNKS + Z_HALF - 1):
        for number in range(Z_HALF, 1, -1):
            j = wave - (number - 2)
            if 0 <= j < CHUNKS:
                hop(j, number)
        if wave == 0:
            shared_step(1)
        j = wave - (Z_HALF - 1)
        if 0 <= j < CHUNKS:
            choose(j)
    for j in range(CHUNKS):
        forward(j)

    def feed_forward(which, mine, job):
        first = job * PER_JOB
        place = 2 * which * (1 - mine) + mine
        rows = slots_ref[place, pl.ds(first, PER_JOB)].reshape(PER_JOB * slots, width)
        contract = (((1,), (1,)), ((), ()))
        for piece in (0, 1):
            gate = lax.dot_general(
                rows, weight_ref[which, piece, 0], contract, preferred_element_type=jnp.float32
            )
            up = lax.dot_general(
                rows, weight_ref[which, piece, 1], contract, preferred_element_type=jnp.float32
            )
            hidden_ref[piece] = (gate / (1.0 + jnp.exp(-gate)) * up).astype(hidden_ref.dtype)
        for j in range(CHUNKS):
            total = jnp.dot(
                hidden_ref[0], weight_ref[which, 0, 2, :, cols[j]],
                preferred_element_type=jnp.float32,
            ) + jnp.dot(
                hidden_ref[1], weight_ref[which, 1, 2, :, cols[j]],
                preferred_element_type=jnp.float32,
            )
            part_ref[which, mine, pl.ds(first, PER_JOB), :, cols[j]] = total.astype(
                part_ref.dtype
            ).reshape(PER_JOB, slots, chunk)

    def side_copy(which, j, k):
        number = (which * CHUNKS + j) * GROUP + k
        neighbour = tile + 1 - 2 * (tile % 2)
        other = NX - 1 - tile
        return pltpu.make_async_remote_copy(
            src_ref=part_ref.at[which, 0, k, :, cols[j]],
            dst_ref=side_ref.at[which, j, k],
            send_sem=side_send.at[number],
            recv_sem=side_recv.at[number],
            device_id={"tile": neighbour + which * (other - neighbour)},
            device_id_type=MESH,
        )

    for copy in loads + own:
        copy.wait()
    for copy in swapped:
        copy.wait_recv()

    def own_job(i, carry):
        feed_forward(i % 2, 1, i // 2)
        return carry

    lax.fori_loop(0, 4, own_job, 0)
    for copy in handed:
        copy.wait_recv()

    def side_job(i, carry):
        which, job = i % 2, i // 2
        feed_forward(which, 0, job)
        for j in range(CHUNKS):
            for k in range(PER_JOB):
                side_copy(which, j, job * PER_JOB + k).start()
        return carry

    lax.fori_loop(0, 4, side_job, 0)

    for half in (0, 1):
        total = shared_ref[tile, part[half]].astype(jnp.float32)
        for sign, this, length in X_STREAMS:
            if this == half:
                copy, slot = sums[(sign, half, length - 1)]
                copy.wait_recv()
                total = total + sum_land_ref[slot].astype(jnp.float32)
        base_ref[part[half]] = total + tokens_ref[part[half]].astype(jnp.float32)
    returns, steps = {}, {}

    def add_up(j, ks):
        for k in ks:
            for which in (0, 1):
                side_copy(which, j, k).wait_recv()
            total = (
                part_ref[0, 1, k, :, cols[j]].astype(jnp.float32)
                + part_ref[1, 1, k, :, cols[j]].astype(jnp.float32)
                + side_ref[0, j, k].astype(jnp.float32)
                + side_ref[1, j, k].astype(jnp.float32)
            ).astype(stage_ref.dtype)
            if k == 0:
                back_ref[j, me] = total
            else:
                stage_ref[j, k] = total
                returns[(j, k)] = post.send(
                    stage_ref.at[j, k], back_ref.at[j, me], group((me - k + GROUP) % GROUP)
                )

    def step(j, number):
        for i, (sign, half, length) in enumerate(Z_STREAMS):
            if number >= length:
                continue
            target = (z + sign * (length - number) + NZ) % NZ
            slot = i * Z_HALF + number
            if number == 0:
                source = mix_ref.at[j, target, part[half]]
            else:
                steps[(j, i, number - 1)].wait_recv()
                step_ref[j, slot] = (
                    mix_ref[j, target, part[half]].astype(jnp.float32)
                    + land_ref[j, slot - 1].astype(jnp.float32)
                ).astype(step_ref.dtype)
                source = step_ref.at[j, slot]
            steps[(j, i, number)] = post.send(
                source, land_ref.at[j, slot], ring((z + sign + NZ) % NZ)
            )

    def combine(j):
        for k in range(1, GROUP):
            returns[(j, k)].wait_recv()
        back = back_ref[j].reshape(high_ref.shape[1], chunk)
        mix_ref[j] = (
            (
                jnp.dot(high_ref[...], back, preferred_element_type=jnp.float32)
                + jnp.dot(low_ref[...], back, preferred_element_type=jnp.float32)
            )
            .astype(mix_ref.dtype)
            .reshape(mix_ref.shape[1:])
        )
        step(j, 0)

    for j in range(CHUNKS):
        add_up(j, range(PER_JOB))
    for wave in range(CHUNKS + Z_HALF + 1):
        if wave < CHUNKS:
            add_up(wave, range(PER_JOB, GROUP))
        if 0 <= wave - 1 < CHUNKS:
            combine(wave - 1)
        for number in range(1, Z_HALF):
            if 0 <= wave - 1 - number < CHUNKS:
                step(wave - 1 - number, number)
    for j in range(CHUNKS):
        for half in (0, 1):
            total = base_ref[part[half], cols[j]] + mix_ref[j, z, part[half]].astype(
                jnp.float32
            )
            for i, (_, this, length) in enumerate(Z_STREAMS):
                if this == half:
                    steps[(j, i, length - 1)].wait_recv()
                    total = total + land_ref[j, i * Z_HALF + length - 1].astype(jnp.float32)
            out_ref[part[half], cols[j]] = total.astype(out_ref.dtype)
    for copy in post.made:
        copy.wait_send()
    for which in (0, 1):
        for j in range(CHUNKS):
            for k in range(GROUP):
                side_copy(which, j, k).wait_send()


def expert_layer(rows, select, shared_rows, gated, tokens_moe, weights, collective_id):
    tokens, width = rows.shape
    slots = NZ * CAP
    chunk = width // CHUNKS
    kind = rows.dtype
    units = weights[-1].shape[0]
    copies = CHUNKS * (2 * Z_COPIES + 2 * (GROUP - 1) + 2 * GROUP) + X_COPIES + 4
    boxes = pltpu.VMEM((CHUNKS, len(Z_STREAMS) * Z_HALF, tokens // 2, chunk), kind)
    blocks = pltpu.VMEM((CHUNKS, GROUP, slots, chunk), kind)
    shared_boxes = pltpu.VMEM((X_COPIES, tokens // 2, width), kind)
    spread = pltpu.VMEM((CHUNKS, NZ, tokens, chunk), kind)
    return pl.pallas_call(
        expert_kernel,
        out_shape=jax.ShapeDtypeStruct((tokens, width), kind),
        in_specs=[pl.BlockSpec(memory_space=pltpu.VMEM)] * 5
        + [pl.BlockSpec(memory_space=pl.ANY)] * len(weights),
        out_specs=pl.BlockSpec(memory_space=pltpu.VMEM),
        scratch_shapes=[
            spread,
            blocks,
            shared_boxes,
            shared_boxes,
            pltpu.VMEM((3, GROUP, slots, width), kind),
            pltpu.VMEM((2, 2, 3, units, width), kind),
            pltpu.VMEM((2, PER_JOB * slots, units), kind),
            pltpu.VMEM((2, 2, GROUP, slots, width), kind),
            pltpu.VMEM(gated.shape[::-1], kind),
            pltpu.VMEM(gated.shape[::-1], kind),
            pltpu.VMEM((2, CHUNKS, GROUP, slots, chunk), kind),
            blocks,
            blocks,
            spread,
            boxes,
            boxes,
            pltpu.VMEM((tokens, width), jnp.float32),
            pltpu.SemaphoreType.DMA((copies,)),
            pltpu.SemaphoreType.DMA((copies,)),
            pltpu.SemaphoreType.DMA((CHUNKS,)),
            pltpu.SemaphoreType.DMA((8,)),
            pltpu.SemaphoreType.DMA((2 * CHUNKS * GROUP,)),
            pltpu.SemaphoreType.DMA((2 * CHUNKS * GROUP,)),
        ],
        compiler_params=pltpu.CompilerParams(
            collective_id=collective_id, has_side_effects=True, vmem_limit_bytes=56 * 2**20
        ),
    )(rows, select, shared_rows, gated, tokens_moe, *weights)


def token_kernel(chunks, block_ref, gain_ref, own_ref, in_ref, page_ref, all_ref, send_sem, recv_sem, local_sem):
    tile = lax.axis_index("tile")
    rows, width = block_ref.shape
    tokens = own_ref.shape[0]
    post = Sender(send_sem, recv_sem)
    greet([{"tile": (tile + sign + NX) % NX} for sign in (1, -1)])

    def at(block, part):
        return all_ref.at[part, pl.ds(pl.multiple_of(block * width, width), width)]

    arrivals = {}
    for hop in (1, 2):
        for sign, i in interleave(
            [(1, i) for i in dir_order(chunks, 1)], [(-1, i) for i in dir_order(chunks, -1)]
        ):
            start, size, far = chunks[i]
            if hop == 2 and far != sign:
                continue
            block, part = (tile - sign * (hop - 1) + NX) % NX, pl.ds(start, size)
            if hop == 1:
                source = block_ref.at[part]
            else:
                arrivals[(sign, i, 1)].wait_recv()
                source = at(block, part)
            arrivals[(sign, i, hop)] = post.send(
                source, at(block, part), {"tile": (tile + sign + NX) % NX}
            )
        if hop == 1:
            own = pltpu.make_async_copy(block_ref, at(tile, pl.ds(0, rows)), local_sem)
            own.start()
    for (sign, i, hop), copy in arrivals.items():
        if hop == 2 or chunks[i][2] != sign:
            copy.wait_recv()
    own.wait()

    def normed(values):
        values = values.astype(jnp.float32)
        mean = jnp.mean(values * values, axis=-1, keepdims=True)
        return (values * lax.rsqrt(mean + norm_eps) * gain_ref[...]).astype(jnp.bfloat16)

    for start in range(0, rows, tokens):
        page_ref[start : start + tokens] = normed(all_ref[start : start + tokens])
    mine = pl.ds(pl.multiple_of(tile * tokens, tokens), tokens)
    own_ref[...] = all_ref[mine]
    in_ref[...] = page_ref[mine]
    for copy in post.made:
        copy.wait_send()


def gather_tokens(block, gain, tokens, collective_id):
    rows, width = block.shape
    chunks = ring_chunks(rows, tokens)
    copies = copies_of("x", chunks)

    def kernel(*refs):
        token_kernel(chunks, *refs)

    return pl.pallas_call(
        kernel,
        out_shape=[
            jax.ShapeDtypeStruct((tokens, NX * width), block.dtype),
            jax.ShapeDtypeStruct((tokens, NX * width), block.dtype),
            jax.ShapeDtypeStruct((rows, NX * width), block.dtype),
        ],
        in_specs=[pl.BlockSpec(memory_space=pltpu.VMEM)] * 2,
        out_specs=[pl.BlockSpec(memory_space=pltpu.VMEM)] * 3,
        scratch_shapes=[
            pltpu.VMEM((rows, NX * width), block.dtype),
            pltpu.SemaphoreType.DMA((copies,)),
            pltpu.SemaphoreType.DMA((copies,)),
            pltpu.SemaphoreType.DMA,
        ],
        compiler_params=pltpu.CompilerParams(collective_id=collective_id, has_side_effects=True),
    )(block, gain.reshape(1, -1))


def slot_tables(table, tokens, top):
    picks = table[:, :top, :tokens].transpose(1, 0, 2).reshape(top, NZ * tokens)
    gates = table[:, 8 : 8 + top, :tokens].transpose(1, 0, 2).reshape(top, NZ * tokens)
    z = (lax.axis_index("expert") // NC) % NZ
    member = jnp.arange(GROUP)
    experts = ((member // NC) * NZ + z) * NC + member % NC
    match = picks[None] == experts.astype(jnp.float32)[:, None, None]
    hit = jnp.any(match, axis=1)
    gate = jnp.sum(jnp.where(match, gates[None], 0.0), axis=1)
    column = jnp.arange(NZ * tokens)
    page = column // tokens
    earlier = (page[:, None] == page[None, :]) & (column[:, None] < column[None, :])
    rank = jnp.dot(
        hit.astype(jnp.bfloat16), earlier.astype(jnp.bfloat16), preferred_element_type=jnp.float32
    )
    slot = jnp.arange(NZ * CAP)
    here = (slot // CAP)[:, None] == page[None, :]
    ranked = rank[:, None, :] == (slot % CAP).astype(jnp.float32)[None, :, None]
    chosen = here[None] & ranked & hit[:, None, :]
    select = chosen.astype(jnp.bfloat16).reshape(GROUP * NZ * CAP, NZ * tokens)
    gated = jnp.where(chosen, gate[:, None, :], 0.0).reshape(GROUP * NZ * CAP, NZ * tokens)
    return select, gated


def per_device(
    patches,
    norm1_gain,
    qkv_weight,
    qkv_bias,
    out_weight,
    out_bias,
    norm2_gain,
    proj_weight,
    moe_gain,
    expert_in,
    expert_out,
    shared_in,
    shared_out,
    routes,
    gates,
):
    tile_id = lax.axis_index("tile")
    row_count = patches.shape[1]
    columns = patches.shape[2]
    width_vit = patches.shape[3]
    local_rows = row_count * columns
    tokens = local_rows // 4
    top = routes.shape[-1]
    side_a = [(t, t + 1 - 2 * (t % 2)) for t in range(NX)]
    side_b = [(t, NX - 1 - t) for t in range(NX)]
    units = expert_out.shape[1] // 2
    in_rows = expert_in[0].transpose(1, 2, 0)
    gate_halves = in_rows[0, :units], in_rows[0, units:]

    def swap(halves, after):
        first, second, after = lax.optimization_barrier((*halves, after))
        from_a = lax.ppermute(first, "tile", side_a)
        from_b = lax.ppermute(second, "tile", side_b)
        return from_a, from_b, after

    project = lax.all_gather(proj_weight, "expert", axis=0, tiled=True)

    inputs = patches.reshape(local_rows, width_vit).astype(jnp.float32)
    normed = layer_norm(inputs, norm1_gain).astype(jnp.bfloat16)
    own_routes = lax.dynamic_index_in_dim(
        routes.reshape(NX, tokens, top), tile_id, 0, keepdims=False
    )
    table = jnp.zeros((16, 128), jnp.float32)
    table = table.at[:top, :tokens].set(own_routes.T.astype(jnp.float32))
    table = table.at[8 : 8 + top, :tokens].set(gates.reshape(tokens, top).T)
    piece, tables_z = ring_gather([("x", normed, 32), ("z", table, 16)], 0)
    gate_a, gate_b, piece = swap(gate_halves, piece)
    piece = piece.reshape(NX * local_rows, width_vit)

    heads_here = qkv_weight.shape[2] // HD
    qkv_flat = qkv_weight.reshape(width_vit, -1)
    bias_rows = qkv_bias.reshape(1, 3, heads_here, HD)
    mixed_flat = jnp.dot(piece, qkv_flat, preferred_element_type=jnp.float32)
    mixed = (
        mixed_flat.reshape(
            piece.shape[0], 3, heads_here, HD
        )
        + bias_rows
    )
    tables = rope_tables(jnp.arange(piece.shape[0]), columns, HD)
    attended = attend(
        rotate(mixed[:, 0], tables).astype(jnp.bfloat16),
        rotate(mixed[:, 1], tables).astype(jnp.bfloat16),
        mixed[:, 2].astype(jnp.bfloat16),
        math.sqrt(HD),
    )
    partial_rows = (
        jnp.dot(attended, out_weight, preferred_element_type=jnp.float32)
        .astype(jnp.bfloat16)
        .reshape(NX, local_rows, width_vit)
    )
    (mixed_heads,) = ring_reduce([("x", partial_rows, 32, jnp.float32)], 1)
    hidden = inputs + mixed_heads + out_bias
    normed_out = layer_norm(hidden, norm2_gain).astype(jnp.bfloat16)
    merged = (
        normed_out.reshape(row_count // 2, 2, columns // 2, 2, width_vit)
        .transpose(0, 2, 1, 3, 4)
        .reshape(tokens, 4 * width_vit)
    )
    (group_merged,) = ring_gather([("x", merged, 16)], 2)
    select, gated = slot_tables(tables_z, tokens, top)
    projected = jnp.dot(
        group_merged.reshape(NX * tokens, -1), project, preferred_element_type=jnp.float32
    ).astype(jnp.bfloat16)
    tokens_moe, moe_in, page_in = gather_tokens(projected, moe_gain, tokens, 3)
    width_moe = page_in.shape[1]
    shared_gated = jnp.dot(
        page_in, shared_in.reshape(width_moe, -1), preferred_element_type=jnp.float32
    ).reshape(NX * tokens, 2, -1)
    shared_hidden = (jax.nn.silu(shared_gated[:, 0]) * shared_gated[:, 1]).astype(jnp.bfloat16)
    shared_rows = (
        jnp.dot(shared_hidden, shared_out, preferred_element_type=jnp.float32)
        .astype(jnp.bfloat16)
        .reshape(NX, tokens, width_moe)
    )

    output = expert_layer(
        moe_in,
        select,
        shared_rows,
        gated,
        tokens_moe,
        (in_rows, expert_out[0], gate_a, gate_b),
        4,
    )
    return output.reshape(1, row_count // 2, columns // 2, width_moe)


def solution(mesh):
    placed = (
        P("expert", "tile", None, None),
        P(),
        P(None, None, "tile"),
        P(None, "tile"),
        P("tile", None),
        P(),
        P(),
        P("expert", "tile"),
        P(),
        P("expert", None, None, "tile"),
        P("expert", "tile", None),
        P(None, None, "tile"),
        P("tile", None),
        P("expert", None, None, None),
        P("expert", "tile", None, None),
    )
    return jax.shard_map(
        per_device,
        mesh=mesh,
        in_specs=placed,
        out_specs=P("expert", "tile", None, None),
        check_vma=False,
    )
```

```python
import math

import jax
import jax.numpy as jnp
from jax import lax
from jax.experimental import pallas as pl
from jax.experimental.pallas import tpu as pltpu
from jax.sharding import PartitionSpec as P


HD = 72
NX, NY, NZ, NC = 4, 4, 8, 2
GROUP = NY * NC
CAP = 6
MESH = pl.DeviceIdType.MESH

norm_eps = 1e-06
rope_base = 10000.0


def layer_norm(values, gain_vec):
    centre = values - jnp.mean(values, axis=-1, keepdims=True)
    spread = jnp.mean(centre * centre, axis=-1, keepdims=True)
    return centre * lax.rsqrt(spread + norm_eps) * gain_vec


def rope_tables(positions, columns, head_size):
    quarter = head_size // 4
    inverse = jnp.exp(jnp.arange(quarter).astype(jnp.float32) * (-math.log(rope_base) / quarter))
    row_angle = (positions // columns).astype(jnp.float32)[:, None] * inverse[None, :]
    col_angle = (positions % columns).astype(jnp.float32)[:, None] * inverse[None, :]
    return (jnp.cos(row_angle), jnp.sin(row_angle), jnp.cos(col_angle), jnp.sin(col_angle))


def rotate(values, tables):
    cos_row, sin_row, cos_col, sin_col = tables
    quarter = values.shape[-1] // 4
    row_a = values[..., :quarter]
    row_b = values[..., quarter : 2 * quarter]
    col_a = values[..., 2 * quarter : 3 * quarter]
    col_b = values[..., 3 * quarter :]
    return jnp.concatenate(
        [
            row_a * cos_row[:, None] - row_b * sin_row[:, None],
            row_b * cos_row[:, None] + row_a * sin_row[:, None],
            col_a * cos_col[:, None] - col_b * sin_col[:, None],
            col_b * cos_col[:, None] + col_a * sin_col[:, None],
        ],
        axis=-1,
    )


def attend(query_rows, key_rows, value_rows, divisor):
    scores = (
        jnp.einsum("qhd,khd->hqk", query_rows, key_rows, preferred_element_type=jnp.float32)
        / divisor
    )
    weights = jax.nn.softmax(scores, axis=-1).astype(jnp.bfloat16)
    attended = jnp.einsum(
        "hqk,khd->qhd", weights, value_rows, preferred_element_type=jnp.float32
    ).astype(jnp.bfloat16)
    return attended.reshape(attended.shape[0], -1)


def ring_place(axis):
    if axis == "x":
        return lax.axis_index("tile"), NX, lambda place: {"tile": place}
    here = lax.axis_index("expert")
    y, z, core = here // (NZ * NC), (here // NC) % NZ, here % NC
    return z, NZ, lambda place: {"expert": (y * NZ + place) * NC + core}


def greet(device_ids):
    barrier = pltpu.get_barrier_semaphore()
    for device_id in device_ids:
        pl.semaphore_signal(barrier, inc=1, device_id=device_id, device_id_type=MESH)
    pl.semaphore_wait(barrier, len(device_ids))


def ring_chunks(rows, step):
    starts = list(range(0, rows, step))
    half = (len(starts) + 1) // 2
    return [(s, step, 1 if i < half else -1) for i, s in enumerate(starts)]


def dir_order(chunks, sign):
    ids = range(len(chunks))
    return [i for i in ids if chunks[i][2] == sign] + [i for i in ids if chunks[i][2] != sign]


def interleave(a, b):
    out = []
    for i in range(max(len(a), len(b))):
        out += a[i : i + 1] + b[i : i + 1]
    return out


def ring_gather_kernel(plan, *refs):
    count = len(plan)
    ins, outs = refs[:count], refs[count : 2 * count]
    send_sem, recv_sem, local_sem = refs[2 * count :]
    rings = {axis: ring_place(axis) for axis, _ in plan}
    greet(
        [
            device((here + sign) % size)
            for here, size, device in rings.values()
            for sign in (1, -1)
        ]
    )
    arrivals, sends, number = {}, [], 0
    longest = max(rings[axis][1] // 2 for axis, _ in plan)
    local = []
    for hop in range(1, longest + 1):
        for task, (axis, chunks) in enumerate(plan):
            here, size, device = rings[axis]
            if hop > size // 2:
                continue
            order = interleave(
                [(1, i) for i in dir_order(chunks, 1)], [(-1, i) for i in dir_order(chunks, -1)]
            )
            for sign, i in order:
                start, rows, far = chunks[i]
                if hop == size // 2 and far != sign:
                    continue
                block = (here - sign * (hop - 1) + size) % size
                part = pl.ds(start, rows)
                if hop == 1:
                    source = ins[task].at[part]
                else:
                    arrivals.pop((task, sign, i)).wait_recv()
                    source = outs[task].at[block, part]
                copy = pltpu.make_async_remote_copy(
                    src_ref=source,
                    dst_ref=outs[task].at[block, part],
                    send_sem=send_sem.at[number],
                    recv_sem=recv_sem.at[number],
                    device_id=device((here + sign + size) % size),
                    device_id_type=MESH,
                )
                copy.start()
                arrivals[(task, sign, i)] = copy
                sends.append(copy)
                number += 1
        if hop == 1:
            for task, (axis, _) in enumerate(plan):
                own = pltpu.make_async_copy(
                    ins[task], outs[task].at[rings[axis][0]], local_sem.at[task]
                )
                own.start()
                local.append(own)
    for copy in arrivals.values():
        copy.wait_recv()
    for copy in sends:
        copy.wait_send()
    for own in local:
        own.wait()


def copies_of(axis, chunks):
    half = (NX if axis == "x" else NZ) // 2
    return sum(half + half - 1 for _ in chunks)


def ring_gather(tasks, collective_id):
    plan = [(axis, ring_chunks(block.shape[0], step)) for axis, block, step in tasks]
    copies = sum(copies_of(*entry) for entry in plan)
    sizes = {"x": NX, "z": NZ}

    def kernel(*refs):
        ring_gather_kernel(plan, *refs)

    return pl.pallas_call(
        kernel,
        out_shape=[
            jax.ShapeDtypeStruct((sizes[axis],) + block.shape, block.dtype)
            for axis, block, _ in tasks
        ],
        in_specs=[pl.BlockSpec(memory_space=pltpu.VMEM)] * len(tasks),
        out_specs=[pl.BlockSpec(memory_space=pltpu.VMEM)] * len(tasks),
        scratch_shapes=[
            pltpu.SemaphoreType.DMA((copies,)),
            pltpu.SemaphoreType.DMA((copies,)),
            pltpu.SemaphoreType.DMA((len(tasks),)),
        ],
        compiler_params=pltpu.CompilerParams(collective_id=collective_id, has_side_effects=True),
    )(*[block for _, block, _ in tasks])


def ring_reduce_kernel(plan, *refs):
    count = len(plan)
    ins, outs = refs[:count], refs[count : 2 * count]
    landed, staged = refs[2 * count : 3 * count], refs[3 * count : 4 * count]
    send_sem, recv_sem = refs[4 * count :]
    rings = {axis: ring_place(axis) for axis, _ in plan}
    greet(
        [
            device((here + sign + size) % size)
            for here, size, device in rings.values()
            for sign in (1, -1)
        ]
    )
    last, sends, number = {}, [], 0
    slots = [0] * count
    for step in range(max(rings[axis][1] // 2 for axis, _ in plan)):
        for task, (axis, chunks) in enumerate(plan):
            here, size, device = rings[axis]
            half = size // 2
            order = interleave(
                [(1, i) for i in dir_order(chunks, 1)], [(-1, i) for i in dir_order(chunks, -1)]
            )
            for sign, i in order:
                start, rows, far = chunks[i]
                length = half if far == sign else half - 1
                if step >= length:
                    continue
                part = pl.ds(start, rows)
                target = (here + sign * (length - step) + size) % size
                slot = slots[task]
                slots[task] += 1
                if step == 0:
                    source = ins[task].at[target, part]
                else:
                    copy, before = last[(task, sign, i)]
                    copy.wait_recv()
                    staged[task][slot] = (
                        ins[task][target, part].astype(jnp.float32)
                        + landed[task][before].astype(jnp.float32)
                    ).astype(staged[task].dtype)
                    source = staged[task].at[slot]
                copy = pltpu.make_async_remote_copy(
                    src_ref=source,
                    dst_ref=landed[task].at[slot],
                    send_sem=send_sem.at[number],
                    recv_sem=recv_sem.at[number],
                    device_id=device((here + sign + size) % size),
                    device_id_type=MESH,
                )
                copy.start()
                last[(task, sign, i)] = (copy, slot)
                sends.append(copy)
                number += 1
    for task, (axis, chunks) in enumerate(plan):
        here = rings[axis][0]
        for i, (start, rows, _) in enumerate(chunks):
            part = pl.ds(start, rows)
            total = ins[task][here, part].astype(jnp.float32)
            for sign in (1, -1):
                if (task, sign, i) in last:
                    copy, slot = last[(task, sign, i)]
                    copy.wait_recv()
                    total = total + landed[task][slot].astype(jnp.float32)
            outs[task][part] = total.astype(outs[task].dtype)
    for copy in sends:
        copy.wait_send()


def ring_reduce(tasks, collective_id):
    plan = [(axis, ring_chunks(block.shape[1], step)) for axis, block, step, _ in tasks]
    copies = [copies_of(*entry) for entry in plan]

    def kernel(*refs):
        ring_reduce_kernel(plan, *refs)

    boxes = [
        pltpu.VMEM((number, step, block.shape[2]), block.dtype)
        for number, (_, block, step, _) in zip(copies, tasks)
    ]
    return pl.pallas_call(
        kernel,
        out_shape=[jax.ShapeDtypeStruct(block.shape[1:], kind) for _, block, _, kind in tasks],
        in_specs=[pl.BlockSpec(memory_space=pltpu.VMEM)] * len(tasks),
        out_specs=[pl.BlockSpec(memory_space=pltpu.VMEM)] * len(tasks),
        scratch_shapes=boxes
        + boxes
        + [pltpu.SemaphoreType.DMA((sum(copies),)), pltpu.SemaphoreType.DMA((sum(copies),))],
        compiler_params=pltpu.CompilerParams(collective_id=collective_id, has_side_effects=True),
    )(*[block for _, block, _, _ in tasks])


CHUNKS = 2


def places():
    tile, here = lax.axis_index("tile"), lax.axis_index("expert")
    y, z, core = here // (NZ * NC), (here // NC) % NZ, here % NC
    across = {"tile": tile + 1 - 2 * (tile % 2)}, {"tile": NX - 1 - tile}

    def group(member):
        return {"expert": ((member // NC) * NZ + z) * NC + member % NC}

    def ring(place):
        return {"expert": (y * NZ + place) * NC + core}

    return tile, z, y * NC + core, across, group, ring


class Sender:
    def __init__(self, send_sem, recv_sem):
        self.send_sem, self.recv_sem, self.made = send_sem, recv_sem, []

    def send(self, source, target, device):
        number = len(self.made)
        copy = pltpu.make_async_remote_copy(
            src_ref=source,
            dst_ref=target,
            send_sem=self.send_sem.at[number],
            recv_sem=self.recv_sem.at[number],
            device_id=device,
            device_id_type=MESH,
        )
        copy.start()
        self.made.append(copy)
        return copy


Z_HALF = NZ // 2
Z_STREAMS = [(sign, half, Z_HALF if (half == 0) == (sign == 1) else Z_HALF - 1)
             for sign in (1, -1) for half in (0, 1)]
Z_STREAMS.sort(key=lambda stream: -stream[2])
X_HALF = NX // 2
X_STREAMS = [(sign, half, X_HALF if (half == 0) == (sign == 1) else X_HALF - 1)
             for sign in (1, -1) for half in (0, 1)]
X_STREAMS.sort(key=lambda stream: -stream[2])
Z_COPIES = sum(length for _, _, length in Z_STREAMS)
X_COPIES = sum(length for _, _, length in X_STREAMS)


PER_JOB = GROUP // 2


def expert_kernel(
    rows_ref, select_ref, shared_ref, gated_ref, tokens_ref, in_ref, down_ref,
    gate_a_ref, up_a_ref, gate_b_ref, up_b_ref,
    out_ref,
    ring_ref, chosen_ref, sum_land_ref, sum_stage_ref, slots_ref, weight_ref, hidden_ref, part_ref,
    high_ref, low_ref, side_ref, stage_ref, back_ref, mix_ref, land_ref, step_ref, base_ref,
    send_sem, recv_sem, local_sem, weight_sem, side_send, side_recv,
):
    tile, z, me, across, group, ring = places()
    tokens, width = rows_ref.shape
    chunk, half_rows = width // CHUNKS, tokens // 2
    slots = NZ * CAP
    units = gate_a_ref.shape[0]
    post = Sender(send_sem, recv_sem)
    peers = [(me + k) % GROUP for k in range(1, GROUP)]
    low_units, high_units = pl.ds(0, units), pl.ds(units, units)
    loads = []
    for where, source in (
        ((0, 0, 0), in_ref.at[0, high_units]),
        ((0, 0, 1), in_ref.at[1, high_units]),
        ((0, 0, 2), down_ref.at[high_units]),
        ((0, 1, 0), gate_b_ref),
        ((0, 1, 1), up_b_ref),
        ((1, 0, 0), in_ref.at[0, low_units]),
        ((1, 0, 1), in_ref.at[1, low_units]),
        ((1, 0, 2), down_ref.at[low_units]),
        ((1, 1, 0), gate_a_ref),
        ((1, 1, 1), up_a_ref),
    ):
        copy = pltpu.make_async_copy(source, weight_ref.at[where], weight_sem.at[len(loads)])
        copy.start()
        loads.append(copy)
    greet(
        [ring((z + 1) % NZ), ring((z + NZ - 1) % NZ)]
        + [group(peer) for peer in peers]
        + list(across)
    )
    cols = [pl.ds(j * chunk, chunk) for j in range(CHUNKS)]
    part = [pl.ds(h * half_rows, half_rows) for h in (0, 1)]
    arrivals = {}

    def hop(j, number):
        for sign, half, length in Z_STREAMS:
            if number > length:
                continue
            block = (z - sign * (number - 1) + NZ) % NZ
            if number == 1:
                source = rows_ref.at[part[half], cols[j]]
            else:
                arrivals[(j, sign, half)].wait_recv()
                source = ring_ref.at[j, block, part[half]]
            arrivals[(j, sign, half)] = post.send(
                source, ring_ref.at[j, block, part[half]], ring((z + sign + NZ) % NZ)
            )

    for j in range(CHUNKS):
        hop(j, 1)

    sums = {}

    def shared_step(step):
        for sign, half, length in X_STREAMS:
            if step >= length:
                continue
            target = (tile + sign * (length - step) + NX) % NX
            slot = len(sums)
            if step == 0:
                source = shared_ref.at[target, part[half]]
            else:
                copy, before = sums[(sign, half, step - 1)]
                copy.wait_recv()
                sum_stage_ref[slot] = (
                    shared_ref[target, part[half]].astype(jnp.float32)
                    + sum_land_ref[before].astype(jnp.float32)
                ).astype(sum_stage_ref.dtype)
                source = sum_stage_ref.at[slot]
            copy = post.send(source, sum_land_ref.at[slot], {"tile": (tile + sign + NX) % NX})
            sums[(sign, half, step)] = (copy, slot)

    shared_step(0)
    swapped = [
        post.send(down_ref.at[half_units], weight_ref.at[1 - side, 1, 2], across[side])
        for side, half_units in ((0, low_units), (1, high_units))
    ]
    for j in range(CHUNKS):
        ring_ref[j, z] = rows_ref[:, j * chunk : (j + 1) * chunk]
    gated = gated_ref[...].T
    high = gated.astype(high_ref.dtype)
    high_ref[...] = high
    low_ref[...] = (gated - high.astype(jnp.float32)).astype(low_ref.dtype)

    swaps, own, handed = {}, [], []

    def hand_on(j, k, source):
        for side in (0, 1):
            handed.append(post.send(source, slots_ref.at[2 * side, k, :, cols[j]], across[side]))

    def choose(j):
        for sign, half, _ in Z_STREAMS:
            arrivals[(j, sign, half)].wait_recv()
        gathered = ring_ref[j].reshape(NZ * tokens, chunk)
        chosen_ref[j] = (
            jnp.dot(select_ref[...], gathered, preferred_element_type=jnp.float32)
            .astype(chosen_ref.dtype)
            .reshape(chosen_ref.shape[1:])
        )
        for k, peer in enumerate(peers, 1):
            swaps[(j, k)] = post.send(
                chosen_ref.at[j, peer], slots_ref.at[1, k, :, cols[j]], group(peer)
            )
        copy = pltpu.make_async_copy(
            chosen_ref.at[j, me], slots_ref.at[1, 0, :, cols[j]], local_sem.at[j]
        )
        copy.start()
        own.append(copy)
        hand_on(j, 0, chosen_ref.at[j, me])

    def forward(j):
        for k in range(1, GROUP):
            swaps[(j, k)].wait_recv()
            hand_on(j, k, slots_ref.at[1, k, :, cols[j]])

    for wave in range(CHUNKS + Z_HALF - 1):
        for number in range(Z_HALF, 1, -1):
            j = wave - (number - 2)
            if 0 <= j < CHUNKS:
                hop(j, number)
        if wave == 0:
            shared_step(1)
        j = wave - (Z_HALF - 1)
        if 0 <= j < CHUNKS:
            choose(j)
    for j in range(CHUNKS):
        forward(j)

    def feed_forward(which, mine, job):
        first = job * PER_JOB
        place = 2 * which * (1 - mine) + mine
        rows = slots_ref[place, pl.ds(first, PER_JOB)].reshape(PER_JOB * slots, width)
        contract = (((1,), (1,)), ((), ()))
        for piece in (0, 1):
            gate = lax.dot_general(
                rows, weight_ref[which, piece, 0], contract, preferred_element_type=jnp.float32
            )
            up = lax.dot_general(
                rows, weight_ref[which, piece, 1], contract, preferred_element_type=jnp.float32
            )
            hidden_ref[piece] = (gate / (1.0 + jnp.exp(-gate)) * up).astype(hidden_ref.dtype)
        for j in range(CHUNKS):
            total = jnp.dot(
                hidden_ref[0], weight_ref[which, 0, 2, :, cols[j]],
                preferred_element_type=jnp.float32,
            ) + jnp.dot(
                hidden_ref[1], weight_ref[which, 1, 2, :, cols[j]],
                preferred_element_type=jnp.float32,
            )
            part_ref[which, mine, pl.ds(first, PER_JOB), :, cols[j]] = total.astype(
                part_ref.dtype
            ).reshape(PER_JOB, slots, chunk)

    def side_copy(which, j, k):
        number = (which * CHUNKS + j) * GROUP + k
        neighbour = tile + 1 - 2 * (tile % 2)
        other = NX - 1 - tile
        return pltpu.make_async_remote_copy(
            src_ref=part_ref.at[which, 0, k, :, cols[j]],
            dst_ref=side_ref.at[which, j, k],
            send_sem=side_send.at[number],
            recv_sem=side_recv.at[number],
            device_id={"tile": neighbour + which * (other - neighbour)},
            device_id_type=MESH,
        )

    for copy in loads + own:
        copy.wait()
    for copy in swapped:
        copy.wait_recv()

    def own_job(i, carry):
        feed_forward(i % 2, 1, i // 2)
        return carry

    lax.fori_loop(0, 4, own_job, 0)
    for copy in handed:
        copy.wait_recv()

    def side_job(i, carry):
        which, job = i % 2, i // 2
        feed_forward(which, 0, job)
        for j in range(CHUNKS):
            for k in range(PER_JOB):
                side_copy(which, j, job * PER_JOB + k).start()
        return carry

    lax.fori_loop(0, 4, side_job, 0)

    for half in (0, 1):
        total = shared_ref[tile, part[half]].astype(jnp.float32)
        for sign, this, length in X_STREAMS:
            if this == half:
                copy, slot = sums[(sign, half, length - 1)]
                copy.wait_recv()
                total = total + sum_land_ref[slot].astype(jnp.float32)
        base_ref[part[half]] = total + tokens_ref[part[half]].astype(jnp.float32)
    returns, steps = {}, {}

    def add_up(j, ks):
        for k in ks:
            for which in (0, 1):
                side_copy(which, j, k).wait_recv()
            total = (
                part_ref[0, 1, k, :, cols[j]].astype(jnp.float32)
                + part_ref[1, 1, k, :, cols[j]].astype(jnp.float32)
                + side_ref[0, j, k].astype(jnp.float32)
                + side_ref[1, j, k].astype(jnp.float32)
            ).astype(stage_ref.dtype)
            if k == 0:
                back_ref[j, me] = total
            else:
                stage_ref[j, k] = total
                returns[(j, k)] = post.send(
                    stage_ref.at[j, k], back_ref.at[j, me], group((me - k + GROUP) % GROUP)
                )

    def step(j, number):
        for i, (sign, half, length) in enumerate(Z_STREAMS):
            if number >= length:
                continue
            target = (z + sign * (length - number) + NZ) % NZ
            slot = i * Z_HALF + number
            if number == 0:
                source = mix_ref.at[j, target, part[half]]
            else:
                steps[(j, i, number - 1)].wait_recv()
                step_ref[j, slot] = (
                    mix_ref[j, target, part[half]].astype(jnp.float32)
                    + land_ref[j, slot - 1].astype(jnp.float32)
                ).astype(step_ref.dtype)
                source = step_ref.at[j, slot]
            steps[(j, i, number)] = post.send(
                source, land_ref.at[j, slot], ring((z + sign + NZ) % NZ)
            )

    def combine(j):
        for k in range(1, GROUP):
            returns[(j, k)].wait_recv()
        back = back_ref[j].reshape(high_ref.shape[1], chunk)
        mix_ref[j] = (
            (
                jnp.dot(high_ref[...], back, preferred_element_type=jnp.float32)
                + jnp.dot(low_ref[...], back, preferred_element_type=jnp.float32)
            )
            .astype(mix_ref.dtype)
            .reshape(mix_ref.shape[1:])
        )
        step(j, 0)

    for j in range(CHUNKS):
        add_up(j, range(PER_JOB))
    for wave in range(CHUNKS + Z_HALF + 1):
        if wave < CHUNKS:
            add_up(wave, range(PER_JOB, GROUP))
        if 0 <= wave - 1 < CHUNKS:
            combine(wave - 1)
        for number in range(1, Z_HALF):
            if 0 <= wave - 1 - number < CHUNKS:
                step(wave - 1 - number, number)
    for j in range(CHUNKS):
        for half in (0, 1):
            total = base_ref[part[half], cols[j]] + mix_ref[j, z, part[half]].astype(
                jnp.float32
            )
            for i, (_, this, length) in enumerate(Z_STREAMS):
                if this == half:
                    steps[(j, i, length - 1)].wait_recv()
                    total = total + land_ref[j, i * Z_HALF + length - 1].astype(jnp.float32)
            out_ref[part[half], cols[j]] = total.astype(out_ref.dtype)
    for copy in post.made:
        copy.wait_send()
    for which in (0, 1):
        for j in range(CHUNKS):
            for k in range(GROUP):
                side_copy(which, j, k).wait_send()


def expert_layer(rows, select, shared_rows, gated, tokens_moe, weights, collective_id):
    tokens, width = rows.shape
    slots = NZ * CAP
    chunk = width // CHUNKS
    kind = rows.dtype
    units = weights[-1].shape[0]
    copies = CHUNKS * (2 * Z_COPIES + 2 * (GROUP - 1) + 2 * GROUP) + X_COPIES + 2
    boxes = pltpu.VMEM((CHUNKS, len(Z_STREAMS) * Z_HALF, tokens // 2, chunk), kind)
    blocks = pltpu.VMEM((CHUNKS, GROUP, slots, chunk), kind)
    shared_boxes = pltpu.VMEM((X_COPIES, tokens // 2, width), kind)
    spread = pltpu.VMEM((CHUNKS, NZ, tokens, chunk), kind)
    return pl.pallas_call(
        expert_kernel,
        out_shape=jax.ShapeDtypeStruct((tokens, width), kind),
        in_specs=[pl.BlockSpec(memory_space=pltpu.VMEM)] * 5
        + [pl.BlockSpec(memory_space=pl.ANY)] * len(weights),
        out_specs=pl.BlockSpec(memory_space=pltpu.VMEM),
        scratch_shapes=[
            spread,
            blocks,
            shared_boxes,
            shared_boxes,
            pltpu.VMEM((3, GROUP, slots, width), kind),
            pltpu.VMEM((2, 2, 3, units, width), kind),
            pltpu.VMEM((2, PER_JOB * slots, units), kind),
            pltpu.VMEM((2, 2, GROUP, slots, width), kind),
            pltpu.VMEM(gated.shape[::-1], kind),
            pltpu.VMEM(gated.shape[::-1], kind),
            pltpu.VMEM((2, CHUNKS, GROUP, slots, chunk), kind),
            blocks,
            blocks,
            spread,
            boxes,
            boxes,
            pltpu.VMEM((tokens, width), jnp.float32),
            pltpu.SemaphoreType.DMA((copies,)),
            pltpu.SemaphoreType.DMA((copies,)),
            pltpu.SemaphoreType.DMA((CHUNKS,)),
            pltpu.SemaphoreType.DMA((10,)),
            pltpu.SemaphoreType.DMA((2 * CHUNKS * GROUP,)),
            pltpu.SemaphoreType.DMA((2 * CHUNKS * GROUP,)),
        ],
        compiler_params=pltpu.CompilerParams(
            collective_id=collective_id, has_side_effects=True, vmem_limit_bytes=56 * 2**20
        ),
    )(rows, select, shared_rows, gated, tokens_moe, *weights)


def token_kernel(chunks, block_ref, gain_ref, own_ref, in_ref, page_ref, all_ref, send_sem, recv_sem, local_sem):
    tile = lax.axis_index("tile")
    rows, width = block_ref.shape
    tokens = own_ref.shape[0]
    post = Sender(send_sem, recv_sem)
    greet([{"tile": (tile + sign + NX) % NX} for sign in (1, -1)])

    def at(block, part):
        return all_ref.at[part, pl.ds(pl.multiple_of(block * width, width), width)]

    arrivals = {}
    for hop in (1, 2):
        for sign, i in interleave(
            [(1, i) for i in dir_order(chunks, 1)], [(-1, i) for i in dir_order(chunks, -1)]
        ):
            start, size, far = chunks[i]
            if hop == 2 and far != sign:
                continue
            block, part = (tile - sign * (hop - 1) + NX) % NX, pl.ds(start, size)
            if hop == 1:
                source = block_ref.at[part]
            else:
                arrivals[(sign, i, 1)].wait_recv()
                source = at(block, part)
            arrivals[(sign, i, hop)] = post.send(
                source, at(block, part), {"tile": (tile + sign + NX) % NX}
            )
        if hop == 1:
            own = pltpu.make_async_copy(block_ref, at(tile, pl.ds(0, rows)), local_sem)
            own.start()
    for (sign, i, hop), copy in arrivals.items():
        if hop == 2 or chunks[i][2] != sign:
            copy.wait_recv()
    own.wait()

    def normed(values):
        values = values.astype(jnp.float32)
        mean = jnp.mean(values * values, axis=-1, keepdims=True)
        return (values * lax.rsqrt(mean + norm_eps) * gain_ref[...]).astype(jnp.bfloat16)

    for start in range(0, rows, tokens):
        page_ref[start : start + tokens] = normed(all_ref[start : start + tokens])
    mine = pl.ds(pl.multiple_of(tile * tokens, tokens), tokens)
    own_ref[...] = all_ref[mine]
    in_ref[...] = page_ref[mine]
    for copy in post.made:
        copy.wait_send()


def gather_tokens(block, gain, tokens, collective_id):
    rows, width = block.shape
    chunks = ring_chunks(rows, tokens)
    copies = copies_of("x", chunks)

    def kernel(*refs):
        token_kernel(chunks, *refs)

    return pl.pallas_call(
        kernel,
        out_shape=[
            jax.ShapeDtypeStruct((tokens, NX * width), block.dtype),
            jax.ShapeDtypeStruct((tokens, NX * width), block.dtype),
            jax.ShapeDtypeStruct((rows, NX * width), block.dtype),
        ],
        in_specs=[pl.BlockSpec(memory_space=pltpu.VMEM)] * 2,
        out_specs=[pl.BlockSpec(memory_space=pltpu.VMEM)] * 3,
        scratch_shapes=[
            pltpu.VMEM((rows, NX * width), block.dtype),
            pltpu.SemaphoreType.DMA((copies,)),
            pltpu.SemaphoreType.DMA((copies,)),
            pltpu.SemaphoreType.DMA,
        ],
        compiler_params=pltpu.CompilerParams(collective_id=collective_id, has_side_effects=True),
    )(block, gain.reshape(1, -1))


def slot_tables(table, tokens, top):
    picks = table[:, :top, :tokens].transpose(1, 0, 2).reshape(top, NZ * tokens)
    gates = table[:, 8 : 8 + top, :tokens].transpose(1, 0, 2).reshape(top, NZ * tokens)
    z = (lax.axis_index("expert") // NC) % NZ
    member = jnp.arange(GROUP)
    experts = ((member // NC) * NZ + z) * NC + member % NC
    match = picks[None] == experts.astype(jnp.float32)[:, None, None]
    hit = jnp.any(match, axis=1)
    gate = jnp.sum(jnp.where(match, gates[None], 0.0), axis=1)
    column = jnp.arange(NZ * tokens)
    page = column // tokens
    earlier = (page[:, None] == page[None, :]) & (column[:, None] < column[None, :])
    rank = jnp.dot(
        hit.astype(jnp.bfloat16), earlier.astype(jnp.bfloat16), preferred_element_type=jnp.float32
    )
    slot = jnp.arange(NZ * CAP)
    here = (slot // CAP)[:, None] == page[None, :]
    ranked = rank[:, None, :] == (slot % CAP).astype(jnp.float32)[None, :, None]
    chosen = here[None] & ranked & hit[:, None, :]
    select = chosen.astype(jnp.bfloat16).reshape(GROUP * NZ * CAP, NZ * tokens)
    gated = jnp.where(chosen, gate[:, None, :], 0.0).reshape(GROUP * NZ * CAP, NZ * tokens)
    return select, gated


def per_device(
    patches,
    norm1_gain,
    qkv_weight,
    qkv_bias,
    out_weight,
    out_bias,
    norm2_gain,
    proj_weight,
    moe_gain,
    expert_in,
    expert_out,
    shared_in,
    shared_out,
    routes,
    gates,
):
    tile_id = lax.axis_index("tile")
    row_count = patches.shape[1]
    columns = patches.shape[2]
    width_vit = patches.shape[3]
    local_rows = row_count * columns
    tokens = local_rows // 4
    top = routes.shape[-1]
    side_a = [(t, t + 1 - 2 * (t % 2)) for t in range(NX)]
    side_b = [(t, NX - 1 - t) for t in range(NX)]
    units = expert_out.shape[1] // 2
    in_rows = expert_in[0].transpose(1, 2, 0)
    gate_halves = in_rows[0, :units], in_rows[0, units:]
    up_halves = in_rows[1, :units], in_rows[1, units:]

    def swap(halves, after):
        first, second, after = lax.optimization_barrier((*halves, after))
        from_a = lax.ppermute(first, "tile", side_a)
        from_b = lax.ppermute(second, "tile", side_b)
        return from_a, from_b, after

    project = lax.all_gather(proj_weight, "expert", axis=0, tiled=True)

    inputs = patches.reshape(local_rows, width_vit).astype(jnp.float32)
    normed = layer_norm(inputs, norm1_gain).astype(jnp.bfloat16)
    own_routes = lax.dynamic_index_in_dim(
        routes.reshape(NX, tokens, top), tile_id, 0, keepdims=False
    )
    table = jnp.zeros((16, 128), jnp.float32)
    table = table.at[:top, :tokens].set(own_routes.T.astype(jnp.float32))
    table = table.at[8 : 8 + top, :tokens].set(gates.reshape(tokens, top).T)
    piece, tables_z = ring_gather([("x", normed, 32), ("z", table, 16)], 0)
    gate_a, gate_b, piece = swap(gate_halves, piece)
    piece = piece.reshape(NX * local_rows, width_vit)

    heads_here = qkv_weight.shape[2] // HD
    qkv_flat = qkv_weight.reshape(width_vit, -1)
    bias_rows = qkv_bias.reshape(1, 3, heads_here, HD)
    mixed_flat = jnp.dot(piece, qkv_flat, preferred_element_type=jnp.float32)
    mixed = (
        mixed_flat.reshape(
            piece.shape[0], 3, heads_here, HD
        )
        + bias_rows
    )
    tables = rope_tables(jnp.arange(piece.shape[0]), columns, HD)
    attended = attend(
        rotate(mixed[:, 0], tables).astype(jnp.bfloat16),
        rotate(mixed[:, 1], tables).astype(jnp.bfloat16),
        mixed[:, 2].astype(jnp.bfloat16),
        math.sqrt(HD),
    )
    partial_rows = (
        jnp.dot(attended, out_weight, preferred_element_type=jnp.float32)
        .astype(jnp.bfloat16)
        .reshape(NX, local_rows, width_vit)
    )
    (mixed_heads,) = ring_reduce([("x", partial_rows, 32, jnp.float32)], 1)
    hidden = inputs + mixed_heads + out_bias
    normed_out = layer_norm(hidden, norm2_gain).astype(jnp.bfloat16)
    merged = (
        normed_out.reshape(row_count // 2, 2, columns // 2, 2, width_vit)
        .transpose(0, 2, 1, 3, 4)
        .reshape(tokens, 4 * width_vit)
    )
    (group_merged,) = ring_gather([("x", merged, 16)], 2)
    up_a, up_b, group_merged = swap(up_halves, group_merged)
    select, gated = slot_tables(tables_z, tokens, top)
    projected = jnp.dot(
        group_merged.reshape(NX * tokens, -1), project, preferred_element_type=jnp.float32
    ).astype(jnp.bfloat16)
    tokens_moe, moe_in, page_in = gather_tokens(projected, moe_gain, tokens, 3)
    width_moe = page_in.shape[1]
    shared_gated = jnp.dot(
        page_in, shared_in.reshape(width_moe, -1), preferred_element_type=jnp.float32
    ).reshape(NX * tokens, 2, -1)
    shared_hidden = (jax.nn.silu(shared_gated[:, 0]) * shared_gated[:, 1]).astype(jnp.bfloat16)
    shared_rows = (
        jnp.dot(shared_hidden, shared_out, preferred_element_type=jnp.float32)
        .astype(jnp.bfloat16)
        .reshape(NX, tokens, width_moe)
    )

    output = expert_layer(
        moe_in,
        select,
        shared_rows,
        gated,
        tokens_moe,
        (in_rows, expert_out[0], gate_a, up_a, gate_b, up_b),
        4,
    )
    return output.reshape(1, row_count // 2, columns // 2, width_moe)


def solution(mesh):
    placed = (
        P("expert", "tile", None, None),
        P(),
        P(None, None, "tile"),
        P(None, "tile"),
        P("tile", None),
        P(),
        P(),
        P("expert", "tile"),
        P(),
        P("expert", None, None, "tile"),
        P("expert", "tile", None),
        P(None, None, "tile"),
        P("tile", None),
        P("expert", None, None, None),
        P("expert", "tile", None, None),
    )
    return jax.shard_map(
        per_device,
        mesh=mesh,
        in_specs=placed,
        out_specs=P("expert", "tile", None, None),
        check_vma=False,
    )
```

```python
import math

import jax
import jax.numpy as jnp
from jax import lax
from jax.experimental import pallas as pl
from jax.experimental.pallas import tpu as pltpu
from jax.sharding import PartitionSpec as P


HD = 72
NX, NY, NZ, NC = 4, 4, 8, 2
GROUP = NY * NC
CAP = 6
MESH = pl.DeviceIdType.MESH

norm_eps = 1e-06
rope_base = 10000.0


def layer_norm(values, gain_vec):
    centre = values - jnp.mean(values, axis=-1, keepdims=True)
    spread = jnp.mean(centre * centre, axis=-1, keepdims=True)
    return centre * lax.rsqrt(spread + norm_eps) * gain_vec


def rope_tables(positions, columns, head_size):
    quarter = head_size // 4
    inverse = jnp.exp(jnp.arange(quarter).astype(jnp.float32) * (-math.log(rope_base) / quarter))
    row_angle = (positions // columns).astype(jnp.float32)[:, None] * inverse[None, :]
    col_angle = (positions % columns).astype(jnp.float32)[:, None] * inverse[None, :]
    return (jnp.cos(row_angle), jnp.sin(row_angle), jnp.cos(col_angle), jnp.sin(col_angle))


def rotate(values, tables):
    cos_row, sin_row, cos_col, sin_col = tables
    quarter = values.shape[-1] // 4
    row_a = values[..., :quarter]
    row_b = values[..., quarter : 2 * quarter]
    col_a = values[..., 2 * quarter : 3 * quarter]
    col_b = values[..., 3 * quarter :]
    return jnp.concatenate(
        [
            row_a * cos_row[:, None] - row_b * sin_row[:, None],
            row_b * cos_row[:, None] + row_a * sin_row[:, None],
            col_a * cos_col[:, None] - col_b * sin_col[:, None],
            col_b * cos_col[:, None] + col_a * sin_col[:, None],
        ],
        axis=-1,
    )


def attend(query_rows, key_rows, value_rows, divisor):
    scores = (
        jnp.einsum("qhd,khd->hqk", query_rows, key_rows, preferred_element_type=jnp.float32)
        / divisor
    )
    weights = jax.nn.softmax(scores, axis=-1).astype(jnp.bfloat16)
    attended = jnp.einsum(
        "hqk,khd->qhd", weights, value_rows, preferred_element_type=jnp.float32
    ).astype(jnp.bfloat16)
    return attended.reshape(attended.shape[0], -1)


def ring_place(axis):
    if axis == "x":
        return lax.axis_index("tile"), NX, lambda place: {"tile": place}
    here = lax.axis_index("expert")
    y, z, core = here // (NZ * NC), (here // NC) % NZ, here % NC
    return z, NZ, lambda place: {"expert": (y * NZ + place) * NC + core}


def greet(device_ids):
    barrier = pltpu.get_barrier_semaphore()
    for device_id in device_ids:
        pl.semaphore_signal(barrier, inc=1, device_id=device_id, device_id_type=MESH)
    pl.semaphore_wait(barrier, len(device_ids))


def ring_chunks(rows, step):
    starts = list(range(0, rows, step))
    half = (len(starts) + 1) // 2
    return [(s, step, 1 if i < half else -1) for i, s in enumerate(starts)]


def dir_order(chunks, sign):
    ids = range(len(chunks))
    return [i for i in ids if chunks[i][2] == sign] + [i for i in ids if chunks[i][2] != sign]


def interleave(a, b):
    out = []
    for i in range(max(len(a), len(b))):
        out += a[i : i + 1] + b[i : i + 1]
    return out


def ring_gather_kernel(plan, *refs):
    count = len(plan)
    ins, outs = refs[:count], refs[count : 2 * count]
    send_sem, recv_sem, local_sem = refs[2 * count :]
    rings = {axis: ring_place(axis) for axis, _ in plan}
    greet(
        [
            device((here + sign) % size)
            for here, size, device in rings.values()
            for sign in (1, -1)
        ]
    )
    arrivals, sends, number = {}, [], 0
    longest = max(rings[axis][1] // 2 for axis, _ in plan)
    local = []
    for hop in range(1, longest + 1):
        for task, (axis, chunks) in enumerate(plan):
            here, size, device = rings[axis]
            if hop > size // 2:
                continue
            order = interleave(
                [(1, i) for i in dir_order(chunks, 1)], [(-1, i) for i in dir_order(chunks, -1)]
            )
            for sign, i in order:
                start, rows, far = chunks[i]
                if hop == size // 2 and far != sign:
                    continue
                block = (here - sign * (hop - 1) + size) % size
                part = pl.ds(start, rows)
                if hop == 1:
                    source = ins[task].at[part]
                else:
                    arrivals.pop((task, sign, i)).wait_recv()
                    source = outs[task].at[block, part]
                copy = pltpu.make_async_remote_copy(
                    src_ref=source,
                    dst_ref=outs[task].at[block, part],
                    send_sem=send_sem.at[number],
                    recv_sem=recv_sem.at[number],
                    device_id=device((here + sign + size) % size),
                    device_id_type=MESH,
                )
                copy.start()
                arrivals[(task, sign, i)] = copy
                sends.append(copy)
                number += 1
        if hop == 1:
            for task, (axis, _) in enumerate(plan):
                own = pltpu.make_async_copy(
                    ins[task], outs[task].at[rings[axis][0]], local_sem.at[task]
                )
                own.start()
                local.append(own)
    for copy in arrivals.values():
        copy.wait_recv()
    for copy in sends:
        copy.wait_send()
    for own in local:
        own.wait()


def copies_of(axis, chunks):
    half = (NX if axis == "x" else NZ) // 2
    return sum(half + half - 1 for _ in chunks)


def ring_gather(tasks, collective_id):
    plan = [(axis, ring_chunks(block.shape[0], step)) for axis, block, step in tasks]
    copies = sum(copies_of(*entry) for entry in plan)
    sizes = {"x": NX, "z": NZ}

    def kernel(*refs):
        ring_gather_kernel(plan, *refs)

    return pl.pallas_call(
        kernel,
        out_shape=[
            jax.ShapeDtypeStruct((sizes[axis],) + block.shape, block.dtype)
            for axis, block, _ in tasks
        ],
        in_specs=[pl.BlockSpec(memory_space=pltpu.VMEM)] * len(tasks),
        out_specs=[pl.BlockSpec(memory_space=pltpu.VMEM)] * len(tasks),
        scratch_shapes=[
            pltpu.SemaphoreType.DMA((copies,)),
            pltpu.SemaphoreType.DMA((copies,)),
            pltpu.SemaphoreType.DMA((len(tasks),)),
        ],
        compiler_params=pltpu.CompilerParams(collective_id=collective_id, has_side_effects=True),
    )(*[block for _, block, _ in tasks])


def ring_reduce_kernel(plan, *refs):
    count = len(plan)
    ins, outs = refs[:count], refs[count : 2 * count]
    landed, staged = refs[2 * count : 3 * count], refs[3 * count : 4 * count]
    send_sem, recv_sem = refs[4 * count :]
    rings = {axis: ring_place(axis) for axis, _ in plan}
    greet(
        [
            device((here + sign + size) % size)
            for here, size, device in rings.values()
            for sign in (1, -1)
        ]
    )
    last, sends, number = {}, [], 0
    slots = [0] * count
    for step in range(max(rings[axis][1] // 2 for axis, _ in plan)):
        for task, (axis, chunks) in enumerate(plan):
            here, size, device = rings[axis]
            half = size // 2
            order = interleave(
                [(1, i) for i in dir_order(chunks, 1)], [(-1, i) for i in dir_order(chunks, -1)]
            )
            for sign, i in order:
                start, rows, far = chunks[i]
                length = half if far == sign else half - 1
                if step >= length:
                    continue
                part = pl.ds(start, rows)
                target = (here + sign * (length - step) + size) % size
                slot = slots[task]
                slots[task] += 1
                if step == 0:
                    source = ins[task].at[target, part]
                else:
                    copy, before = last[(task, sign, i)]
                    copy.wait_recv()
                    staged[task][slot] = (
                        ins[task][target, part].astype(jnp.float32)
                        + landed[task][before].astype(jnp.float32)
                    ).astype(staged[task].dtype)
                    source = staged[task].at[slot]
                copy = pltpu.make_async_remote_copy(
                    src_ref=source,
                    dst_ref=landed[task].at[slot],
                    send_sem=send_sem.at[number],
                    recv_sem=recv_sem.at[number],
                    device_id=device((here + sign + size) % size),
                    device_id_type=MESH,
                )
                copy.start()
                last[(task, sign, i)] = (copy, slot)
                sends.append(copy)
                number += 1
    for task, (axis, chunks) in enumerate(plan):
        here = rings[axis][0]
        for i, (start, rows, _) in enumerate(chunks):
            part = pl.ds(start, rows)
            total = ins[task][here, part].astype(jnp.float32)
            for sign in (1, -1):
                if (task, sign, i) in last:
                    copy, slot = last[(task, sign, i)]
                    copy.wait_recv()
                    total = total + landed[task][slot].astype(jnp.float32)
            outs[task][part] = total.astype(outs[task].dtype)
    for copy in sends:
        copy.wait_send()


def ring_reduce(tasks, collective_id):
    plan = [(axis, ring_chunks(block.shape[1], step)) for axis, block, step, _ in tasks]
    copies = [copies_of(*entry) for entry in plan]

    def kernel(*refs):
        ring_reduce_kernel(plan, *refs)

    boxes = [
        pltpu.VMEM((number, step, block.shape[2]), block.dtype)
        for number, (_, block, step, _) in zip(copies, tasks)
    ]
    return pl.pallas_call(
        kernel,
        out_shape=[jax.ShapeDtypeStruct(block.shape[1:], kind) for _, block, _, kind in tasks],
        in_specs=[pl.BlockSpec(memory_space=pltpu.VMEM)] * len(tasks),
        out_specs=[pl.BlockSpec(memory_space=pltpu.VMEM)] * len(tasks),
        scratch_shapes=boxes
        + boxes
        + [pltpu.SemaphoreType.DMA((sum(copies),)), pltpu.SemaphoreType.DMA((sum(copies),))],
        compiler_params=pltpu.CompilerParams(collective_id=collective_id, has_side_effects=True),
    )(*[block for _, block, _, _ in tasks])


CHUNKS = 2


def places():
    tile, here = lax.axis_index("tile"), lax.axis_index("expert")
    y, z, core = here // (NZ * NC), (here // NC) % NZ, here % NC
    across = {"tile": tile + 1 - 2 * (tile % 2)}, {"tile": NX - 1 - tile}

    def group(member):
        return {"expert": ((member // NC) * NZ + z) * NC + member % NC}

    def ring(place):
        return {"expert": (y * NZ + place) * NC + core}

    return tile, z, y * NC + core, across, group, ring


class Sender:
    def __init__(self, send_sem, recv_sem):
        self.send_sem, self.recv_sem, self.made = send_sem, recv_sem, []

    def send(self, source, target, device):
        number = len(self.made)
        copy = pltpu.make_async_remote_copy(
            src_ref=source,
            dst_ref=target,
            send_sem=self.send_sem.at[number],
            recv_sem=self.recv_sem.at[number],
            device_id=device,
            device_id_type=MESH,
        )
        copy.start()
        self.made.append(copy)
        return copy


Z_HALF = NZ // 2
Z_STREAMS = [(sign, half, Z_HALF if (half == 0) == (sign == 1) else Z_HALF - 1)
             for sign in (1, -1) for half in (0, 1)]
Z_STREAMS.sort(key=lambda stream: -stream[2])
X_HALF = NX // 2
X_STREAMS = [(sign, half, X_HALF if (half == 0) == (sign == 1) else X_HALF - 1)
             for sign in (1, -1) for half in (0, 1)]
X_STREAMS.sort(key=lambda stream: -stream[2])
Z_COPIES = sum(length for _, _, length in Z_STREAMS)
X_COPIES = sum(length for _, _, length in X_STREAMS)


PER_JOB = GROUP // 2


def expert_kernel(
    rows_ref, select_ref, shared_ref, gated_ref, tokens_ref, in_ref, down_ref,
    gate_a_ref, up_a_ref, gate_b_ref, up_b_ref,
    out_ref,
    ring_ref, chosen_ref, sum_land_ref, sum_stage_ref, slots_ref, weight_ref, hidden_ref, part_ref,
    high_ref, low_ref, side_ref, stage_ref, back_ref, mix_ref, land_ref, step_ref, base_ref,
    send_sem, recv_sem, local_sem, weight_sem, side_send, side_recv,
):
    tile, z, me, across, group, ring = places()
    tokens, width = rows_ref.shape
    chunk, half_rows = width // CHUNKS, tokens // 2
    slots = NZ * CAP
    units = gate_a_ref.shape[0]
    post = Sender(send_sem, recv_sem)
    peers = [(me + k) % GROUP for k in range(1, GROUP)]
    low_units, high_units = pl.ds(0, units), pl.ds(units, units)
    loads = []
    for where, source in (
        ((0, 0, 0), in_ref.at[0, high_units]),
        ((0, 0, 1), in_ref.at[1, high_units]),
        ((0, 0, 2), down_ref.at[high_units]),
        ((0, 1, 0), gate_b_ref),
        ((0, 1, 1), up_b_ref),
        ((1, 0, 0), in_ref.at[0, low_units]),
        ((1, 0, 1), in_ref.at[1, low_units]),
        ((1, 0, 2), down_ref.at[low_units]),
        ((1, 1, 0), gate_a_ref),
        ((1, 1, 1), up_a_ref),
    ):
        copy = pltpu.make_async_copy(source, weight_ref.at[where], weight_sem.at[len(loads)])
        copy.start()
        loads.append(copy)
    greet(
        [ring((z + 1) % NZ), ring((z + NZ - 1) % NZ)]
        + [group(peer) for peer in peers]
        + list(across)
    )
    cols = [pl.ds(j * chunk, chunk) for j in range(CHUNKS)]
    part = [pl.ds(h * half_rows, half_rows) for h in (0, 1)]
    arrivals = {}

    def hop(j, number):
        for sign, half, length in Z_STREAMS:
            if number > length:
                continue
            block = (z - sign * (number - 1) + NZ) % NZ
            if number == 1:
                source = rows_ref.at[part[half], cols[j]]
            else:
                arrivals[(j, sign, half)].wait_recv()
                source = ring_ref.at[j, block, part[half]]
            arrivals[(j, sign, half)] = post.send(
                source, ring_ref.at[j, block, part[half]], ring((z + sign + NZ) % NZ)
            )

    for j in range(CHUNKS):
        hop(j, 1)

    sums = {}

    def shared_step(step):
        for sign, half, length in X_STREAMS:
            if step >= length:
                continue
            target = (tile + sign * (length - step) + NX) % NX
            slot = len(sums)
            if step == 0:
                source = shared_ref.at[target, part[half]]
            else:
                copy, before = sums[(sign, half, step - 1)]
                copy.wait_recv()
                sum_stage_ref[slot] = (
                    shared_ref[target, part[half]].astype(jnp.float32)
                    + sum_land_ref[before].astype(jnp.float32)
                ).astype(sum_stage_ref.dtype)
                source = sum_stage_ref.at[slot]
            copy = post.send(source, sum_land_ref.at[slot], {"tile": (tile + sign + NX) % NX})
            sums[(sign, half, step)] = (copy, slot)

    shared_step(0)
    swapped = [
        post.send(down_ref.at[half_units], weight_ref.at[1 - side, 1, 2], across[side])
        for side, half_units in ((0, low_units), (1, high_units))
    ]
    for j in range(CHUNKS):
        ring_ref[j, z] = rows_ref[:, j * chunk : (j + 1) * chunk]
    gated = gated_ref[...].T
    high = gated.astype(high_ref.dtype)
    high_ref[...] = high
    low_ref[...] = (gated - high.astype(jnp.float32)).astype(low_ref.dtype)

    swaps, own, handed = {}, [], []

    def hand_on(j, k, source):
        for side in (0, 1):
            copy = post.send(source, slots_ref.at[2 * side, k, :, cols[j]], across[side])
            handed.append((k // PER_JOB, copy))

    def choose(j):
        for sign, half, _ in Z_STREAMS:
            arrivals[(j, sign, half)].wait_recv()
        gathered = ring_ref[j].reshape(NZ * tokens, chunk)
        chosen_ref[j] = (
            jnp.dot(select_ref[...], gathered, preferred_element_type=jnp.float32)
            .astype(chosen_ref.dtype)
            .reshape(chosen_ref.shape[1:])
        )
        for k, peer in enumerate(peers, 1):
            swaps[(j, k)] = post.send(
                chosen_ref.at[j, peer], slots_ref.at[1, k, :, cols[j]], group(peer)
            )
        copy = pltpu.make_async_copy(
            chosen_ref.at[j, me], slots_ref.at[1, 0, :, cols[j]], local_sem.at[j]
        )
        copy.start()
        own.append(copy)
        hand_on(j, 0, chosen_ref.at[j, me])

    def forward(j):
        for k in range(1, GROUP):
            swaps[(j, k)].wait_recv()
            hand_on(j, k, slots_ref.at[1, k, :, cols[j]])

    for wave in range(CHUNKS + Z_HALF - 1):
        for number in range(Z_HALF, 1, -1):
            j = wave - (number - 2)
            if 0 <= j < CHUNKS:
                hop(j, number)
        if wave == 0:
            shared_step(1)
        j = wave - (Z_HALF - 1)
        if 0 <= j < CHUNKS:
            choose(j)
    for j in range(CHUNKS):
        forward(j)

    def feed_forward(which, mine, job):
        first = job * PER_JOB
        place = 2 * which * (1 - mine) + mine
        rows = slots_ref[place, pl.ds(first, PER_JOB)].reshape(PER_JOB * slots, width)
        contract = (((1,), (1,)), ((), ()))
        for piece in (0, 1):
            gate = lax.dot_general(
                rows, weight_ref[which, piece, 0], contract, preferred_element_type=jnp.float32
            )
            up = lax.dot_general(
                rows, weight_ref[which, piece, 1], contract, preferred_element_type=jnp.float32
            )
            hidden_ref[piece] = (gate / (1.0 + jnp.exp(-gate)) * up).astype(hidden_ref.dtype)
        for j in range(CHUNKS):
            total = jnp.dot(
                hidden_ref[0], weight_ref[which, 0, 2, :, cols[j]],
                preferred_element_type=jnp.float32,
            ) + jnp.dot(
                hidden_ref[1], weight_ref[which, 1, 2, :, cols[j]],
                preferred_element_type=jnp.float32,
            )
            part_ref[which, mine, pl.ds(first, PER_JOB), :, cols[j]] = total.astype(
                part_ref.dtype
            ).reshape(PER_JOB, slots, chunk)

    def side_copy(which, j, k):
        number = (which * CHUNKS + j) * GROUP + k
        neighbour = tile + 1 - 2 * (tile % 2)
        other = NX - 1 - tile
        return pltpu.make_async_remote_copy(
            src_ref=part_ref.at[which, 0, k, :, cols[j]],
            dst_ref=side_ref.at[which, j, k],
            send_sem=side_send.at[number],
            recv_sem=side_recv.at[number],
            device_id={"tile": neighbour + which * (other - neighbour)},
            device_id_type=MESH,
        )

    for copy in loads + own:
        copy.wait()
    for copy in swapped:
        copy.wait_recv()

    def own_job(i, carry):
        feed_forward(i % 2, 1, i // 2)
        return carry

    lax.fori_loop(0, 4, own_job, 0)

    def side_job(i, carry):
        which, job = i % 2, i // 2
        feed_forward(which, 0, job)
        for j in range(CHUNKS):
            for k in range(PER_JOB):
                side_copy(which, j, job * PER_JOB + k).start()
        return carry

    for job in (0, 1):
        for this, copy in handed:
            if this == job:
                copy.wait_recv()
        lax.fori_loop(2 * job, 2 * job + 2, side_job, 0)

    for half in (0, 1):
        total = shared_ref[tile, part[half]].astype(jnp.float32)
        for sign, this, length in X_STREAMS:
            if this == half:
                copy, slot = sums[(sign, half, length - 1)]
                copy.wait_recv()
                total = total + sum_land_ref[slot].astype(jnp.float32)
        base_ref[part[half]] = total + tokens_ref[part[half]].astype(jnp.float32)
    returns, steps = {}, {}

    def add_up(j, ks):
        for k in ks:
            for which in (0, 1):
                side_copy(which, j, k).wait_recv()
            total = (
                part_ref[0, 1, k, :, cols[j]].astype(jnp.float32)
                + part_ref[1, 1, k, :, cols[j]].astype(jnp.float32)
                + side_ref[0, j, k].astype(jnp.float32)
                + side_ref[1, j, k].astype(jnp.float32)
            ).astype(stage_ref.dtype)
            if k == 0:
                back_ref[j, me] = total
            else:
                stage_ref[j, k] = total
                returns[(j, k)] = post.send(
                    stage_ref.at[j, k], back_ref.at[j, me], group((me - k + GROUP) % GROUP)
                )

    def step(j, number):
        for i, (sign, half, length) in enumerate(Z_STREAMS):
            if number >= length:
                continue
            target = (z + sign * (length - number) + NZ) % NZ
            slot = i * Z_HALF + number
            if number == 0:
                source = mix_ref.at[j, target, part[half]]
            else:
                steps[(j, i, number - 1)].wait_recv()
                step_ref[j, slot] = (
                    mix_ref[j, target, part[half]].astype(jnp.float32)
                    + land_ref[j, slot - 1].astype(jnp.float32)
                ).astype(step_ref.dtype)
                source = step_ref.at[j, slot]
            steps[(j, i, number)] = post.send(
                source, land_ref.at[j, slot], ring((z + sign + NZ) % NZ)
            )

    def combine(j):
        for k in range(1, GROUP):
            returns[(j, k)].wait_recv()
        back = back_ref[j].reshape(high_ref.shape[1], chunk)
        mix_ref[j] = (
            (
                jnp.dot(high_ref[...], back, preferred_element_type=jnp.float32)
                + jnp.dot(low_ref[...], back, preferred_element_type=jnp.float32)
            )
            .astype(mix_ref.dtype)
            .reshape(mix_ref.shape[1:])
        )
        step(j, 0)

    for j in range(CHUNKS):
        add_up(j, range(PER_JOB))
    for wave in range(CHUNKS + Z_HALF + 1):
        if wave < CHUNKS:
            add_up(wave, range(PER_JOB, GROUP))
        if 0 <= wave - 1 < CHUNKS:
            combine(wave - 1)
        for number in range(1, Z_HALF):
            if 0 <= wave - 1 - number < CHUNKS:
                step(wave - 1 - number, number)
    for j in range(CHUNKS):
        for half in (0, 1):
            total = base_ref[part[half], cols[j]] + mix_ref[j, z, part[half]].astype(
                jnp.float32
            )
            for i, (_, this, length) in enumerate(Z_STREAMS):
                if this == half:
                    steps[(j, i, length - 1)].wait_recv()
                    total = total + land_ref[j, i * Z_HALF + length - 1].astype(jnp.float32)
            out_ref[part[half], cols[j]] = total.astype(out_ref.dtype)
    for copy in post.made:
        copy.wait_send()
    for which in (0, 1):
        for j in range(CHUNKS):
            for k in range(GROUP):
                side_copy(which, j, k).wait_send()


def expert_layer(rows, select, shared_rows, gated, tokens_moe, weights, collective_id):
    tokens, width = rows.shape
    slots = NZ * CAP
    chunk = width // CHUNKS
    kind = rows.dtype
    units = weights[-1].shape[0]
    copies = CHUNKS * (2 * Z_COPIES + 2 * (GROUP - 1) + 2 * GROUP) + X_COPIES + 2
    boxes = pltpu.VMEM((CHUNKS, len(Z_STREAMS) * Z_HALF, tokens // 2, chunk), kind)
    blocks = pltpu.VMEM((CHUNKS, GROUP, slots, chunk), kind)
    shared_boxes = pltpu.VMEM((X_COPIES, tokens // 2, width), kind)
    spread = pltpu.VMEM((CHUNKS, NZ, tokens, chunk), kind)
    return pl.pallas_call(
        expert_kernel,
        out_shape=jax.ShapeDtypeStruct((tokens, width), kind),
        in_specs=[pl.BlockSpec(memory_space=pltpu.VMEM)] * 5
        + [pl.BlockSpec(memory_space=pl.ANY)] * len(weights),
        out_specs=pl.BlockSpec(memory_space=pltpu.VMEM),
        scratch_shapes=[
            spread,
            blocks,
            shared_boxes,
            shared_boxes,
            pltpu.VMEM((3, GROUP, slots, width), kind),
            pltpu.VMEM((2, 2, 3, units, width), kind),
            pltpu.VMEM((2, PER_JOB * slots, units), kind),
            pltpu.VMEM((2, 2, GROUP, slots, width), kind),
            pltpu.VMEM(gated.shape[::-1], kind),
            pltpu.VMEM(gated.shape[::-1], kind),
            pltpu.VMEM((2, CHUNKS, GROUP, slots, chunk), kind),
            blocks,
            blocks,
            spread,
            boxes,
            boxes,
            pltpu.VMEM((tokens, width), jnp.float32),
            pltpu.SemaphoreType.DMA((copies,)),
            pltpu.SemaphoreType.DMA((copies,)),
            pltpu.SemaphoreType.DMA((CHUNKS,)),
            pltpu.SemaphoreType.DMA((10,)),
            pltpu.SemaphoreType.DMA((2 * CHUNKS * GROUP,)),
            pltpu.SemaphoreType.DMA((2 * CHUNKS * GROUP,)),
        ],
        compiler_params=pltpu.CompilerParams(
            collective_id=collective_id, has_side_effects=True, vmem_limit_bytes=56 * 2**20
        ),
    )(rows, select, shared_rows, gated, tokens_moe, *weights)


def token_kernel(chunks, block_ref, gain_ref, own_ref, in_ref, page_ref, all_ref, send_sem, recv_sem, local_sem):
    tile = lax.axis_index("tile")
    rows, width = block_ref.shape
    tokens = own_ref.shape[0]
    post = Sender(send_sem, recv_sem)
    greet([{"tile": (tile + sign + NX) % NX} for sign in (1, -1)])

    def at(block, part):
        return all_ref.at[part, pl.ds(pl.multiple_of(block * width, width), width)]

    arrivals = {}
    for hop in (1, 2):
        for sign, i in interleave(
            [(1, i) for i in dir_order(chunks, 1)], [(-1, i) for i in dir_order(chunks, -1)]
        ):
            start, size, far = chunks[i]
            if hop == 2 and far != sign:
                continue
            block, part = (tile - sign * (hop - 1) + NX) % NX, pl.ds(start, size)
            if hop == 1:
                source = block_ref.at[part]
            else:
                arrivals[(sign, i, 1)].wait_recv()
                source = at(block, part)
            arrivals[(sign, i, hop)] = post.send(
                source, at(block, part), {"tile": (tile + sign + NX) % NX}
            )
        if hop == 1:
            own = pltpu.make_async_copy(block_ref, at(tile, pl.ds(0, rows)), local_sem)
            own.start()
    for (sign, i, hop), copy in arrivals.items():
        if hop == 2 or chunks[i][2] != sign:
            copy.wait_recv()
    own.wait()

    def normed(values):
        values = values.astype(jnp.float32)
        mean = jnp.mean(values * values, axis=-1, keepdims=True)
        return (values * lax.rsqrt(mean + norm_eps) * gain_ref[...]).astype(jnp.bfloat16)

    for start in range(0, rows, tokens):
        page_ref[start : start + tokens] = normed(all_ref[start : start + tokens])
    mine = pl.ds(pl.multiple_of(tile * tokens, tokens), tokens)
    own_ref[...] = all_ref[mine]
    in_ref[...] = page_ref[mine]
    for copy in post.made:
        copy.wait_send()


def gather_tokens(block, gain, tokens, collective_id):
    rows, width = block.shape
    chunks = ring_chunks(rows, tokens)
    copies = copies_of("x", chunks)

    def kernel(*refs):
        token_kernel(chunks, *refs)

    return pl.pallas_call(
        kernel,
        out_shape=[
            jax.ShapeDtypeStruct((tokens, NX * width), block.dtype),
            jax.ShapeDtypeStruct((tokens, NX * width), block.dtype),
            jax.ShapeDtypeStruct((rows, NX * width), block.dtype),
        ],
        in_specs=[pl.BlockSpec(memory_space=pltpu.VMEM)] * 2,
        out_specs=[pl.BlockSpec(memory_space=pltpu.VMEM)] * 3,
        scratch_shapes=[
            pltpu.VMEM((rows, NX * width), block.dtype),
            pltpu.SemaphoreType.DMA((copies,)),
            pltpu.SemaphoreType.DMA((copies,)),
            pltpu.SemaphoreType.DMA,
        ],
        compiler_params=pltpu.CompilerParams(collective_id=collective_id, has_side_effects=True),
    )(block, gain.reshape(1, -1))


def slot_tables(table, tokens, top):
    picks = table[:, :top, :tokens].transpose(1, 0, 2).reshape(top, NZ * tokens)
    gates = table[:, 8 : 8 + top, :tokens].transpose(1, 0, 2).reshape(top, NZ * tokens)
    z = (lax.axis_index("expert") // NC) % NZ
    member = jnp.arange(GROUP)
    experts = ((member // NC) * NZ + z) * NC + member % NC
    match = picks[None] == experts.astype(jnp.float32)[:, None, None]
    hit = jnp.any(match, axis=1)
    gate = jnp.sum(jnp.where(match, gates[None], 0.0), axis=1)
    column = jnp.arange(NZ * tokens)
    page = column // tokens
    earlier = (page[:, None] == page[None, :]) & (column[:, None] < column[None, :])
    rank = jnp.dot(
        hit.astype(jnp.bfloat16), earlier.astype(jnp.bfloat16), preferred_element_type=jnp.float32
    )
    slot = jnp.arange(NZ * CAP)
    here = (slot // CAP)[:, None] == page[None, :]
    ranked = rank[:, None, :] == (slot % CAP).astype(jnp.float32)[None, :, None]
    chosen = here[None] & ranked & hit[:, None, :]
    select = chosen.astype(jnp.bfloat16).reshape(GROUP * NZ * CAP, NZ * tokens)
    gated = jnp.where(chosen, gate[:, None, :], 0.0).reshape(GROUP * NZ * CAP, NZ * tokens)
    return select, gated


def per_device(
    patches,
    norm1_gain,
    qkv_weight,
    qkv_bias,
    out_weight,
    out_bias,
    norm2_gain,
    proj_weight,
    moe_gain,
    expert_in,
    expert_out,
    shared_in,
    shared_out,
    routes,
    gates,
):
    tile_id = lax.axis_index("tile")
    row_count = patches.shape[1]
    columns = patches.shape[2]
    width_vit = patches.shape[3]
    local_rows = row_count * columns
    tokens = local_rows // 4
    top = routes.shape[-1]
    side_a = [(t, t + 1 - 2 * (t % 2)) for t in range(NX)]
    side_b = [(t, NX - 1 - t) for t in range(NX)]
    units = expert_out.shape[1] // 2
    in_rows = expert_in[0].transpose(1, 2, 0)
    gate_halves = in_rows[0, :units], in_rows[0, units:]
    up_halves = in_rows[1, :units], in_rows[1, units:]

    def swap(halves, after):
        first, second, after = lax.optimization_barrier((*halves, after))
        from_a = lax.ppermute(first, "tile", side_a)
        from_b = lax.ppermute(second, "tile", side_b)
        return from_a, from_b, after

    project = lax.all_gather(proj_weight, "expert", axis=0, tiled=True)

    inputs = patches.reshape(local_rows, width_vit).astype(jnp.float32)
    normed = layer_norm(inputs, norm1_gain).astype(jnp.bfloat16)
    own_routes = lax.dynamic_index_in_dim(
        routes.reshape(NX, tokens, top), tile_id, 0, keepdims=False
    )
    table = jnp.zeros((16, 128), jnp.float32)
    table = table.at[:top, :tokens].set(own_routes.T.astype(jnp.float32))
    table = table.at[8 : 8 + top, :tokens].set(gates.reshape(tokens, top).T)
    piece, tables_z = ring_gather([("x", normed, 32), ("z", table, 16)], 0)
    gate_a, gate_b, piece = swap(gate_halves, piece)
    piece = piece.reshape(NX * local_rows, width_vit)

    heads_here = qkv_weight.shape[2] // HD
    qkv_flat = qkv_weight.reshape(width_vit, -1)
    bias_rows = qkv_bias.reshape(1, 3, heads_here, HD)
    mixed_flat = jnp.dot(piece, qkv_flat, preferred_element_type=jnp.float32)
    mixed = (
        mixed_flat.reshape(
            piece.shape[0], 3, heads_here, HD
        )
        + bias_rows
    )
    tables = rope_tables(jnp.arange(piece.shape[0]), columns, HD)
    attended = attend(
        rotate(mixed[:, 0], tables).astype(jnp.bfloat16),
        rotate(mixed[:, 1], tables).astype(jnp.bfloat16),
        mixed[:, 2].astype(jnp.bfloat16),
        math.sqrt(HD),
    )
    partial_rows = (
        jnp.dot(attended, out_weight, preferred_element_type=jnp.float32)
        .astype(jnp.bfloat16)
        .reshape(NX, local_rows, width_vit)
    )
    (mixed_heads,) = ring_reduce([("x", partial_rows, 32, jnp.float32)], 1)
    hidden = inputs + mixed_heads + out_bias
    normed_out = layer_norm(hidden, norm2_gain).astype(jnp.bfloat16)
    merged = (
        normed_out.reshape(row_count // 2, 2, columns // 2, 2, width_vit)
        .transpose(0, 2, 1, 3, 4)
        .reshape(tokens, 4 * width_vit)
    )
    (group_merged,) = ring_gather([("x", merged, 16)], 2)
    up_a, up_b, group_merged = swap(up_halves, group_merged)
    select, gated = slot_tables(tables_z, tokens, top)
    projected = jnp.dot(
        group_merged.reshape(NX * tokens, -1), project, preferred_element_type=jnp.float32
    ).astype(jnp.bfloat16)
    tokens_moe, moe_in, page_in = gather_tokens(projected, moe_gain, tokens, 3)
    width_moe = page_in.shape[1]
    shared_gated = jnp.dot(
        page_in, shared_in.reshape(width_moe, -1), preferred_element_type=jnp.float32
    ).reshape(NX * tokens, 2, -1)
    shared_hidden = (jax.nn.silu(shared_gated[:, 0]) * shared_gated[:, 1]).astype(jnp.bfloat16)
    shared_rows = (
        jnp.dot(shared_hidden, shared_out, preferred_element_type=jnp.float32)
        .astype(jnp.bfloat16)
        .reshape(NX, tokens, width_moe)
    )

    output = expert_layer(
        moe_in,
        select,
        shared_rows,
        gated,
        tokens_moe,
        (in_rows, expert_out[0], gate_a, up_a, gate_b, up_b),
        4,
    )
    return output.reshape(1, row_count // 2, columns // 2, width_moe)


def solution(mesh):
    placed = (
        P("expert", "tile", None, None),
        P(),
        P(None, None, "tile"),
        P(None, "tile"),
        P("tile", None),
        P(),
        P(),
        P("expert", "tile"),
        P(),
        P("expert", None, None, "tile"),
        P("expert", "tile", None),
        P(None, None, "tile"),
        P("tile", None),
        P("expert", None, None, None),
        P("expert", "tile", None, None),
    )
    return jax.shard_map(
        per_device,
        mesh=mesh,
        in_specs=placed,
        out_specs=P("expert", "tile", None, None),
        check_vma=False,
    )
```
